32 devices in a mesh: dp: 8 (over z, y), tensor: 4 (over x, core).
Axes of the slice: x: 2, y: 2, z: 4, core: 2. Of those that a mesh axis runs over, the one named last changes fastest.
Arguments:
- tokens: bfloat16 [8192, 768], P('dp'), may hold values from -6 to 6
- cotangent: bfloat16 [8192, 768], P('dp'), may hold values from -6 to 6
- item_count: int32 [8], P('dp'), may hold values from 0 to 1, as said below
- timestep: int32 [8], P('dp'), may hold values from 0 to 999
- class_id: int32 [8], P('dp'), may hold values from 0 to 1000
- class_table: bfloat16 [1001, 768], replicated, may hold values from -6 to 6
- w_mod: bfloat16 [4608, 768], replicated, may hold values from -0.21875 to 0.21875
- b_mod: bfloat16 [4608], replicated, may hold values from -3 to 3
- k_att: bfloat16 [9, 768], replicated, may hold values from -2 to 2
- w_qkv: bfloat16 [768, 3, 768], P(None, None, 'tensor'), may hold values from -0.21875 to 0.21875
- w_out: bfloat16 [768, 768], P(None, 'tensor'), may hold values from -0.875 to 0.875
- b_out: bfloat16 [768], replicated, may hold values from -2 to 2
- w_up: bfloat16 [768, 3072], P(None, 'tensor'), may hold values from -0.21875 to 0.21875
- b_up: bfloat16 [3072], P('tensor'), may hold values from -2 to 2
- k_ffn: bfloat16 [9, 3072], P(None, 'tensor'), may hold values from -2 to 2
- w_down: bfloat16 [768, 3072], P(None, 'tensor'), may hold values from -0.109375 to 0.109375
- b_down: bfloat16 [768], replicated, may hold values from -2 to 2
Outputs:
- block_out: bfloat16 [8192, 768], P(('dp', 'tensor'))
- grad_tokens: float32 [8192, 768], P(('dp', 'tensor'))
- grad_class_table: float32 [1001, 768], replicated
- grad_w_mod: float32 [4608, 768], P('dp')
- grad_b_mod: float32 [4608], replicated
- grad_k_att: float32 [9, 768], replicated
- grad_w_qkv: float32 [768, 3, 768], P('dp', None, 'tensor')
- grad_w_out: float32 [768, 768], P('dp', 'tensor')
- grad_b_out: float32 [768], replicated
- grad_w_up: float32 [768, 3072], P('dp', 'tensor')
- grad_b_up: float32 [3072], P('tensor')
- grad_k_ffn: float32 [9, 3072], P(None, 'tensor')
- grad_w_down: float32 [768, 3072], P('dp', 'tensor')
- grad_b_down: float32 [768], replicated
The draws below stay inside these ranges and needn't reach their ends.
Inputs may be any that keep to these rules, and one draw needn't show every extreme that they name: Item slots below item_count of their dp index hold live items, the others padding; some index of dp has all 1 slots live and some none.
All inputs are finite; a program needn't handle non-finite values.
Results may differ from the reference program's by a relative error of at most 0.028.
The reference program's roundings to bfloat16 on the way count: a program that leaves them out, or rounds other values in their place, can miss the bound.
Values may be sent and summed in bfloat16 or wider, within the bound.
No kernel may reach another device: no remote copies, remote signals or barrier semaphores. Data moves between devices by JAX's collectives and lax.ppermute only.
A program may use at most 192 MiB of HBM per device.

```python
import math
import jax
import jax.numpy as jnp
from jax import lax

HEADS = 12
HEAD_DIM = 64
FF = 3072
NCLASS = 1001
SIDE = 32
ITEMS_DEV = 1
D = 768
ITEM_TOK = 1024
ITEMS = 8
TOKENS = 8192
GROUPS = 8


def draw_item_count(key, part):
    base = jax.random.randint(jax.random.fold_in(key, 11), (GROUPS,), 1, ITEMS_DEV + 1)
    order = jax.random.permutation(jax.random.fold_in(key, 12), GROUPS)
    filled = jnp.where(order == 0, ITEMS_DEV, base)
    return jnp.where(order == 1, 0, filled).astype(jnp.int32)


def touch_ends(values, key, smallest, high):
    longest = values.shape.index(max(values.shape))
    spots = []
    for shift in (0, 1):
        where = [jax.random.randint(jax.random.fold_in(key, axis), (), 0, length) for axis, length in enumerate(values.shape)]
        where[longest] = (where[longest] + shift) % values.shape[longest]
        spots.append(tuple(where))
    return values.at[spots[0]].set(smallest).at[spots[1]].set(high)


def steps_of(rng, dims, cuts, low, high):
    loudness = 1.0
    for axis_at, shards_of in cuts:
        steps = jax.random.uniform(jax.random.fold_in(jax.random.fold_in(rng, 6), axis_at), (shards_of,), jnp.float32, low / len(cuts), high / len(cuts))
        loudness = loudness * jnp.repeat(jnp.exp(steps), dims[axis_at] // shards_of).reshape((-1,) + (1,) * (len(dims) - 1 - axis_at))
    return loudness


def scatter_about(key, extent, scale, reach, pieces=(), kind=jnp.bfloat16):
    values = scale * jax.random.normal(key, extent, jnp.float32)
    if pieces:
        values = values * steps_of(key, extent, pieces, -0.22, 0.18)
    return jnp.clip(values, -reach, reach).astype(kind)


def setup_inputs(seed: int = 0) -> dict:
    splits = jax.random.split(jax.random.key(seed), 18)
    return {
        "tokens": scatter_about(splits[0], (TOKENS, D), 1.0, 6.0, ((0, 8),)),
        "cotangent": scatter_about(splits[1], (TOKENS, D), 1.0, 6.0, ((0, 8),)),
        "item_count": draw_item_count(jax.random.fold_in(splits[17], 71), 0),
        "timestep": touch_ends(jax.random.randint(splits[3], (ITEMS,), 0, 1000), jax.random.fold_in(splits[3], 1), 0, 999).astype(jnp.int32),
        "class_id": touch_ends(jax.random.randint(splits[4], (ITEMS,), 0, NCLASS), jax.random.fold_in(splits[4], 1), 0, NCLASS - 1).astype(jnp.int32),
        "class_table": scatter_about(splits[5], (NCLASS, D), 1.0, 6.0),
        "w_mod": scatter_about(splits[6], (6 * D, D), D ** -0.5, 0.21875),
        "b_mod": scatter_about(splits[7], (6 * D,), 0.5, 3.0),
        "k_att": scatter_about(splits[8], (9, D), 9 ** -0.5, 2.0),
        "w_qkv": scatter_about(splits[9], (D, 3, D), D ** -0.5, 0.21875, ((2, 4),)),
        "w_out": scatter_about(splits[10], (D, D), (D // 16) ** -0.5, 0.875, ((1, 4),)),
        "b_out": scatter_about(splits[11], (D,), 0.3, 2.0),
        "w_up": scatter_about(splits[12], (D, FF), D ** -0.5, 0.21875, ((1, 4),)),
        "b_up": scatter_about(splits[13], (FF,), 0.3, 2.0, ((0, 4),)),
        "k_ffn": scatter_about(splits[14], (9, FF), 9 ** -0.5, 2.0, ((1, 4),)),
        "w_down": scatter_about(splits[15], (D, FF), FF ** -0.5, 0.109375, ((1, 4),)),
        "b_down": scatter_about(splits[16], (D,), 0.3, 2.0),
    }


@jax.custom_vjp
def low(v):
    return lax.optimization_barrier(v.astype(jnp.bfloat16)).astype(jnp.float32)

@jax.custom_vjp
def low_back(v):
    return v

def low_keep(v):
    return (low(v), None)

def low_pass(kept, grad):
    return (grad,)

def back_keep(v):
    return (v, None)

def back_low(kept, grad):
    return (low(grad),)
low.defvjp(low_keep, low_pass)
low_back.defvjp(back_keep, back_low)
highest = lax.Precision.HIGHEST
norm_eps = 1e-06

def layer_norm(values):
    center = values - lax.optimization_barrier(jnp.mean(values, axis=-1, keepdims=True))
    return center * lax.rsqrt(lax.optimization_barrier(jnp.mean(center * center, axis=-1, keepdims=True)) + norm_eps)

def time_features(timestep, width):
    half_width = width // 2
    freqs = jnp.exp(-math.log(10000.0) * jnp.arange(half_width, dtype=jnp.float32) / half_width)
    angles = timestep.astype(jnp.float32)[:, None] * freqs[None, :]
    return jnp.concatenate([jnp.cos(angles), jnp.sin(angles)], axis=1)

def depthwise(field, kernel):
    grid_side = field.shape[1]
    padded = jnp.pad(field, ((0, 0), (1, 1), (1, 1), (0, 0)))
    total = jnp.zeros_like(field)
    for vertical in range(3):
        for horizontal in range(3):
            total = total + kernel[vertical * 3 + horizontal] * padded[:, vertical:vertical + grid_side, horizontal:horizontal + grid_side]
    return total

def item_forward(params, item_tokens, modulate):
    k_att, w_qkv, w_out, b_out, w_up, b_up, k_ffn, w_down, b_down = params
    shift_att, scale_att, gate_att, shift_ffn, scale_ffn, gate_ffn = jnp.split(modulate, 6)
    normed = layer_norm(item_tokens)
    shaped = normed * (1.0 + scale_att) + shift_att
    mixed = depthwise(shaped.reshape(1, SIDE, SIDE, D), k_att).reshape(ITEM_TOK, D)
    mixed = low(low_back(mixed))
    project = jnp.einsum('td,dcj->tcj', mixed, w_qkv, precision=highest)
    project = low(low_back(project))
    half_side = SIDE // 2
    grouped = project.reshape(half_side, 2, half_side, 2, 3, HEADS, HEAD_DIM)
    grouped = grouped.transpose(1, 3, 0, 2, 4, 5, 6).reshape(4, ITEM_TOK // 4, 3, HEADS, HEAD_DIM)
    query = grouped[:, :, 0]
    keys = grouped[:, :, 1]
    vals = grouped[:, :, 2]
    scores = low_back(jnp.einsum('gqhd,gkhd->ghqk', query, keys, precision=highest) * 0.125)
    weights = low(jax.nn.softmax(scores, axis=-1))
    attended = jnp.einsum('ghqk,gkhd->gqhd', weights, vals, precision=highest)
    attended = attended.reshape(2, 2, half_side, half_side, D).transpose(2, 0, 3, 1, 4).reshape(ITEM_TOK, D)
    attended = low(low_back(attended))
    branch = low_back(jnp.dot(attended, w_out.T, precision=highest) + b_out)
    middle = item_tokens + gate_att * branch
    shaped_ffn = low(layer_norm(middle) * (1.0 + scale_ffn) + shift_ffn)
    hidden = low_back(jnp.dot(shaped_ffn, w_up, precision=highest) + b_up)
    convolved = depthwise(hidden.reshape(1, SIDE, SIDE, FF), k_ffn).reshape(ITEM_TOK, FF)
    activated = low(jax.nn.gelu(convolved))
    branch_ffn = low_back(jnp.dot(activated, w_down.T, precision=highest) + b_down)
    return middle + gate_ffn * branch_ffn

def reference(tokens, cotangent, item_count, timestep, class_id, class_table, w_mod, b_mod, k_att, w_qkv, w_out, b_out, w_up, b_up, k_ffn, w_down, b_down):
    live = (jnp.arange(ITEMS_DEV)[None, :] < item_count[:, None]).reshape(ITEMS).astype(jnp.float32)
    floats = tuple((source.astype(jnp.float32) for source in (tokens, class_table, w_mod, b_mod, k_att, w_qkv, w_out, b_out, w_up, b_up, k_ffn, w_down, b_down)))

    def whole(all_tokens, table, weight_mod, bias_mod, *params):
        cond = time_features(timestep, D) + table[class_id]
        act = low(jax.nn.silu(cond))
        modulate = low_back(jnp.dot(act, weight_mod.T, precision=highest) + bias_mod)

        def one_item(inputs):
            return item_forward(params, inputs[0], inputs[1])
        result = lax.map(jax.checkpoint(one_item), (all_tokens.reshape(ITEMS, ITEM_TOK, D), modulate))
        return (result * live[:, None, None]).reshape(TOKENS, D)
    block_out, pullback = jax.vjp(whole, *floats)
    grads = pullback(cotangent.astype(jnp.float32))
    return (block_out.astype(jnp.bfloat16), grads[0], grads[1], grads[2], grads[3], grads[4], grads[5], grads[6], grads[7], grads[8], grads[9], grads[10], grads[11], grads[12])
```

```python
import math

import jax
import jax.numpy as jnp
from jax import lax
from jax.sharding import PartitionSpec as P

HEAD_DIM = 64
SIDE = 32
HALF = SIDE // 2
ITEM = SIDE * SIDE

norm_eps = 1e-06
score_scale = 0.125
highest = lax.Precision.HIGHEST
f32 = jnp.float32
bf16 = jnp.bfloat16


def swap(values, axis, bit):
    size = lax.axis_size(axis)
    return lax.ppermute(values, axis, [(i, i ^ bit) for i in range(size)])


def bits_of(axis):
    return [1 << b for b in range(lax.axis_size(axis).bit_length() - 1)]


def take(values, index):
    return lax.dynamic_index_in_dim(values, index, 0, keepdims=False)


def add_low(left, right):
    return (left.astype(f32) + right.astype(f32)).astype(bf16)


def scatter_sum(grad):
    size = lax.axis_size("dp")
    here = lax.axis_index("dp")
    held = grad.reshape((size, grad.shape[0] // size) + grad.shape[1:])
    for bit in bits_of("dp"):
        mine = (here // bit) % 2
        halves = held.reshape((held.shape[0] // 2, 2) + held.shape[1:])
        sent = lax.dynamic_index_in_dim(halves, 1 - mine, 1, keepdims=False).astype(bf16)
        kept = lax.dynamic_index_in_dim(halves, mine, 1, keepdims=False)
        held = kept.astype(f32) + swap(sent, "dp", bit).astype(f32)
    return held[0]


def butterfly(values, axis):
    for bit in bits_of(axis):
        values = values + swap(values, axis, bit)
    return values


def gather_xor(values):
    for bit in bits_of("dp"):
        values = jnp.concatenate([values, swap(values, "dp", bit)], axis=0)
    return values


def tree_sum(values):
    while values.shape[0] > 1:
        values = values[0::2] + values[1::2]
    return values[0]


def layer_norm(values):
    center = values - jnp.mean(values, axis=-1, keepdims=True)
    return center * lax.rsqrt(jnp.mean(center * center, axis=-1, keepdims=True) + norm_eps)


def time_features(timestep, width):
    half_width = width // 2
    freqs = jnp.exp(-math.log(10000.0) * jnp.arange(half_width, dtype=f32) / half_width)
    angles = timestep.astype(f32)[:, None] * freqs[None, :]
    return jnp.concatenate([jnp.cos(angles), jnp.sin(angles)], axis=1)


def depthwise(field, kernel):
    rows, cols = field.shape[:2]
    padded = jnp.pad(field, ((1, 1), (1, 1), (0, 0)))
    total = jnp.zeros_like(field)
    for a in range(3):
        for b in range(3):
            total = total + kernel[a * 3 + b] * padded[a : a + rows, b : b + cols]
    return total


def depthwise_back(field, grad_rows, kernel):
    rows, cols = field.shape[:2]
    padded = jnp.pad(grad_rows, ((0, 0), (1, 1), (0, 0)))
    total = jnp.zeros_like(field)
    kernel_rows = []
    for a in range(3):
        for b in range(3):
            seen = padded[2 - a : 2 - a + rows, 2 - b : 2 - b + cols]
            total = total + kernel[a * 3 + b] * seen
            kernel_rows.append(jnp.sum(field * seen, axis=(0, 1)))
    return (total, jnp.stack(kernel_rows))


def to_groups(values, rows):
    width = values.shape[-1]
    shaped = values.reshape((rows // 2, 2, HALF, 2, width))
    return shaped.transpose((1, 3, 0, 2, 4)).reshape((rows * SIDE, width))


def from_groups(values, rows):
    width = values.shape[-1]
    shaped = values.reshape((2, 2, rows // 2, HALF, width))
    return shaped.transpose((2, 0, 3, 1, 4)).reshape((rows * SIDE, width))


def to_halves(values):
    width = values.shape[-1]
    shaped = values.reshape((4, 2, 2, 64, width))
    return shaped.transpose((2, 1, 0, 3, 4)).reshape((2, ITEM // 2, width))


def from_halves(own, other, core):
    width = own.shape[-1]
    both = jnp.stack([jnp.where(core == 0, own, other), jnp.where(core == 0, other, own)])
    shaped = both.reshape((2, 2, 4, 64, width))
    return shaped.transpose((2, 1, 0, 3, 4)).reshape((ITEM, width))


def dot_nn(left, right):
    return lax.dot_general(left, right, (((1,), (0,)), ((), ())), preferred_element_type=f32)


def dot_nt(left, right):
    return lax.dot_general(left, right, (((1,), (1,)), ((), ())), preferred_element_type=f32)


def dot_tn(left, right):
    return lax.dot_general(left, right, (((0,), (0,)), ((), ())), preferred_element_type=f32)


def split_heads(values):
    return values.reshape(4, ITEM // 4, -1, HEAD_DIM)


def stage_a(tokens, mods, k_att, w_qkv, w_out):
    shaped = layer_norm(tokens.astype(f32)) * (1.0 + mods[1]) + mods[0]
    mixed = depthwise(shaped.reshape(SIDE, SIDE, -1), k_att.astype(f32))
    mixed = to_groups(mixed.reshape(ITEM, -1).astype(bf16), SIDE)
    project = [dot_nn(mixed, w_qkv[:, kind]).astype(bf16) for kind in range(3)]
    query, keys, vals = (split_heads(p) for p in project)
    scores = jnp.einsum("bqhd,bkhd->bhqk", query, keys, preferred_element_type=f32) * score_scale
    top = jnp.max(scores, axis=-1, keepdims=True)
    log_total = top + jnp.log(jnp.sum(jnp.exp(scores - top), axis=-1, keepdims=True))
    probs_low = jnp.exp(scores - log_total).astype(bf16)
    attended = jnp.einsum("bhqk,bkhd->bqhd", probs_low, vals, preferred_element_type=f32)
    attended = attended.reshape(ITEM, -1).astype(bf16)
    partial = to_halves(dot_nt(attended, w_out).astype(bf16))
    return mixed, project, attended, log_total, partial


def stage_b(source, summed, mods, b_out):
    branch = summed + b_out.astype(f32)
    middle = source + mods[2] * branch
    shaped = (layer_norm(middle) * (1.0 + mods[4]) + mods[3]).astype(bf16)
    return branch, middle, shaped


def stage_c(shaped, grad_branch, w_up, b_up, k_ffn, w_down):
    taps = k_ffn.astype(f32)
    hidden = dot_nn(shaped, w_up) + b_up.astype(f32)
    hidden = from_groups(hidden, SIDE).reshape(SIDE, SIDE, -1)
    convolved = depthwise(hidden, taps)
    activated, back = jax.vjp(jax.nn.gelu, convolved)
    activated = to_groups(activated.reshape(ITEM, -1).astype(bf16), SIDE)
    grad_activated = from_groups(dot_nn(grad_branch, w_down), SIDE)
    grad_convolved = back(grad_activated.reshape(convolved.shape))[0]
    padded = jnp.pad(grad_convolved, ((1, 1), (0, 0), (0, 0)))
    grad_hidden, grad_k = depthwise_back(hidden, padded, taps)
    grad_hidden = to_groups(grad_hidden.reshape(ITEM, -1).astype(bf16), SIDE)
    grad_b_up = jnp.sum(grad_hidden.astype(f32), axis=0)
    branch = to_halves(dot_nt(activated, w_down).astype(bf16))
    grad_shaped = to_halves(dot_nt(grad_hidden, w_up).astype(bf16))
    return activated, grad_hidden, grad_k, grad_b_up, branch, grad_shaped


def stage_d(middle, branch, grad_out, grad_shaped, mods):
    normed, back = jax.vjp(layer_norm, middle)
    grad_middle = grad_out + back(grad_shaped * (1.0 + mods[4]))[0]
    sums = (
        jnp.sum(grad_middle * branch, axis=0),
        jnp.sum(grad_shaped, axis=0),
        jnp.sum(grad_shaped * normed, axis=0),
    )
    return grad_middle, (grad_middle * mods[2]).astype(bf16), sums


def stage_e(grad_branch, project, log_total, w_qkv, w_out):
    grad_attended = dot_nn(grad_branch, w_out).astype(bf16)
    query, keys, vals = (split_heads(p) for p in project)
    grads = split_heads(grad_attended)
    scores = jnp.einsum("bqhd,bkhd->bhqk", query, keys, preferred_element_type=f32) * score_scale
    probs = jnp.exp(scores - log_total)
    grad_probs = jnp.einsum("bqhd,bkhd->bhqk", grads, vals, preferred_element_type=f32)
    grad_scores = probs * (grad_probs - jnp.sum(probs * grad_probs, axis=-1, keepdims=True))
    grad_scores = grad_scores.astype(bf16)
    g_query = jnp.einsum("bhqk,bkhd->bqhd", grad_scores, keys, preferred_element_type=f32)
    g_keys = jnp.einsum("bhqk,bqhd->bkhd", grad_scores, query, preferred_element_type=f32)
    g_vals = jnp.einsum("bhqk,bqhd->bkhd", probs.astype(bf16), grads, preferred_element_type=f32)
    grad_project = [
        g.reshape(ITEM, -1).astype(bf16)
        for g in (g_query * score_scale, g_keys * score_scale, g_vals)
    ]
    grad_mixed = sum(dot_nt(grad_project[kind], w_qkv[:, kind]) for kind in range(3))
    return grad_project, with_halos(grad_mixed.astype(bf16))


def with_halos(values):
    width = values.shape[-1]
    padded = jnp.pad(values.reshape(4, HALF, HALF, width), ((0, 0), (1, 1), (0, 0), (0, 0)))
    shares = []
    for share in range(4):
        first = 4 * share
        main = padded[:, first + 1 : first + 5].reshape(-1, width)
        above = padded[2:, first].reshape(-1, width)
        below = padded[:2, first + 5].reshape(-1, width)
        shares.append(jnp.concatenate([main, above, below]))
    return jnp.stack(shares).reshape(2, 2, -1, width).swapaxes(0, 1)


def stage_f(tokens, grad_middle, grad_mixed, mods, k_att):
    width = tokens.shape[-1]
    rows = tokens.shape[0] // SIDE
    inner = from_groups(grad_mixed[:256], rows).reshape(rows, SIDE, width)
    above = grad_mixed[256:288].reshape(2, HALF, width).swapaxes(0, 1).reshape(1, SIDE, width)
    below = grad_mixed[288:].reshape(2, HALF, width).swapaxes(0, 1).reshape(1, SIDE, width)
    grad_rows = jnp.concatenate([above, inner, below])
    normed, back = jax.vjp(layer_norm, tokens)
    shaped = normed * (1.0 + mods[1]) + mods[0]
    grad_shaped, grad_k = depthwise_back(
        shaped.reshape(rows, SIDE, width), grad_rows, k_att.astype(f32)
    )
    grad_shaped = grad_shaped.reshape(tokens.shape)
    grad_tokens = from_groups(grad_middle, rows) + back(grad_shaped * (1.0 + mods[1]))[0]
    sums = (jnp.sum(grad_shaped, axis=0), jnp.sum(grad_shaped * normed, axis=0))
    return grad_tokens, grad_k, sums


def shards(
    tokens,
    cotangent,
    item_count,
    timestep,
    class_id,
    class_table,
    w_mod,
    b_mod,
    k_att,
    w_qkv,
    w_out,
    b_out,
    w_up,
    b_up,
    k_ffn,
    w_down,
    b_down,
):
    width = tokens.shape[1]
    place = lax.axis_index("tensor")
    core = place % 2
    side = place // 2
    live = (item_count[0] > 0).astype(f32)

    cond = time_features(timestep, width) + class_table[class_id[0]].astype(f32)[None, :]
    act_low = jax.nn.silu(cond).astype(bf16)
    mods = (dot_nt(act_low, w_mod) + b_mod.astype(f32)).reshape(6, width)
    card = jnp.concatenate([cond, jnp.broadcast_to(class_id.astype(f32)[:, None], (1, 128))], axis=1)
    cards = gather_xor(card)

    mixed, project, attended, log_total, partial = stage_a(tokens, mods, k_att, w_qkv, w_out)
    chip = add_low(take(partial, core), swap(take(partial, 1 - core), "tensor", 1))
    summed = chip.astype(f32) + swap(chip, "tensor", 2).astype(f32)

    source = take(to_halves(to_groups(tokens, SIDE)), core).astype(f32)
    branch, middle, shaped_own = stage_b(source, summed, mods, b_out)
    shaped = from_halves(shaped_own, swap(shaped_own, "tensor", 1), core)

    cot_groups = to_groups(cotangent, SIDE)
    grad_branch_ffn = (cot_groups.astype(f32) * (live * mods[5])).astype(bf16)
    grad_out = take(to_halves(cot_groups), core).astype(f32) * live
    activated, grad_hidden, grad_k_ffn, grad_b_up, ffn_part, grad_part = stage_c(
        shaped, grad_branch_ffn, w_up, b_up, k_ffn, w_down
    )
    chip = add_low(take(grad_part, core), swap(take(grad_part, 1 - core), "tensor", 1))
    grad_shaped = chip.astype(f32) + swap(chip, "tensor", 2).astype(f32)
    grad_w_down = scatter_sum(dot_tn(grad_branch_ffn, activated))
    grad_w_up = scatter_sum(dot_tn(shaped, grad_hidden))

    def own_share(values):
        return take(values.reshape(2, 256, -1), side)

    def reduce_share(values):
        shares = values.reshape(2, -1, width)
        return take(shares, side).astype(f32) + swap(take(shares, 1 - side), "tensor", 2).astype(f32)

    chip = add_low(take(ffn_part, core), swap(take(ffn_part, 1 - core), "tensor", 1))
    branch_ffn = reduce_share(chip) + b_down.astype(f32)
    block_out = (own_share(middle) + mods[5] * branch_ffn) * live
    block_out = from_groups(block_out.astype(bf16), SIDE // 4)
    grad_gate_ffn = jnp.sum(own_share(grad_out) * branch_ffn, axis=0)

    grad_middle, grad_attn_own, sums_d = stage_d(middle, branch, grad_out, grad_shaped, mods)
    grad_branch = from_halves(grad_attn_own, swap(grad_attn_own, "tensor", 1), core)
    grad_project, halo_part = stage_e(grad_branch, project, log_total, w_qkv, w_out)
    chip = add_low(take(halo_part, core), swap(take(halo_part, 1 - core), "tensor", 1))
    grad_mixed = reduce_share(chip).astype(bf16).astype(f32)
    grad_w_out = scatter_sum(dot_tn(grad_branch, attended))
    grad_w_qkv = scatter_sum(
        jnp.stack([dot_tn(mixed, g) for g in grad_project], axis=1)
    )

    rows = ITEM // 4
    own_tokens = lax.dynamic_slice_in_dim(tokens, place * rows, rows, 0).astype(f32)
    grad_tokens, grad_k_att, sums_f = stage_f(
        own_tokens, own_share(grad_middle), grad_mixed, mods, k_att
    )

    early = jnp.concatenate(
        [
            grad_k_ffn,
            grad_b_up[None],
            jnp.sum(grad_branch_ffn.astype(f32), axis=0)[None],
            jnp.sum(grad_branch.astype(f32), axis=0)[None],
        ]
    )
    early = butterfly(early, "dp")

    once = jnp.where(side == 0, 1.0, 0.0)
    late = jnp.concatenate(
        [
            jnp.stack(
                [
                    sums_f[0],
                    sums_f[1],
                    sums_d[0] * once,
                    sums_d[1] * once,
                    sums_d[2] * once,
                    grad_gate_ffn,
                ]
            ),
            grad_k_att,
        ]
    )
    late = butterfly(late, "tensor")
    grad_k_att = butterfly(late[6:], "dp")
    grad_modulate = gather_xor(late[None, :6].reshape(1, -1).astype(bf16))

    grad_b_mod = tree_sum(grad_modulate.astype(f32))
    conds = cards[:, :width]
    classes = cards[:, width]
    act, silu_back = jax.vjp(jax.nn.silu, conds)
    share = w_mod.shape[0] // lax.axis_size("dp")
    own_rows = lax.dynamic_slice_in_dim(grad_modulate, lax.axis_index("dp") * share, share, 1)
    grad_w_mod = dot_tn(own_rows, act.astype(bf16))
    grad_cond = silu_back(dot_nn(grad_modulate, w_mod))[0]
    same = (classes[:, None] == classes[None, :]).astype(f32)
    class_rows = tree_sum(same[:, :, None] * grad_cond[:, None, :])
    grad_class = jnp.zeros(class_table.shape, f32).at[classes.astype(jnp.int32)].set(class_rows)

    return (
        block_out,
        grad_tokens,
        grad_class,
        grad_w_mod,
        grad_b_mod,
        grad_k_att,
        grad_w_qkv,
        grad_w_out,
        early[11],
        grad_w_up,
        early[9],
        early[:9],
        grad_w_down,
        early[10],
    )


def solution(mesh):
    placed = (
        P("dp", None),
        P("dp", None),
        P("dp"),
        P("dp"),
        P("dp"),
        P(),
        P(),
        P(),
        P(),
        P(None, None, "tensor"),
        P(None, "tensor"),
        P(),
        P(None, "tensor"),
        P("tensor"),
        P(None, "tensor"),
        P(None, "tensor"),
        P(),
    )
    return jax.shard_map(
        shards,
        mesh=mesh,
        in_specs=placed,
        out_specs=(
            P(("dp", "tensor"), None),
            P(("dp", "tensor"), None),
            P(),
            P("dp", None),
            P(),
            P(),
            P("dp", None, "tensor"),
            P("dp", "tensor"),
            P(),
            P("dp", "tensor"),
            P("tensor"),
            P(None, "tensor"),
            P("dp", "tensor"),
            P(),
        ),
        check_vma=False,
    )
```

```python
import functools
import math

import jax
import jax.numpy as jnp
from jax import lax
from jax.experimental import pallas as pl
from jax.experimental.pallas import tpu as pltpu
from jax.sharding import PartitionSpec as P

f32 = jnp.float32
bf16 = jnp.bfloat16

PITCH=40
GRID_ROWS=34*PITCH+8
SLOPE=math.sqrt(2.0/math.pi)
CUBIC=0.044715

def dot_nn(l,r): return lax.dot_general(l,r,(((1,),(0,)),((),())),preferred_element_type=f32)
def dot_nt(l,r): return lax.dot_general(l,r,(((1,),(1,)),((),())),preferred_element_type=f32)
def dot_tn(l,r): return lax.dot_general(l,r,(((0,),(0,)),((),())),preferred_element_type=f32)

def place(row, col):
    return (row+1)*PITCH+8+col

def strided(start):
    return pl.ds(start,16,stride=2)

def patch(ref, tile, i):
    return [[ref[tile, strided(place(2*i+row, col)), :] for col in range(-1,3)] for row in range(-1,3)]

def halves_out(values_ref, core, group, keep_ref, send_ref):
    for x in range(2):
        rows=pl.ds(x*256+group*64,64)
        rows=pl.ds(pl.multiple_of(x*256+group*64,64),64)
        keep_ref[rows,:]=values_ref[pl.ds(pl.multiple_of((2*x+core)*64,64),64),:].astype(bf16)
        send_ref[rows,:]=values_ref[pl.ds(pl.multiple_of((2*x+1-core)*64,64),64),:].astype(bf16)

def kernel_c(core_ref, own_ref, other_ref, gb_ref, up_ref, bup_ref, k_ref, down_ref,
             shaped_ref, act_ref, gh_ref, sums_ref, bkeep_ref, bsend_ref, gkeep_ref, gsend_ref,
             hid, gcv, gact, temp):
    core=core_ref[0]
    hid[...]=jnp.zeros_like(hid)
    gcv[...]=jnp.zeros_like(gcv)
    for half_ref, h in ((own_ref,core),(other_ref,1-core)):
        for x in range(2):
            for g in range(4):
                row=pl.multiple_of(g*256+(8*x+4*h)*16,64)
                shaped_ref[pl.ds(row,64),:]=half_ref[x*256+g*64:x*256+g*64+64,:]
    def up(g,_):
        rows=pl.ds(pl.multiple_of(g*256,256),256)
        a=g//2; b=g%2
        gact[rows,:]=dot_nn(gb_ref[rows,:],down_ref[...])
        temp[...]=dot_nn(shaped_ref[rows,:],up_ref[...])+bup_ref[...]
        def spread(i,_):
            for tile in range(6):
                hid[tile,strided(place(2*i+a,b)),:]=temp[pl.ds(pl.multiple_of(i*16,16),16),tile*128:tile*128+128]
            return 0
        lax.fori_loop(0,16,spread,0)
        return 0
    lax.fori_loop(0,4,up,0)
    def conv(tile,_):
        cols=pl.ds(pl.multiple_of(tile*128,128),128)
        taps=[k_ref[t:t+1,cols] for t in range(9)]
        def row(i,_):
            seen=patch(hid,tile,i)
            for a in range(2):
                for b in range(2):
                    g=2*a+b
                    rows=pl.ds(pl.multiple_of(g*256+i*16,16),16)
                    u=taps[0]*seen[a][b]
                    for t in range(1,9):
                        u=u+taps[t]*seen[a+t//3][b+t%3]
                    sq=u*u
                    th=jnp.tanh(SLOPE*u*(1.0+CUBIC*sq))
                    half=0.5+0.5*th
                    act_ref[rows,cols]=(u*half).astype(bf16)
                    slope=half+(0.5*SLOPE)*u*(1.0-th*th)*(1.0+(3*CUBIC)*sq)
                    gcv[tile,strided(place(2*i+a,b)),:]=gact[rows,cols]*slope
            return 0
        lax.fori_loop(0,16,row,0)
        return 0
    lax.fori_loop(0,6,conv,0)
    def back(tile,_):
        cols=pl.ds(pl.multiple_of(tile*128,128),128)
        taps=[k_ref[t:t+1,cols] for t in range(9)]
        def row(i,acc):
            seen=patch(gcv,tile,i)
            acc=list(acc)
            for a in range(2):
                for b in range(2):
                    g=2*a+b
                    rows=pl.ds(pl.multiple_of(g*256+i*16,16),16)
                    here=hid[tile,strided(place(2*i+a,b)),:]
                    total=None
                    for t in range(9):
                        s=seen[a+2-t//3][b+2-t%3]
                        total=taps[t]*s if total is None else total+taps[t]*s
                        p=here*s
                        acc[t]=acc[t]+(p[:8]+p[8:])
                    low=total.astype(bf16)
                    gh_ref[rows,cols]=low
                    p=low.astype(f32)
                    acc[9]=acc[9]+(p[:8]+p[8:])
            return tuple(acc)
        acc=lax.fori_loop(0,16,row,tuple(jnp.zeros((8,128),f32) for _ in range(10)))
        for t in range(10):
            sums_ref[t:t+1,cols]=jnp.sum(acc[t],axis=0,keepdims=True)
        return 0
    lax.fori_loop(0,6,back,0)
    def out(g,total):
        rows=pl.ds(pl.multiple_of(g*256,256),256)
        temp[...]=dot_nt(gh_ref[rows,:],up_ref[...])
        halves_out(temp,core,g,gkeep_ref,gsend_ref)
        temp[...]=dot_nt(act_ref[rows,:],down_ref[...])
        halves_out(temp,core,g,bkeep_ref,bsend_ref)
        return total+jnp.sum(gb_ref[rows,:].astype(f32),axis=0,keepdims=True)
    sums_ref[10:11,:]=lax.fori_loop(0,4,out,jnp.zeros((1,768),f32))

def call_c(core, own, other, gb, w_up, b_up, k, w_down):
    half=jax.ShapeDtypeStruct((512,768),bf16)
    full=jax.ShapeDtypeStruct((1024,768),bf16)
    vm=pl.BlockSpec(memory_space=pltpu.VMEM)
    return pl.pallas_call(kernel_c,
        out_shape=(full,full,full,jax.ShapeDtypeStruct((16,768),f32),half,half,half,half),
        in_specs=[pl.BlockSpec(memory_space=pltpu.SMEM)]+[vm]*7,
        out_specs=[vm]*8,
        scratch_shapes=[pltpu.VMEM((6,GRID_ROWS,128),f32),pltpu.VMEM((6,GRID_ROWS,128),f32),pltpu.VMEM((1024,768),f32),pltpu.VMEM((256,768),f32)],
        compiler_params=pltpu.CompilerParams(vmem_limit_bytes=56<<20),
        cost_estimate=pl.CostEstimate(flops=5*10**9,bytes_accessed=12*10**6,transcendentals=10**6),
    )(core,own,other,gb,w_up,b_up.astype(f32)[None],k.astype(f32),w_down)


eps=1e-6
def vm(): return pl.BlockSpec(memory_space=pltpu.VMEM)
def sm(): return pl.BlockSpec(memory_space=pltpu.SMEM)
def sds(shape,dt): return jax.ShapeDtypeStruct(shape,dt)
def at(start,size): return pl.ds(pl.multiple_of(start,size),size)

def normed_of(x):
    center=x-jnp.mean(x,axis=-1,keepdims=True)
    rs=lax.rsqrt(jnp.mean(center*center,axis=-1,keepdims=True)+eps)
    return center*rs, rs

def head_masks():
    lane=lax.broadcasted_iota(jnp.int32,(256,192),1)
    return [(lane>=64*h)&(lane<64*h+64) for h in range(3)]

def kernel_a(core_ref, tok_ref, mods_ref, k_ref, wqkv_ref, wout_ref,
             mixed_ref, q_ref, kk_ref, v_ref, att_ref, lse_ref, src_ref, keep_ref, send_ref,
             grid, xs, temp):
    core=core_ref[0]
    grid[...]=jnp.zeros_like(grid)
    shift=mods_ref[0:1,:]; scale=1.0+mods_ref[1:2,:]
    def norm(i,_):
        x=tok_ref[at(i*64,64),:].astype(f32)
        n,_r=normed_of(x)
        y=n*scale+shift
        for tile in range(6):
            cols=slice(tile*128,tile*128+128)
            xs[tile,at(i*64,64),:]=x[:,cols]
            for r in range(2):
                grid[tile,pl.ds(pl.multiple_of((2*i+r+1)*PITCH+8,8),32),:]=y[32*r:32*r+32,cols]
        return 0
    lax.fori_loop(0,16,norm,0)
    def conv(tile,_):
        cols=pl.ds(pl.multiple_of(tile*128,128),128)
        taps=[k_ref[t:t+1,cols] for t in range(9)]
        def row(i,_):
            seen=patch(grid,tile,i)
            for a in range(2):
                for b in range(2):
                    u=taps[0]*seen[a][b]
                    for t in range(1,9):
                        u=u+taps[t]*seen[a+t//3][b+t%3]
                    mixed_ref[at((2*a+b)*256+i*16,16),cols]=u.astype(bf16)
            return 0
        lax.fori_loop(0,16,row,0)
        for x in range(2):
            for g in range(4):
                for ii in range(4):
                    i=8*x+4*core+ii
                    src_ref[x*256+g*64+ii*16:x*256+g*64+ii*16+16,cols]=xs[tile,strided((2*i+g//2)*32+g%2),:]
        return 0
    lax.fori_loop(0,6,conv,0)
    masks=head_masks()
    lane=lax.broadcasted_iota(jnp.int32,(256,128),1)
    def attend(g,_):
        rows=at(g*256,256)
        m=mixed_ref[rows,:]
        q,k,v=(dot_nn(m,wqkv_ref[t]).astype(bf16) for t in range(3))
        q_ref[rows,:]=q; kk_ref[rows,:]=k; v_ref[rows,:]=v
        att=jnp.zeros((256,192),f32)
        lse=jnp.zeros((256,128),f32)
        for h in range(3):
            s=dot_nt(jnp.where(masks[h],q,jnp.zeros_like(q)),k)*0.125
            top=jnp.max(s,axis=-1,keepdims=True)
            lt=top+jnp.log(jnp.sum(jnp.exp(s-top),axis=-1,keepdims=True))
            p=jnp.exp(s-lt).astype(bf16)
            att=jnp.where(masks[h],dot_nn(p,v),att)
            lse=jnp.where(lane==h,lt,lse)
        lse_ref[rows,:]=lse
        att=att.astype(bf16)
        att_ref[rows,:]=att
        temp[...]=dot_nt(att,wout_ref[...])
        halves_out(temp,core,g,keep_ref,send_ref)
        return 0
    lax.fori_loop(0,4,attend,0)

def call_a(core,tokens,mods,k,wqkv,w_out):
    half=sds((512,768),bf16); head=sds((1024,192),bf16)
    return pl.pallas_call(kernel_a,
        out_shape=(sds((1024,768),bf16),head,head,head,head,sds((1024,128),f32),sds((512,768),f32),half,half),
        in_specs=[sm()]+[vm()]*5, out_specs=[vm()]*9,
        scratch_shapes=[pltpu.VMEM((6,GRID_ROWS,128),f32),pltpu.VMEM((6,1024,128),f32),pltpu.VMEM((256,768),f32)],
        compiler_params=pltpu.CompilerParams(vmem_limit_bytes=56<<20),
        cost_estimate=pl.CostEstimate(flops=3*10**9,bytes_accessed=12*10**6,transcendentals=2*10**6),
    )(core,tokens,mods,k.astype(f32),wqkv,w_out)

def kernel_b(chip_ref, far_ref, src_ref, mods_ref, bout_ref, branch_ref, middle_ref, shaped_ref):
    gate=mods_ref[2:3,:]; shift=mods_ref[3:4,:]; scale=1.0+mods_ref[4:5,:]
    bias=bout_ref[...]
    def step(r,_):
        rows=at(r*64,64)
        br=chip_ref[rows,:].astype(f32)+far_ref[rows,:].astype(f32)+bias
        mid=src_ref[rows,:]+gate*br
        branch_ref[rows,:]=br; middle_ref[rows,:]=mid
        shaped_ref[rows,:]=(normed_of(mid)[0]*scale+shift).astype(bf16)
        return 0
    lax.fori_loop(0,8,step,0)

def call_b(chip,far,src,mods,b_out):
    big=sds((512,768),f32)
    return pl.pallas_call(kernel_b,out_shape=(big,big,sds((512,768),bf16)),
        in_specs=[vm()]*5,out_specs=[vm()]*3,
        cost_estimate=pl.CostEstimate(flops=10**7,bytes_accessed=7*10**6,transcendentals=0),
    )(chip,far,src,mods,b_out.astype(f32)[None])

def kernel_d(chip_ref, far_ref, branch_ref, middle_ref, cot_ref, mods_ref, gm_ref, ga_ref, sums_ref):
    gate=mods_ref[2:3,:]; scale=1.0+mods_ref[4:5,:]
    def step(r,acc):
        rows=at(r*64,64)
        gs=chip_ref[rows,:].astype(f32)+far_ref[rows,:].astype(f32)
        n,rs=normed_of(middle_ref[rows,:])
        gn=gs*scale
        gm=cot_ref[rows,:].astype(f32)+rs*(gn-jnp.mean(gn,axis=-1,keepdims=True)-n*jnp.mean(gn*n,axis=-1,keepdims=True))
        gm_ref[rows,:]=gm
        ga_ref[rows,:]=(gm*gate).astype(bf16)
        return tuple(o+jnp.sum(v,axis=0,keepdims=True) for o,v in zip(acc,(gm*branch_ref[rows,:],gs,gs*n)))
    acc=lax.fori_loop(0,8,step,tuple(jnp.zeros((1,768),f32) for _ in range(3)))
    for t in range(3): sums_ref[t:t+1,:]=acc[t]

def call_d(chip,far,branch,middle,cot,mods):
    return pl.pallas_call(kernel_d,out_shape=(sds((512,768),f32),sds((512,768),bf16),sds((8,768),f32)),
        in_specs=[vm()]*6,out_specs=[vm()]*3,
        cost_estimate=pl.CostEstimate(flops=10**7,bytes_accessed=8*10**6,transcendentals=0),
    )(chip,far,branch,middle,cot,mods)

def kernel_e(core_ref, own_ref, other_ref, q_ref, k_ref, v_ref, lse_ref, wqkv_ref, wout_ref,
             gb_ref, gp_ref, sums_ref, keep_ref, send_ref, mix):
    core=core_ref[0]
    for half_ref, h in ((own_ref,core),(other_ref,1-core)):
        for x in range(2):
            for g in range(4):
                gb_ref[at(g*256+(8*x+4*h)*16,64),:]=half_ref[x*256+g*64:x*256+g*64+64,:]
    masks=head_masks()
    for g in range(4):
        mix[g,0:16,:]=jnp.zeros((16,768),bf16)
        mix[g,272:288,:]=jnp.zeros((16,768),bf16)
    def attend(g,total):
        rows=at(g*256,256)
        gb=gb_ref[rows,:]
        ga=dot_nn(gb,wout_ref[...]).astype(bf16)
        q=q_ref[rows,:]; k=k_ref[rows,:]; v=v_ref[rows,:]
        zero=jnp.zeros_like(q)
        gq=jnp.zeros((256,192),f32); gk=gq; gv=gq
        for h in range(3):
            s=dot_nt(jnp.where(masks[h],q,zero),k)*0.125
            p=jnp.exp(s-lse_ref[rows,h:h+1])
            gp=dot_nt(jnp.where(masks[h],ga,zero),v)
            ds=(p*(gp-jnp.sum(p*gp,axis=-1,keepdims=True))).astype(bf16)
            gq=jnp.where(masks[h],dot_nn(ds,k),gq)
            gk=jnp.where(masks[h],dot_tn(ds,q),gk)
            gv=jnp.where(masks[h],dot_tn(p.astype(bf16),ga),gv)
        gq=(gq*0.125).astype(bf16); gk=(gk*0.125).astype(bf16); gv=gv.astype(bf16)
        gp_ref[rows,:]=jnp.concatenate([gq,gk,gv],axis=1)
        gm=dot_nt(gq,wqkv_ref[0])+dot_nt(gk,wqkv_ref[1])+dot_nt(gv,wqkv_ref[2])
        mix[g,16:272,:]=gm.astype(bf16)
        return total+jnp.sum(gb.astype(f32),axis=0,keepdims=True)
    sums_ref[0:1,:]=lax.fori_loop(0,4,attend,jnp.zeros((1,768),f32))
    for out_ref, h in ((keep_ref,core),(send_ref,1-core)):
        for x in range(2):
            t=2*x+h
            for g in range(4):
                out_ref[x*320+g*64:x*320+g*64+64,:]=mix[g,pl.ds(pl.multiple_of((1+4*t)*16,16),64),:]
            for b in range(2):
                out_ref[x*320+256+b*16:x*320+272+b*16,:]=mix[2+b,pl.ds(pl.multiple_of(4*t*16,16),16),:]
                out_ref[x*320+288+b*16:x*320+304+b*16,:]=mix[b,pl.ds(pl.multiple_of((4*t+5)*16,16),16),:]

def call_e(core,own,other,q,k,v,lse,wqkv,w_out):
    head=sds((1024,192),bf16); halo=sds((640,768),bf16)
    return pl.pallas_call(kernel_e,out_shape=(sds((1024,768),bf16),sds((1024,576),bf16),sds((8,768),f32),halo,halo),
        in_specs=[sm()]+[vm()]*8,out_specs=[vm()]*5,
        scratch_shapes=[pltpu.VMEM((4,288,768),bf16)],
        compiler_params=pltpu.CompilerParams(vmem_limit_bytes=56<<20),
        cost_estimate=pl.CostEstimate(flops=3*10**9,bytes_accessed=12*10**6,transcendentals=10**6),
    )(core,own,other,q,k,v,lse,wqkv,w_out)

def kernel_f(pos_ref, chip_ref, far_ref, tok_ref, gmid_ref, mods_ref, k_ref, out_ref, sums_ref, grid, shp, gsh, gmn):
    side=pos_ref[1]; place_t=pos_ref[2]
    grid[...]=jnp.zeros_like(grid)
    shift=mods_ref[0:1,:]; scale=1.0+mods_ref[1:2,:]
    def fetch(start,rows):
        keep=chip_ref[pl.ds(pl.multiple_of(side*320+start,16),rows),:].astype(f32)
        return (keep+far_ref[start:start+rows,:].astype(f32)).astype(bf16).astype(f32)
    for g in range(4):
        a,b=g//2,g%2
        v=fetch(g*64,64)
        gm=gmid_ref[pl.ds(pl.multiple_of(side*256+g*64,64),64),:]
        for ii in range(4):
            for tile in range(6):
                cols=slice(tile*128,tile*128+128)
                grid[tile,strided(place(2*ii+a,b)),:]=v[ii*16:ii*16+16,cols]
                gmn[tile,strided((2*ii+a)*32+b),:]=gm[ii*16:ii*16+16,cols]
    for b in range(2):
        up=fetch(256+b*16,16); dn=fetch(288+b*16,16)
        for tile in range(6):
            cols=slice(tile*128,tile*128+128)
            grid[tile,strided(place(-1,b)),:]=up[:,cols]
            grid[tile,strided(place(8,b)),:]=dn[:,cols]
    def norm(r,_):
        n,_r=normed_of(tok_ref[pl.ds(pl.multiple_of(place_t*256+r*32,32),32),:].astype(f32))
        y=n*scale+shift
        for tile in range(6):
            shp[tile,at(r*32,32),:]=y[:,tile*128:tile*128+128]
        return 0
    lax.fori_loop(0,8,norm,0)
    def back(tile,_):
        cols=pl.ds(pl.multiple_of(tile*128,128),128)
        taps=[k_ref[t:t+1,cols] for t in range(9)]
        def row(i,acc):
            seen=patch(grid,tile,i)
            acc=list(acc)
            for a in range(2):
                for b in range(2):
                    here=shp[tile,strided((2*i+a)*32+b),:]
                    total=None
                    for t in range(9):
                        s=seen[a+2-t//3][b+2-t%3]
                        total=taps[t]*s if total is None else total+taps[t]*s
                        p=here*s
                        acc[t]=acc[t]+(p[:8]+p[8:])
                    gsh[tile,strided((2*i+a)*32+b),:]=total
            return tuple(acc)
        acc=lax.fori_loop(0,4,row,tuple(jnp.zeros((8,128),f32) for _ in range(9)))
        for t in range(9):
            sums_ref[t:t+1,cols]=jnp.sum(acc[t],axis=0,keepdims=True)
        return 0
    lax.fori_loop(0,6,back,0)
    def fin(r,acc):
        n,rs=normed_of(tok_ref[pl.ds(pl.multiple_of(place_t*256+r*32,32),32),:].astype(f32))
        gs=jnp.concatenate([gsh[tile,at(r*32,32),:] for tile in range(6)],axis=1)
        gm=jnp.concatenate([gmn[tile,at(r*32,32),:] for tile in range(6)],axis=1)
        gn=gs*scale
        out_ref[at(r*32,32),:]=gm+rs*(gn-jnp.mean(gn,axis=-1,keepdims=True)-n*jnp.mean(gn*n,axis=-1,keepdims=True))
        return (acc[0]+jnp.sum(gs,axis=0,keepdims=True),acc[1]+jnp.sum(gs*n,axis=0,keepdims=True))
    acc=lax.fori_loop(0,8,fin,tuple(jnp.zeros((1,768),f32) for _ in range(2)))
    sums_ref[9:10,:]=acc[0]; sums_ref[10:11,:]=acc[1]

def call_f(pos,chip,far,tokens,gmid,mods,k):
    return pl.pallas_call(kernel_f,out_shape=(sds((256,768),f32),sds((16,768),f32)),
        in_specs=[sm()]+[vm()]*6,out_specs=[vm()]*2,
        scratch_shapes=[pltpu.VMEM((6,10*PITCH+16,128),f32)]+[pltpu.VMEM((6,256,128),f32)]*3,
        compiler_params=pltpu.CompilerParams(vmem_limit_bytes=56<<20),
        cost_estimate=pl.CostEstimate(flops=10**7,bytes_accessed=6*10**6,transcendentals=0),
    )(pos,chip,far,tokens,gmid,mods,k.astype(f32))

def kernel_p(core_ref, live_ref, cot_ref, mods_ref, gb_ref, half_ref, xs):
    core=core_ref[0]; live=live_ref[0]
    def spread(i,_):
        x=cot_ref[at(i*64,64),:].astype(f32)*live
        for tile in range(6):
            xs[tile,at(i*64,64),:]=x[:,tile*128:tile*128+128]
        return 0
    lax.fori_loop(0,16,spread,0)
    def group(tile,_):
        cols=pl.ds(pl.multiple_of(tile*128,128),128)
        gate=mods_ref[5:6,cols]
        def row(i,_):
            for g in range(4):
                gb_ref[at(g*256+i*16,16),cols]=(xs[tile,strided((2*i+g//2)*32+g%2),:]*gate).astype(bf16)
            return 0
        lax.fori_loop(0,16,row,0)
        for x in range(2):
            for g in range(4):
                for ii in range(4):
                    i=8*x+4*core+ii
                    half_ref[x*256+g*64+ii*16:x*256+g*64+ii*16+16,cols]=xs[tile,strided((2*i+g//2)*32+g%2),:].astype(bf16)
        return 0
    lax.fori_loop(0,6,group,0)

def call_p(core,live,cot,mods):
    return pl.pallas_call(kernel_p,out_shape=(sds((1024,768),bf16),sds((512,768),bf16)),
        in_specs=[sm(),sm(),vm(),vm()],out_specs=[vm()]*2,
        scratch_shapes=[pltpu.VMEM((6,1024,128),f32)],
        compiler_params=pltpu.CompilerParams(vmem_limit_bytes=56<<20),
        cost_estimate=pl.CostEstimate(flops=10**7,bytes_accessed=4*10**6,transcendentals=0),
    )(core,live,cot,mods)

def kernel_o(pos_ref, live_ref, chip_ref, far_ref, middle_ref, cot_ref, mods_ref, bias_ref, out_ref, sums_ref, nat):
    side=pos_ref[1]; live=live_ref[0]
    gate=mods_ref[5:6,:]; bias=bias_ref[...]
    total=jnp.zeros((1,768),f32)
    for g in range(4):
        a,b=g//2,g%2
        rows=pl.ds(pl.multiple_of(side*256+g*64,64),64)
        br=chip_ref[rows,:].astype(f32)+far_ref[g*64:g*64+64,:].astype(f32)+bias
        res=(middle_ref[rows,:]+gate*br)*live
        total=total+jnp.sum(cot_ref[rows,:].astype(f32)*br,axis=0,keepdims=True)
        for ii in range(4):
            for tile in range(6):
                nat[tile,strided((2*ii+a)*32+b),:]=res[ii*16:ii*16+16,tile*128:tile*128+128]
    sums_ref[0:1,:]=total
    for tile in range(6):
        out_ref[:,tile*128:tile*128+128]=nat[tile,:,:].astype(bf16)

def call_o(pos,live,chip,far,middle,cot,mods,bias):
    return pl.pallas_call(kernel_o,out_shape=(sds((256,768),bf16),sds((8,768),f32)),
        in_specs=[sm(),sm()]+[vm()]*6,out_specs=[vm()]*2,
        scratch_shapes=[pltpu.VMEM((6,256,128),f32)],
        compiler_params=pltpu.CompilerParams(vmem_limit_bytes=56<<20),
        cost_estimate=pl.CostEstimate(flops=10**7,bytes_accessed=4*10**6,transcendentals=0),
    )(pos,live,chip,far,middle,cot,mods,bias.astype(f32)[None])


def kernel_w(split, pos_ref, a_ref, b_ref, *outs):
    m=a_ref.shape[1];
    if split:
        keep_ref,send_ref,total=outs
    else:
        (total,)=outs
    def step(i,_):
        total[at(i*256,256),:]=dot_tn(a_ref[:,at(i*256,256)],b_ref[...])
        return 0
    lax.fori_loop(0,m//256,step,0)
    if split:
        mine=pos_ref[3]%2
        block=m//split
        for j in range(split//2):
            keep_ref[j*block:(j+1)*block,:]=total[pl.ds(pl.multiple_of((2*j+mine)*block,8),block),:]
            send_ref[j*block:(j+1)*block,:]=total[pl.ds(pl.multiple_of((2*j+1-mine)*block,8),block),:].astype(bf16)

def call_w(pos,a,b,n):
    m,w=a.shape[1],b.shape[1]
    split=n if (m//n)%16==0 else 0
    params=dict(in_specs=[sm(),vm(),vm()],
        compiler_params=pltpu.CompilerParams(vmem_limit_bytes=56<<20),
        cost_estimate=pl.CostEstimate(flops=2*1024*m*w,bytes_accessed=6*10**6,transcendentals=0))
    if split:
        return pl.pallas_call(functools.partial(kernel_w,split),out_shape=(sds((m//2,w),f32),sds((m//2,w),bf16)),
            out_specs=[vm()]*2,scratch_shapes=[pltpu.VMEM((m,w),f32)],**params)(pos,a,b)
    return pl.pallas_call(functools.partial(kernel_w,0),out_shape=sds((m,w),f32),out_specs=vm(),**params)(pos,a,b)


def swap(values, axis, bit):
    size = lax.axis_size(axis)
    return lax.ppermute(values, axis, [(i, i ^ bit) for i in range(size)])


def bits_of(axis):
    return [1 << b for b in range(lax.axis_size(axis).bit_length() - 1)]


def take(values, index):
    return lax.dynamic_index_in_dim(values, index, 0, keepdims=False)


def add_low(left, right):
    return (left.astype(f32) + right.astype(f32)).astype(bf16)


def scatter_sum(grad):
    size = lax.axis_size("dp")
    width = grad.shape[1]
    return scatter_rest(grad.reshape(size, grad.shape[0] // size, width), bits_of("dp"))


def scatter_rest(held, bits):
    here = lax.axis_index("dp")
    for bit in bits:
        mine = (here // bit) % 2
        halves = held.reshape((held.shape[0] // 2, 2) + held.shape[1:])
        sent = lax.dynamic_index_in_dim(halves, 1 - mine, 1, keepdims=False).astype(bf16)
        kept = lax.dynamic_index_in_dim(halves, mine, 1, keepdims=False)
        held = kept + swap(sent, "dp", bit).astype(f32)
    return held[0]


def weight_grad(pos, left, right):
    size = lax.axis_size("dp")
    if right.shape[1] % 256:
        return scatter_sum(dot_tn(left, right))
    made = call_w(pos, left, right, size)
    if not isinstance(made, (tuple, list)):
        return scatter_sum(made)
    keep, send = made
    held = keep + swap(send, "dp", 1).astype(f32)
    return scatter_rest(held.reshape(size // 2, -1, held.shape[1]), bits_of("dp")[1:])


def butterfly(values, axis):
    for bit in bits_of(axis):
        values = values + swap(values, axis, bit)
    return values


def gather_xor(values):
    for bit in bits_of("dp"):
        values = jnp.concatenate([values, swap(values, "dp", bit)], axis=0)
    return values


def tree_sum(values):
    while values.shape[0] > 1:
        values = values[0::2] + values[1::2]
    return values[0]


def time_features(timestep, width):
    half_width = width // 2
    freqs = jnp.exp(-math.log(10000.0) * jnp.arange(half_width, dtype=f32) / half_width)
    angles = timestep.astype(f32)[:, None] * freqs[None, :]
    return jnp.concatenate([jnp.cos(angles), jnp.sin(angles)], axis=1)


def shards(
    tokens,
    cotangent,
    item_count,
    timestep,
    class_id,
    class_table,
    w_mod,
    b_mod,
    k_att,
    w_qkv,
    w_out,
    b_out,
    w_up,
    b_up,
    k_ffn,
    w_down,
    b_down,
):
    width = tokens.shape[1]
    place_t = lax.axis_index("tensor")
    core = place_t % 2
    side = place_t // 2
    here = lax.axis_index("dp")
    pos = jnp.stack([core, side, place_t, here]).astype(jnp.int32)
    live = (item_count > 0).astype(f32)

    cond = time_features(timestep, width) + class_table[class_id[0]].astype(f32)[None, :]
    act_low = jax.nn.silu(cond).astype(bf16)
    mods = (dot_nt(act_low, w_mod) + b_mod.astype(f32)).reshape(6, width)
    card = jnp.concatenate([cond, jnp.broadcast_to(class_id.astype(f32)[:, None], (1, 128))], axis=1)
    cards = gather_xor(card)
    w_three = jnp.swapaxes(w_qkv, 0, 1)

    mixed, query, keys, vals, attended, log_total, source, keep, send = call_a(
        pos, tokens, mods, k_att, w_three, w_out
    )
    chip = add_low(keep, swap(send, "tensor", 1))
    far = swap(chip, "tensor", 2)
    grad_branch_ffn, cot_half = call_p(pos, live, cotangent, mods)
    branch, middle, shaped_own = call_b(chip, far, source, mods, b_out)
    shaped_other = swap(shaped_own, "tensor", 1)

    shaped, activated, grad_hidden, sums_c, b_keep, b_send, g_keep, g_send = call_c(
        pos, shaped_own, shaped_other, grad_branch_ffn, w_up, b_up, k_ffn, w_down
    )
    chip = add_low(g_keep, swap(g_send, "tensor", 1))
    far = swap(chip, "tensor", 2)
    grad_w_down = weight_grad(pos, grad_branch_ffn, activated)
    grad_w_up = weight_grad(pos, shaped, grad_hidden)
    grad_middle, attn_own, sums_d = call_d(chip, far, branch, middle, cot_half, mods)
    attn_other = swap(attn_own, "tensor", 1)

    chip = add_low(b_keep, swap(b_send, "tensor", 1))
    far = swap(take(chip.reshape(2, -1, width), 1 - side), "tensor", 2)
    block_out, sums_o = call_o(pos, live, chip, far, middle, cot_half, mods, b_down)

    grad_branch, grad_project, sums_e, h_keep, h_send = call_e(
        pos, attn_own, attn_other, query, keys, vals, log_total, w_three, w_out
    )
    chip = add_low(h_keep, swap(h_send, "tensor", 1))
    far = swap(take(chip.reshape(2, -1, width), 1 - side), "tensor", 2)
    grad_w_out = weight_grad(pos, grad_branch, attended)
    grad_w_qkv = weight_grad(pos, mixed, grad_project)
    grad_w_qkv = grad_w_qkv.reshape(grad_w_qkv.shape[0], 3, -1)
    grad_tokens, sums_f = call_f(pos, chip, far, tokens, grad_middle, mods, k_att)

    early = butterfly(jnp.concatenate([sums_c[:11], sums_e[:1]]), "dp")

    once = jnp.where(side == 0, 1.0, 0.0)
    late = jnp.concatenate([sums_f[9:11], sums_d[:3] * once, sums_o[:1], sums_f[:9]])
    late = butterfly(late, "tensor")
    grad_k_att = butterfly(late[6:], "dp")
    grad_modulate = gather_xor(late[:6].reshape(1, -1).astype(bf16))

    grad_b_mod = tree_sum(grad_modulate.astype(f32))
    conds = cards[:, :width]
    classes = cards[:, width]
    act, silu_back = jax.vjp(jax.nn.silu, conds)
    share = w_mod.shape[0] // lax.axis_size("dp")
    own_rows = lax.dynamic_slice_in_dim(grad_modulate, here * share, share, 1)
    grad_w_mod = dot_tn(own_rows, act.astype(bf16))
    grad_cond = silu_back(dot_nn(grad_modulate, w_mod))[0]
    same = (classes[:, None] == classes[None, :]).astype(f32)
    class_rows = tree_sum(same[:, :, None] * grad_cond[:, None, :])
    grad_class = jnp.zeros(class_table.shape, f32).at[classes.astype(jnp.int32)].set(class_rows)

    return (
        block_out,
        grad_tokens,
        grad_class,
        grad_w_mod,
        grad_b_mod,
        grad_k_att,
        grad_w_qkv,
        grad_w_out,
        early[11],
        grad_w_up,
        early[9],
        early[:9],
        grad_w_down,
        early[10],
    )


def solution(mesh):
    placed = (
        P("dp", None),
        P("dp", None),
        P("dp"),
        P("dp"),
        P("dp"),
        P(),
        P(),
        P(),
        P(),
        P(None, None, "tensor"),
        P(None, "tensor"),
        P(),
        P(None, "tensor"),
        P("tensor"),
        P(None, "tensor"),
        P(None, "tensor"),
        P(),
    )
    return jax.shard_map(
        shards,
        mesh=mesh,
        in_specs=placed,
        out_specs=(
            P(("dp", "tensor"), None),
            P(("dp", "tensor"), None),
            P(),
            P("dp", None),
            P(),
            P(),
            P("dp", None, "tensor"),
            P("dp", "tensor"),
            P(),
            P("dp", "tensor"),
            P("tensor"),
            P(None, "tensor"),
            P("dp", "tensor"),
            P(),
        ),
        check_vma=False,
    )
```

```python
import math

import jax
import jax.numpy as jnp
from jax import lax
from jax.experimental import pallas as pl
from jax.experimental.pallas import tpu as pltpu
from jax.sharding import PartitionSpec as P

f32 = jnp.float32
bf16 = jnp.bfloat16

WIDTH = 768
TILES = WIDTH // 128
SIDE = 32
ITEM = SIDE * SIDE
HALF = ITEM // 2
SHARE = ITEM // 4
HALO = SHARE + 2 * SIDE
HEADS_HERE = 3
HEAD_WIDTH = 192
PITCH = 40
GRID_ROWS = 34 * PITCH + 8
SHARE_GRID_ROWS = 10 * PITCH + 16

norm_eps = 1e-06
score_scale = 0.125
gelu_slope = math.sqrt(2.0 / math.pi)
gelu_cubic = 0.044715
COST = 1000
BLOCK = 96
TAIL = 16


def dot_nn(left, right):
    return lax.dot_general(left, right, (((1,), (0,)), ((), ())), preferred_element_type=f32)


def dot_nt(left, right):
    return lax.dot_general(left, right, (((1,), (1,)), ((), ())), preferred_element_type=f32)


def dot_tn(left, right):
    return lax.dot_general(left, right, (((0,), (0,)), ((), ())), preferred_element_type=f32)


def at(start, size):
    return pl.ds(pl.multiple_of(start, size), size)


def at16(start, size):
    return pl.ds(pl.multiple_of(start, 16), size)


def tile_cols(tile):
    return pl.ds(pl.multiple_of(tile * 128, 128), 128)


def spot(row, col):
    return (row + 1) * PITCH + 8 + col


def every_other(start):
    return pl.ds(start, 16, stride=2)


def window(grid, tile, i):
    return [
        [grid[tile, every_other(spot(2 * i + row, col)), :] for col in range(-1, 3)]
        for row in range(-1, 3)
    ]


def here_core():
    place = lax.axis_index("tensor")
    return lax.rem(place, 2), lax.div(place, 2), place


def normed_of(values):
    center = values - jnp.mean(values, axis=-1, keepdims=True)
    scale = lax.rsqrt(jnp.mean(center * center, axis=-1, keepdims=True) + norm_eps)
    return center * scale, scale


def norm_back(normed, scale, grad):
    spread = jnp.mean(grad * normed, axis=-1, keepdims=True)
    return scale * (grad - jnp.mean(grad, axis=-1, keepdims=True) - normed * spread)


def row_of(flat, start=0):
    return flat[pl.ds(start, WIDTH)].astype(f32).reshape(1, WIDTH)


def column_sum(values):
    return jnp.sum(values, axis=0, keepdims=True)


def head_masks():
    lane = lax.broadcasted_iota(jnp.int32, (SHARE, HEAD_WIDTH), 1)
    return [(lane >= 64 * h) & (lane < 64 * h + 64) for h in range(HEADS_HERE)]


def split_halves(values, core, group, keep, send):
    for x in range(2):
        rows = at(x * SHARE + group * 64, 64)
        keep[rows, :] = values[at((2 * x + core) * 64, 64), :].astype(bf16)
        send[rows, :] = values[at((2 * x + 1 - core) * 64, 64), :].astype(bf16)


def join_halves(own, other, core, full):
    for half, h in ((own, core), (other, 1 - core)):
        for x in range(2):
            for g in range(4):
                rows = at(g * SHARE + (8 * x + 4 * h) * 16, 64)
                full[rows, :] = half[x * SHARE + g * 64 : x * SHARE + g * 64 + 64, :]


def take_half(natural, core, tile, half, cols):
    for x in range(2):
        for g in range(4):
            for ii in range(4):
                i = 8 * x + 4 * core + ii
                row = x * SHARE + g * 64 + ii * 16
                seen = natural[tile, every_other((2 * i + g // 2) * SIDE + g % 2), :]
                half[row : row + 16, cols] = seen.astype(half.dtype)


def modulation(act, weights, bias, pieces, first):
    return [
        dot_nt(act, weights[(p - first) * WIDTH : (p - first + 1) * WIDTH, :])[:1]
        + row_of(bias, p * WIDTH)
        for p in pieces
    ]


def kernel_a(
    tokens, act, b_mod, k_att, w_qkv, w_out, w_mod,
    mods_out, source, keep, send, mixed_out, q_out, k_out, v_out, att_out, lse_out,
    grid, natural, temp, kernel, weights, mixed, q_all, k_all, v_all, att_all, lse_all, sems, mod_sem,
):
    core, _, _ = here_core()
    fetch = pltpu.make_async_copy(w_mod.at[pl.ds(0, 2 * WIDTH), :], weights, mod_sem)
    fetch.start()
    grid[...] = jnp.zeros_like(grid)
    kernel[0:9, :] = k_att[...].astype(f32)
    fetch.wait()
    shift, scale = modulation(act[...], weights, b_mod, (0, 1), 0)
    mods_out[0:1, :] = shift
    mods_out[1:2, :] = scale
    scale = 1.0 + scale

    def norm(i, carry):
        values = tokens[at(i * 64, 64), :].astype(f32)
        shaped = normed_of(values)[0] * scale + shift
        for tile in range(TILES):
            cols = slice(tile * 128, tile * 128 + 128)
            natural[tile, at(i * 64, 64), :] = values[:, cols]
            for r in range(2):
                rows = pl.ds(pl.multiple_of((2 * i + r + 1) * PITCH + 8, 8), SIDE)
                grid[tile, rows, :] = shaped[SIDE * r : SIDE * r + SIDE, cols]
        return carry

    lax.fori_loop(0, 16, norm, 0)

    def conv(tile, carry):
        cols = tile_cols(tile)
        taps = [kernel[t : t + 1, cols] for t in range(9)]

        def row(i, inner):
            seen = window(grid, tile, i)
            for a in range(2):
                for b in range(2):
                    total = taps[0] * seen[a][b]
                    for t in range(1, 9):
                        total = total + taps[t] * seen[a + t // 3][b + t % 3]
                    mixed[at16((2 * a + b) * SHARE + i * 16, 16), cols] = total.astype(bf16)
            return inner

        lax.fori_loop(0, 16, row, 0)
        take_half(natural, core, tile, source, cols)
        return carry

    lax.fori_loop(0, TILES, conv, 0)
    masks = head_masks()
    lane = lax.broadcasted_iota(jnp.int32, (SHARE, 128), 1)
    pairs = (
        (mixed, mixed_out), (q_all, q_out), (k_all, k_out),
        (v_all, v_out), (att_all, att_out), (lse_all, lse_out),
    )

    def copies(g):
        rows = at(g * SHARE, SHARE)
        return [
            pltpu.make_async_copy(left.at[rows, :], right.at[rows, :], sems.at[n, g])
            for n, (left, right) in enumerate(pairs)
        ]

    def attend(g, carry):
        rows = at(g * SHARE, SHARE)
        values = mixed[rows, :]
        query, keys, vals = (dot_nt(values, w_qkv[kind]).astype(bf16) for kind in range(3))
        q_all[rows, :] = query
        k_all[rows, :] = keys
        v_all[rows, :] = vals
        attended = jnp.zeros((SHARE, HEAD_WIDTH), f32)
        lse = jnp.zeros((SHARE, 128), f32)
        for h in range(HEADS_HERE):
            scores = dot_nt(jnp.where(masks[h], query, jnp.zeros_like(query)), keys) * score_scale
            top = jnp.max(scores, axis=-1, keepdims=True)
            grown = jnp.exp(scores - top)
            total = jnp.sum(grown, axis=-1, keepdims=True)
            probs = (grown * (1.0 / total)).astype(bf16)
            attended = jnp.where(masks[h], dot_nn(probs, vals), attended)
            lse = jnp.where(lane == h, top + jnp.log(total), lse)
        lse_all[rows, :] = lse
        attended = attended.astype(bf16)
        att_all[rows, :] = attended
        for copy in copies(g):
            copy.start()
        temp[...] = dot_nn(attended, w_out[...])
        split_halves(temp, core, g, keep, send)
        return carry

    lax.fori_loop(0, 4, attend, 0)

    def finish(g, carry):
        for copy in copies(g):
            copy.wait()
        return carry

    lax.fori_loop(0, 4, finish, 0)


def kernel_p(
    count, cotangent, act, b_mod, w_mod,
    mods_out, grad_branch, half, other,
    natural, weights, sem,
):
    core, _, _ = here_core()
    fetch = pltpu.make_async_copy(w_mod.at[pl.ds(2 * WIDTH, 4 * WIDTH), :], weights, sem)
    fetch.start()
    live = jnp.where(count[0] > 0, 1.0, 0.0)

    def spread(i, carry):
        values = cotangent[at(i * 64, 64), :].astype(f32) * live
        for tile in range(TILES):
            natural[tile, at(i * 64, 64), :] = values[:, tile * 128 : tile * 128 + 128]
        return carry

    lax.fori_loop(0, 16, spread, 0)
    fetch.wait()
    for p, row in zip(range(2, 6), modulation(act[...], weights, b_mod, range(2, 6), 2)):
        mods_out[p : p + 1, :] = row

    def group(tile, carry):
        cols = tile_cols(tile)
        gate = mods_out[5:6, cols]

        def row(i, inner):
            for g in range(4):
                seen = natural[tile, every_other((2 * i + g // 2) * SIDE + g % 2), :]
                grad_branch[at16(g * SHARE + i * 16, 16), cols] = (seen * gate).astype(bf16)
            return inner

        lax.fori_loop(0, 16, row, 0)
        take_half(natural, core, tile, half, cols)
        take_half(natural, 1 - core, tile, other, cols)
        return carry

    lax.fori_loop(0, TILES, group, 0)


def kernel_b(chip, far, source, mods, b_out, branch_out, middle_out, shaped_out):
    gate = mods[2:3, :]
    shift = mods[3:4, :]
    scale = 1.0 + mods[4:5, :]
    bias = row_of(b_out)

    def step(r, carry):
        rows = at(r * 64, 64)
        branch = chip[rows, :].astype(f32) + far[rows, :].astype(f32) + bias
        middle = source[rows, :] + gate * branch
        branch_out[rows, :] = branch
        middle_out[rows, :] = middle
        shaped_out[rows, :] = (normed_of(middle)[0] * scale + shift).astype(bf16)
        return carry

    lax.fori_loop(0, HALF // 64, step, 0)


def kernel_c(
    own, other, grad_branch, w_up, w_down, b_up, k_ffn,
    shaped, activated, grad_hidden, sums, b_keep, b_send, g_keep, g_send,
    hidden, grad_conv, grad_act, temp, kernel,
):
    core, _, _ = here_core()
    hidden[...] = jnp.zeros_like(hidden)
    grad_conv[...] = jnp.zeros_like(grad_conv)
    kernel[0:9, :] = k_ffn[...].astype(f32)
    bias = row_of(b_up)
    join_halves(own, other, core, shaped)

    def up(g, carry):
        rows = at(g * SHARE, SHARE)
        a = lax.div(g, 2)
        b = lax.rem(g, 2)
        grad_act[rows, :] = dot_nn(grad_branch[rows, :], w_down[...])
        temp[...] = dot_nn(shaped[rows, :], w_up[...]) + bias

        def place(i, inner):
            for tile in range(TILES):
                values = temp[at(i * 16, 16), tile * 128 : tile * 128 + 128]
                hidden[tile, every_other(spot(2 * i + a, b)), :] = values
            return inner

        lax.fori_loop(0, 16, place, 0)
        return carry

    lax.fori_loop(0, 4, up, 0)

    def conv(tile, carry):
        cols = tile_cols(tile)
        taps = [kernel[t : t + 1, cols] for t in range(9)]

        def row(i, inner):
            seen = window(hidden, tile, i)
            for a in range(2):
                for b in range(2):
                    rows = at16((2 * a + b) * SHARE + i * 16, 16)
                    u = taps[0] * seen[a][b]
                    for t in range(1, 9):
                        u = u + taps[t] * seen[a + t // 3][b + t % 3]
                    square = u * u
                    bent = jnp.tanh(gelu_slope * u * (1.0 + gelu_cubic * square))
                    part = 0.5 + 0.5 * bent
                    activated[rows, cols] = (u * part).astype(bf16)
                    bend = (1.0 - bent * bent) * (1.0 + (3.0 * gelu_cubic) * square)
                    slope = part + (0.5 * gelu_slope) * u * bend
                    back = grad_act[rows, cols] * slope
                    grad_conv[tile, every_other(spot(2 * i + a, b)), :] = back
            return inner

        lax.fori_loop(0, 16, row, 0)
        return carry

    lax.fori_loop(0, TILES, conv, 0)

    def back(tile, carry):
        cols = tile_cols(tile)
        taps = [kernel[t : t + 1, cols] for t in range(9)]

        def row(i, held):
            held = list(held)
            seen = window(grad_conv, tile, i)
            for a in range(2):
                for b in range(2):
                    here = hidden[tile, every_other(spot(2 * i + a, b)), :]
                    total = None
                    for t in range(9):
                        view = seen[a + 2 - t // 3][b + 2 - t % 3]
                        term = taps[t] * view
                        total = term if total is None else total + term
                        product = here * view
                        held[t] = held[t] + (product[:8] + product[8:])
                    low = total.astype(bf16)
                    grad_hidden[at16((2 * a + b) * SHARE + i * 16, 16), cols] = low
                    low = low.astype(f32)
                    held[9] = held[9] + (low[:8] + low[8:])
            return tuple(held)

        zeros = tuple(jnp.zeros((8, 128), f32) for _ in range(10))
        held = lax.fori_loop(0, 16, row, zeros)
        for t in range(10):
            sums[t : t + 1, cols] = column_sum(held[t])
        return carry

    lax.fori_loop(0, TILES, back, 0)

    def out(g, total):
        rows = at(g * SHARE, SHARE)
        temp[...] = dot_nt(grad_hidden[rows, :], w_up[...])
        split_halves(temp, core, g, g_keep, g_send)
        temp[...] = dot_nt(activated[rows, :], w_down[...])
        split_halves(temp, core, g, b_keep, b_send)
        return total + column_sum(grad_branch[rows, :].astype(f32))

    sums[10:11, :] = lax.fori_loop(0, 4, out, jnp.zeros((1, WIDTH), f32))
    sums[11:16, :] = jnp.zeros((5, WIDTH), f32)


def kernel_d(chip, far, branch, middle, half, mods, grad_middle, grad_attn, sums):
    gate = mods[2:3, :]
    scale = 1.0 + mods[4:5, :]

    def step(r, held):
        rows = at(r * 64, 64)
        grad = chip[rows, :].astype(f32) + far[rows, :].astype(f32)
        normed, size = normed_of(middle[rows, :])
        total = half[rows, :].astype(f32) + norm_back(normed, size, grad * scale)
        low = (total * gate).astype(bf16)
        grad_middle[rows, :] = total
        grad_attn[rows, :] = low
        terms = (total * branch[rows, :], grad, grad * normed, low.astype(f32))
        return tuple(h + column_sum(t) for h, t in zip(held, terms))

    zeros = tuple(jnp.zeros((1, WIDTH), f32) for _ in range(4))
    held = lax.fori_loop(0, HALF // 64, step, zeros)
    for t in range(4):
        sums[t : t + 1, :] = held[t]


def kernel_o(count, near, far, middle, mods, b_down, out, natural):
    _, side, _ = here_core()
    live = jnp.where(count[0] > 0, 1.0, 0.0)
    gate = mods[5:6, :]
    bias = row_of(b_down)
    for g in range(4):
        part = slice(g * 64, g * 64 + 64)
        rows = at(side * SHARE + g * 64, 64)
        branch = near[part, :].astype(f32) + far[part, :].astype(f32) + bias
        result = (middle[rows, :] + gate * branch) * live
        for ii in range(4):
            place = every_other((2 * ii + g // 2) * SIDE + g % 2)
            for tile in range(TILES):
                cols = slice(tile * 128, tile * 128 + 128)
                natural[tile, place, :] = result[ii * 16 : ii * 16 + 16, cols]
    for tile in range(TILES):
        out[:, tile * 128 : tile * 128 + 128] = natural[tile, :, :].astype(bf16)


def kernel_e(
    own, other, q_all, k_all, v_all, att_all, lse_all, w_qkv, w_out,
    grad_branch, right, mixed, keep, send,
    padded,
):
    core, _, _ = here_core()
    join_halves(own, other, core, grad_branch)
    masks = head_masks()
    for g in range(4):
        padded[g, 0:16, :] = jnp.zeros((16, WIDTH), bf16)
        padded[g, 272:288, :] = jnp.zeros((16, WIDTH), bf16)

    def attend(g, carry):
        rows = at(g * SHARE, SHARE)
        grad = dot_nt(grad_branch[rows, :], w_out[...]).astype(bf16)
        query = q_all[rows, :]
        keys = k_all[rows, :]
        vals = v_all[rows, :]
        zero = jnp.zeros_like(query)
        g_query = jnp.zeros((SHARE, HEAD_WIDTH), f32)
        g_keys = g_query
        g_vals = g_query
        for h in range(HEADS_HERE):
            scores = dot_nt(jnp.where(masks[h], query, zero), keys) * score_scale
            probs = jnp.exp(scores - lse_all[rows, h : h + 1])
            g_probs = dot_nt(jnp.where(masks[h], grad, zero), vals)
            spread = jnp.sum(probs * g_probs, axis=-1, keepdims=True)
            g_scores = (probs * (g_probs - spread)).astype(bf16)
            g_query = jnp.where(masks[h], dot_nn(g_scores, keys), g_query)
            g_keys = jnp.where(masks[h], dot_tn(g_scores, query), g_keys)
            g_vals = jnp.where(masks[h], dot_tn(probs.astype(bf16), grad), g_vals)
        g_query = (g_query * score_scale).astype(bf16)
        g_keys = (g_keys * score_scale).astype(bf16)
        g_vals = g_vals.astype(bf16)
        right[rows, :] = jnp.concatenate([g_query, g_keys, g_vals, att_all[rows, :]], axis=1)
        total = dot_nn(g_query, w_qkv[0]) + dot_nn(g_keys, w_qkv[1]) + dot_nn(g_vals, w_qkv[2])
        low = total.astype(bf16)
        padded[g, 16:272, :] = low
        mixed[rows, :] = low
        return carry

    lax.fori_loop(0, 4, attend, 0)
    for out, h in ((keep, core), (send, 1 - core)):
        for x in range(2):
            share = 2 * x + h
            first = x * HALO
            for g in range(4):
                rows = at16((1 + 4 * share) * 16, 64)
                out[first + g * 64 : first + g * 64 + 64, :] = padded[g, rows, :]
            for b in range(2):
                row = first + SHARE + b * 16
                out[row : row + 16, :] = padded[2 + b, at16(4 * share * 16, 16), :]
                row = row + SIDE
                out[row : row + 16, :] = padded[b, at16((4 * share + 5) * 16, 16), :]


def kernel_n(tokens, natural):
    def step(i, carry):
        normed = normed_of(tokens[at(i * 64, 64), :].astype(f32))[0]
        for tile in range(TILES):
            natural[tile, at(i * 64, 64), :] = normed[:, tile * 128 : tile * 128 + 128]
        return carry

    lax.fori_loop(0, 16, step, 0)


def kernel_q(keep, send, own, other, b_down, sums):
    _, _, place = here_core()
    once = jnp.where(place == 0, 1.0, 0.0)
    bias = row_of(b_down) * once

    def step(r, total):
        rows = at(r * 64, 64)
        near = own[rows, :].astype(f32) * (keep[rows, :].astype(f32) + bias)
        away = other[rows, :].astype(f32) * (send[rows, :].astype(f32) + bias)
        return total + column_sum(near + away)

    sums[0:1, :] = lax.fori_loop(0, HALF // 64, step, jnp.zeros((1, WIDTH), f32))


def kernel_s(natural, mixed, mods, k_att, sums_d, sums_q, out, grid, kernel):
    _, side, _ = here_core()
    grid[...] = jnp.zeros_like(grid)
    kernel[0:9, :] = k_att[...].astype(f32)

    def norm(i, carry):
        for g in range(4):
            values = mixed[at16(g * SHARE + i * 16, 16), :].astype(f32)
            place = every_other(spot(2 * i + g // 2, g % 2))
            for tile in range(TILES):
                grid[tile, place, :] = values[:, tile * 128 : tile * 128 + 128]
        return carry

    lax.fori_loop(0, 16, norm, 0)

    def gather(tile, carry):
        cols = tile_cols(tile)
        taps = [kernel[t : t + 1, cols] for t in range(9)]

        def row(i, held):
            held = list(held)
            seen = window(grid, tile, i)
            for a in range(2):
                for b in range(2):
                    here = natural[tile, every_other((2 * i + a) * SIDE + b), :]
                    for t in range(9):
                        product = here * seen[a + 2 - t // 3][b + 2 - t % 3]
                        held[t] = held[t] + (product[:8] + product[8:])
                    center = seen[a + 1][b + 1]
                    held[9] = held[9] + (center[:8] + center[8:])
            return tuple(held)

        zeros = tuple(jnp.zeros((8, 128), f32) for _ in range(10))
        held = [column_sum(h) for h in lax.fori_loop(0, 16, row, zeros)]
        edge_row = [
            column_sum(grid[tile, pl.ds(spot(r, 0), SIDE), :]) if r is not None else 0.0
            for r in (0, None, SIDE - 1)
        ]
        edge_col = [
            column_sum(grid[tile, pl.ds(spot(0, c), SIDE, stride=PITCH), :])
            if c is not None
            else 0.0
            for c in (0, None, SIDE - 1)
        ]
        shift = mods[0:1, cols]
        scale = 1.0 + mods[1:2, cols]
        shift_sum = jnp.zeros((1, 128), f32)
        scale_sum = jnp.zeros((1, 128), f32)
        for t in range(9):
            a, b = t // 3, t % 3
            plain = held[9] - edge_row[a] - edge_col[b]
            if a != 1 and b != 1:
                corner = spot((SIDE - 1) * (a // 2), (SIDE - 1) * (b // 2))
                plain = plain + grid[tile, pl.ds(corner, 1), :]
            out[6 + t : 7 + t, cols] = scale * held[t] + shift * plain
            shift_sum = shift_sum + taps[t] * plain
            scale_sum = scale_sum + taps[t] * held[t]
        out[0:1, cols] = shift_sum
        out[1:2, cols] = scale_sum
        return carry

    lax.fori_loop(0, TILES, gather, 0)
    once = jnp.where(side == 0, 1.0, 0.0)
    out[2:5, :] = sums_d[0:3, :] * once
    out[5:6, :] = sums_q[0:1, :]
    out[15:16, :] = sums_d[3:4, :] * once


def kernel_f(tokens, near, far, grad_middle, mods, k_att, out, grid, grad_shaped, middle, kernel):
    _, side, place = here_core()
    grid[...] = jnp.zeros_like(grid)
    kernel[0:9, :] = k_att[...].astype(f32)
    scale = 1.0 + mods[1:2, :]

    def fetch(start, rows):
        part = slice(start, start + rows)
        total = near[part, :].astype(f32) + far[part, :].astype(f32)
        return total.astype(bf16).astype(f32)

    for g in range(4):
        a, b = g // 2, g % 2
        values = fetch(g * 64, 64)
        grads = grad_middle[at(side * SHARE + g * 64, 64), :]
        for ii in range(4):
            rows = slice(ii * 16, ii * 16 + 16)
            for tile in range(TILES):
                cols = slice(tile * 128, tile * 128 + 128)
                grid[tile, every_other(spot(2 * ii + a, b)), :] = values[rows, cols]
                middle[tile, every_other((2 * ii + a) * SIDE + b), :] = grads[rows, cols]
    for b in range(2):
        above = fetch(SHARE + b * 16, 16)
        below = fetch(SHARE + SIDE + b * 16, 16)
        for tile in range(TILES):
            cols = slice(tile * 128, tile * 128 + 128)
            grid[tile, every_other(spot(-1, b)), :] = above[:, cols]
            grid[tile, every_other(spot(8, b)), :] = below[:, cols]

    def conv(tile, carry):
        cols = tile_cols(tile)
        taps = [kernel[t : t + 1, cols] for t in range(9)]

        def row(i, inner):
            seen = window(grid, tile, i)
            for a in range(2):
                for b in range(2):
                    total = taps[0] * seen[a + 2][b + 2]
                    for t in range(1, 9):
                        total = total + taps[t] * seen[a + 2 - t // 3][b + 2 - t % 3]
                    grad_shaped[tile, every_other((2 * i + a) * SIDE + b), :] = total
            return inner

        lax.fori_loop(0, 4, row, 0)
        return carry

    lax.fori_loop(0, TILES, conv, 0)

    def finish(r, carry):
        rows = at(r * SIDE, SIDE)
        values = tokens[at(place * SHARE + r * SIDE, SIDE), :].astype(f32)
        normed, size = normed_of(values)
        grad = jnp.concatenate([grad_shaped[tile, rows, :] for tile in range(TILES)], axis=1)
        base = jnp.concatenate([middle[tile, rows, :] for tile in range(TILES)], axis=1)
        out[rows, :] = base + norm_back(normed, size, grad * scale)
        return carry

    lax.fori_loop(0, SHARE // SIDE, finish, 0)


def bit_here(bit):
    return lax.rem(lax.div(lax.axis_index("dp"), bit), 2)


def split_blocks(blocks, stride, bit, values, keep, send):
    mine = bit_here(bit)
    for j in range(blocks // 2):
        base = (j // stride) * 2 * stride + j % stride
        rows = slice(j * BLOCK, (j + 1) * BLOCK)
        keep[rows, :] = values(at16((base + mine * stride) * BLOCK, BLOCK))
        send[rows, :] = values(at16((base + (1 - mine) * stride) * BLOCK, BLOCK)).astype(bf16)


def summed(held, came):
    return lambda rows: held[rows, :] + came[rows, :].astype(f32)


def kernel_w(grad, activated, shaped, hidden, sums, d_keep, d_send, u_keep, u_send, total):
    for left, right, stride, keep, send in (
        (grad, activated, 1, d_keep, d_send),
        (shaped, hidden, 2, u_keep, u_send),
    ):

        def step(i, carry):
            total[at(i * 256, 256), :] = dot_tn(left[:, at(i * 256, 256)], right[...])
            return carry

        lax.fori_loop(0, 3, step, 0)
        split_blocks(8, stride, stride, lambda rows: total[rows, :], keep, send)
    d_keep[4 * BLOCK :, :] = sums[...].astype(bf16).astype(f32)
    d_send[4 * BLOCK :, :] = sums[...].astype(bf16)


def kernel_w_one(d_held, d_came, u_held, u_came, d_keep, d_send, u_keep, u_send):
    split_blocks(4, 1, 2, summed(d_held, d_came), d_keep, d_send)
    tail = summed(d_held, d_came)(slice(4 * BLOCK, 4 * BLOCK + TAIL)).astype(bf16)
    d_keep[2 * BLOCK :, :] = tail.astype(f32)
    d_send[2 * BLOCK :, :] = tail
    split_blocks(4, 2, 4, summed(u_held, u_came), u_keep, u_send)


def kernel_w_two(d_held, d_came, u_held, u_came, d_keep, d_send, u_keep, u_send):
    split_blocks(2, 1, 4, summed(d_held, d_came), d_keep, d_send)
    tail = summed(d_held, d_came)(slice(2 * BLOCK, 2 * BLOCK + TAIL)).astype(bf16)
    d_keep[BLOCK:, :] = tail.astype(f32)
    d_send[BLOCK:, :] = tail
    split_blocks(2, 1, 1, summed(u_held, u_came), u_keep, u_send)


def kernel_w_end(d_held, d_came, u_held, u_came, down, up, k_out, b_up, b_down):
    total = summed(d_held, d_came)
    down[...] = total(slice(0, BLOCK))
    up[...] = summed(u_held, u_came)(slice(0, BLOCK))
    tail = total(slice(BLOCK, BLOCK + TAIL))
    k_out[...] = tail[0:9, :]
    b_up[...] = tail[9:10, :].reshape(WIDTH)
    b_down[...] = tail[10:11, :].reshape(WIDTH)


def kernel_v(mixed, grad_branch, right, a_keep, a_send, b_keep, b_send, total):
    lane = lax.broadcasted_iota(jnp.int32, (256, 256), 1)

    def step(i, carry):
        cols = at(i * 256, 256)
        total[cols, 0:512] = dot_tn(mixed[:, cols], right[:, 0:512])
        last = right[:, 512:768]
        total[cols, 512:768] = jnp.where(
            lane < 64, dot_tn(mixed[:, cols], last), dot_tn(grad_branch[:, cols], last)
        )
        return carry

    lax.fori_loop(0, 3, step, 0)
    split_blocks(8, 1, 1, lambda rows: total[rows, 0:384], a_keep, a_send)
    split_blocks(8, 2, 2, lambda rows: total[rows, 384:768], b_keep, b_send)


def kernel_v_one(a_held, a_came, b_held, b_came, a_keep, a_send, b_keep, b_send):
    split_blocks(4, 1, 2, summed(a_held, a_came), a_keep, a_send)
    split_blocks(4, 2, 4, summed(b_held, b_came), b_keep, b_send)


def kernel_v_two(a_held, a_came, b_held, b_came, a_keep, a_send, b_keep, b_send):
    split_blocks(2, 1, 4, summed(a_held, a_came), a_keep, a_send)
    split_blocks(2, 1, 1, summed(b_held, b_came), b_keep, b_send)


def kernel_v_end(a_held, a_came, b_held, b_came, qkv, out):
    first = summed(a_held, a_came)(slice(0, BLOCK))
    last = summed(b_held, b_came)(slice(0, BLOCK))
    qkv[0] = first[:, :HEAD_WIDTH]
    qkv[1] = first[:, HEAD_WIDTH:]
    qkv[2] = last[:, :HEAD_WIDTH]
    out[...] = last[:, HEAD_WIDTH:]


def kernel_join(near, came, chip):
    chip[...] = (near[...].astype(f32) + came[...].astype(f32)).astype(bf16)


def kernel_join_split(near, came, own, send):
    _, side, _ = here_core()
    rows = own.shape[0]
    for out, x in ((own, side), (send, 1 - side)):
        part = at16(x * rows, rows)
        out[...] = (near[part, :].astype(f32) + came[part, :].astype(f32)).astype(bf16)


def kernel_slot(late, came, cond, out):
    total = late[...] + came[...]
    out[0, 0:6, :] = total[0:6, :].astype(bf16).astype(f32)
    out[0, 6:7, :] = cond[...]
    out[0, 7:8, :] = cond[...]
    out[1] = total[6:14, :]
    out[2, 0:2, :] = total[14:16, :]
    out[2, 2:8, :] = jnp.zeros((6, WIDTH), f32)


def kernel_gather(slots, held, came, out):
    out[0:slots] = held[0:slots]
    out[slots : 2 * slots] = came[0:slots]
    out[2 * slots : 2 * slots + 2] = held[slots : slots + 2] + came[slots : slots + 2]


def kernel_g(
    size, share, ids, near, came, w_mod,
    w_out, b_out, class_out, k_out, bias_out,
    held, lanes, grads, outer,
):
    here = lax.axis_index("dp")
    kernel_gather(size // 2, near, came, held)
    class_out[...] = jnp.zeros_like(class_out)
    conds = held[0:size, 6, :]
    sig = 1.0 / (1.0 + jnp.exp(-conds))
    act = (conds * sig).astype(bf16)
    total = jnp.zeros((size, WIDTH), f32)
    for p in range(6):
        piece = held[0:size, p, :].astype(bf16)
        lanes[:, p * WIDTH : (p + 1) * WIDTH] = piece
        total = total + dot_nn(piece, w_mod[p * WIDTH : (p + 1) * WIDTH, :])
    grads[...] = total * (sig * (1.0 + conds * (1.0 - sig)))
    reach = outer.shape[0]
    first = jnp.minimum(lax.div(here * share, 128) * 128, 6 * WIDTH - reach)
    outer[...] = dot_tn(lanes[:, pl.ds(pl.multiple_of(first, 128), reach)], act)
    w_out[...] = outer[pl.ds(pl.multiple_of(here * share - first, 8), share), :]

    def item(i, bias):
        slot = lax.bitwise_xor(here, i)
        row = pl.ds(ids[slot], 1)
        class_out[row, :] = class_out[row, :] + grads[pl.ds(slot, 1), :]
        return bias + held[slot]

    bias = lax.fori_loop(0, size, item, jnp.zeros((8, WIDTH), f32))
    for p in range(6):
        b_out[pl.ds(p * WIDTH, WIDTH)] = bias[p : p + 1, :].reshape(WIDTH)
    k_out[0:8, :] = held[size]
    k_out[8:9, :] = held[size + 1, 0:1, :]
    bias_out[...] = held[size + 1, 1:2, :].reshape(WIDTH)


def vmem(shape, dtype):
    return pltpu.VMEM(shape, dtype)


def hbm(shape, dtype):
    return pltpu.HBM(shape, dtype)


def plain(shape, dtype):
    return jax.ShapeDtypeStruct(shape, dtype)


def call(kernel, scalars, arrays, far_arrays, outs, scratch, mebibytes, flops, moved):
    spots = (
        [pl.BlockSpec(memory_space=pltpu.SMEM)] * len(scalars)
        + [pl.BlockSpec(memory_space=pltpu.VMEM)] * len(arrays)
        + [pl.BlockSpec(memory_space=pltpu.HBM)] * len(far_arrays)
    )
    spaces = [pltpu.VMEM if getattr(o, "memory_space", None) != pltpu.HBM else pltpu.HBM for o in outs]
    return pl.pallas_call(
        kernel,
        out_shape=tuple(outs),
        in_specs=spots,
        out_specs=tuple(pl.BlockSpec(memory_space=m) for m in spaces),
        scratch_shapes=scratch,
        compiler_params=pltpu.CompilerParams(vmem_limit_bytes=mebibytes << 20),
        cost_estimate=pl.CostEstimate(flops=flops // COST, bytes_accessed=moved // COST, transcendentals=0),
    )(
        *scalars,
        *(pltpu.with_memory_space_constraint(a, pltpu.VMEM) for a in arrays),
        *(pltpu.with_memory_space_constraint(a, pltpu.HBM) for a in far_arrays),
    )


def swap(values, axis, bit):
    size = lax.axis_size(axis)
    return lax.ppermute(values, axis, [(i, i ^ bit) for i in range(size)])


def bits_of(axis):
    return [1 << b for b in range(lax.axis_size(axis).bit_length() - 1)]


def butterfly(values, axis):
    for bit in bits_of(axis):
        values = values + swap(values, axis, bit)
    return values


def gather_xor(values):
    for bit in bits_of("dp"):
        values = jnp.concatenate([values, swap(values, "dp", bit)], axis=0)
    return values


def scatter_plain(total):
    size = lax.axis_size("dp")
    here = lax.axis_index("dp")
    held = total.reshape(total.shape[0], size, -1, total.shape[-1])
    for bit in bits_of("dp"):
        mine = (here // bit) % 2
        parts, blocks, rows, width = held.shape
        halves = held.reshape(parts, blocks // 2, 2, rows, width)
        keep = lax.dynamic_index_in_dim(halves, mine, 2, keepdims=False)
        send = lax.dynamic_index_in_dim(halves, 1 - mine, 2, keepdims=False).astype(bf16)
        held = keep + swap(send, "dp", bit).astype(f32)
    return held[:, 0]


def join(near, came):
    (chip,) = call(kernel_join, [], [near, came], [], [vmem(near.shape, bf16)], [], 4, 10**6, 3 * 10**6)
    return chip


def join_split(near, came):
    part = vmem((near.shape[0] // 2, WIDTH), bf16)
    return call(kernel_join_split, [], [near, came], [], [part, part], [], 4, 10**6, 3 * 10**6)


def weight_step(kernel, blocks, tail, width, *arrays):
    first = (blocks * BLOCK + tail, width)
    last = (blocks * BLOCK, width)
    outs = [vmem(first, f32), vmem(first, bf16), vmem(last, f32), vmem(last, bf16)]
    return call(kernel, [], list(arrays), [], outs, [], 4, 10**6, 4 * 10**6)


def time_features(timestep):
    half_width = WIDTH // 2
    freqs = jnp.exp(-math.log(10000.0) * jnp.arange(half_width, dtype=f32) / half_width)
    angles = timestep.astype(f32)[:, None] * freqs[None, :]
    return jnp.concatenate([jnp.cos(angles), jnp.sin(angles)], axis=1)


def together(*values):
    return lax.optimization_barrier(values)


def shards(
    tokens,
    cotangent,
    item_count,
    timestep,
    class_id,
    class_table,
    w_mod,
    b_mod,
    k_att,
    w_qkv,
    w_out,
    b_out,
    w_up,
    b_up,
    k_ffn,
    w_down,
    b_down,
):
    items = lax.axis_size("dp")
    bits = bits_of("dp")
    eight = items * BLOCK == WIDTH
    full = (ITEM, WIDTH)
    half = (HALF, WIDTH)
    head = (ITEM, HEAD_WIDTH)
    grid = pltpu.VMEM((TILES, GRID_ROWS, 128), f32)
    natural = pltpu.VMEM((TILES, ITEM, 128), f32)
    share_tiles = pltpu.VMEM((TILES, SHARE, 128), f32)
    temp = pltpu.VMEM((SHARE, WIDTH), f32)
    taps = pltpu.VMEM((16, WIDTH), f32)
    sem = pltpu.SemaphoreType.DMA

    row = lax.dynamic_slice(class_table, (class_id[0], 0), (1, WIDTH), allow_negative_indices=False)
    cond = time_features(timestep) + row.astype(f32)
    act = jnp.broadcast_to(jax.nn.silu(cond).astype(bf16), (16, WIDTH))
    w_three = jnp.transpose(w_qkv, (1, 2, 0))
    w_back = w_out.T

    mods_a, source, keep, send, mixed, query, keys, vals, attended, lse = call(
        kernel_a, [], [tokens, act, b_mod, k_att, w_three, w_back], [w_mod],
        [
            vmem((8, WIDTH), f32), vmem(half, f32), vmem(half, bf16), vmem(half, bf16),
            hbm(full, bf16), hbm(head, bf16), hbm(head, bf16), hbm(head, bf16), hbm(head, bf16),
            hbm((ITEM, 128), f32),
        ],
        [
            grid, natural, temp, taps, pltpu.VMEM((2 * WIDTH, WIDTH), bf16), pltpu.VMEM(full, bf16),
            pltpu.VMEM(head, bf16), pltpu.VMEM(head, bf16), pltpu.VMEM(head, bf16),
            pltpu.VMEM(head, bf16), pltpu.VMEM((ITEM, 128), f32), sem((6, 4)), sem,
        ],
        22, 3 * 10**9, 10**7,
    )
    chip = join(keep, swap(send, "tensor", 1))
    far = swap(chip, "tensor", 2)
    _, cotangent, class_id = together(chip, cotangent, class_id)
    mods_p, grad_ffn, cot_half, cot_other = call(
        kernel_p, [item_count], [cotangent, act, b_mod], [w_mod],
        [vmem((8, WIDTH), f32), vmem(full, bf16), vmem(half, bf16), vmem(half, bf16)],
        [natural, pltpu.VMEM((4 * WIDTH, WIDTH), bf16), sem], 12, 10**8, 8 * 10**6,
    )
    ids = gather_xor(class_id)
    far, mods_p, ids = together(far, mods_p, ids)
    branch, middle, shaped_own = call(
        kernel_b, [], [chip, far, source, mods_p, b_out], [],
        [vmem(half, f32), vmem(half, f32), vmem(half, bf16)], [], 6, 10**7, 7 * 10**6,
    )
    shaped_other = swap(shaped_own, "tensor", 1)

    shaped, activated, grad_hidden, sums_c, b_keep, b_send, g_keep, g_send = call(
        kernel_c, [], [shaped_own, shaped_other, grad_ffn, w_up, w_down, b_up, k_ffn], [],
        [vmem(full, bf16)] * 3 + [vmem((16, WIDTH), f32)] + [vmem(half, bf16)] * 4,
        [grid, grid, pltpu.VMEM(full, f32), temp, taps], 16, 5 * 10**9, 12 * 10**6,
    )
    chip = join(g_keep, swap(g_send, "tensor", 1))
    far = swap(chip, "tensor", 2)
    _, activated, b_send, sums_c = together(chip, activated, b_send, sums_c)
    b_own, b_part = join_split(b_keep, swap(b_send, "tensor", 1))
    b_far = swap(b_part, "tensor", 2)
    if eight:
        d_keep, d_send, u_keep, u_send = call(
            kernel_w, [], [grad_ffn, activated, shaped, grad_hidden, sums_c], [],
            [
                vmem((4 * BLOCK + TAIL, WIDTH), f32), vmem((4 * BLOCK + TAIL, WIDTH), bf16),
                vmem((4 * BLOCK, WIDTH), f32), vmem((4 * BLOCK, WIDTH), bf16),
            ],
            [pltpu.VMEM((WIDTH, WIDTH), f32)], 6, 24 * 10**8, 9 * 10**6,
        )
        d_came = swap(d_send, "dp", 1)
        u_came = swap(u_send, "dp", 2)
        tokens_n, b_keep, _, _ = together(tokens, b_keep, d_send, u_send)
    else:
        ffn_grads = scatter_plain(
            jnp.stack([dot_tn(grad_ffn, activated), dot_tn(shaped, grad_hidden)])
        )
        early = butterfly(sums_c, "dp")
        tokens_n = tokens
    (normed,) = call(
        kernel_n, [], [tokens_n], [], [vmem((TILES, ITEM, 128), f32)], [], 4, 10**7, 5 * 10**6
    )
    (sums_q,) = call(
        kernel_q, [], [b_keep, b_send, cot_half, cot_other, b_down], [], [vmem((8, WIDTH), f32)], [],
        4, 10**7, 4 * 10**6,
    )
    far, _, _ = together(far, normed, sums_q)
    if eight:
        far, d_came, u_came = together(far, d_came, u_came)
        d_keep, d_send, u_keep, u_send = weight_step(
            kernel_w_one, 2, TAIL, WIDTH, d_keep, d_came, u_keep, u_came
        )
        d_came = swap(d_send, "dp", 2)
        u_came = swap(u_send, "dp", 4)
    grad_middle, attn_own, sums_d = call(
        kernel_d, [], [chip, far, branch, middle, cot_half, mods_p], [],
        [vmem(half, f32), vmem(half, bf16), vmem((8, WIDTH), f32)], [], 6, 10**7, 8 * 10**6,
    )
    attn_other = swap(attn_own, "tensor", 1)

    grad_attn, right, mixed_grad, h_keep, h_send = call(
        kernel_e, [],
        [attn_own, attn_other, query, keys, vals, attended, lse, w_three, w_back], [],
        [vmem(full, bf16)] * 3 + [vmem((2 * HALO, WIDTH), bf16)] * 2,
        [pltpu.VMEM((4, 288, WIDTH), bf16)], 8, 3 * 10**9, 10**7,
    )
    h_came = swap(h_send, "tensor", 1)
    w_mod_late, _ = together(w_mod, mixed_grad)
    if eight:
        a_keep, a_send, e_keep, e_send = call(
            kernel_v, [], [mixed, grad_attn, right], [],
            [vmem((4 * BLOCK, 384), f32), vmem((4 * BLOCK, 384), bf16)] * 2,
            [pltpu.VMEM((WIDTH, WIDTH), f32)], 6, 16 * 10**8, 7 * 10**6,
        )
        h_came, d_came, u_came, mixed_grad, _, _ = together(
            h_came, d_came, u_came, mixed_grad, a_send, e_send
        )
        a_came = swap(a_send, "dp", 1)
        e_came = swap(e_send, "dp", 2)
        d_keep, d_send, u_keep, u_send = weight_step(
            kernel_w_two, 1, TAIL, WIDTH, d_keep, d_came, u_keep, u_came
        )
        d_came = swap(d_send, "dp", 4)
        u_came = swap(u_send, "dp", 1)
    else:
        last = dot_tn(grad_attn, right[:, 3 * HEAD_WIDTH :])
        total = jnp.concatenate([dot_tn(mixed, right[:, : 3 * HEAD_WIDTH]), last], axis=1)
        att_grads = scatter_plain(total[None])[0]
    h_own, h_part = join_split(h_keep, h_came)
    h_far = swap(h_part, "tensor", 2)
    (late,) = call(
        kernel_s, [], [normed, mixed_grad, mods_a, k_att, sums_d, sums_q], [],
        [vmem((16, WIDTH), f32)], [grid, taps], 8, 10**8, 4 * 10**6,
    )
    late = late + swap(late, "tensor", 1)
    late_came = swap(late, "tensor", 2)
    b_far, _ = together(b_far, late)
    (block_out,) = call(
        kernel_o, [item_count], [b_own, b_far, middle, mods_p, b_down], [],
        [plain((SHARE, WIDTH), bf16)], [share_tiles], 4, 10**7, 4 * 10**6,
    )
    late_came, _ = together(late_came, block_out)
    (held,) = call(
        kernel_slot, [], [late, late_came, cond], [], [vmem((3, 8, WIDTH), f32)], [], 2, 10**5, 10**5
    )
    came = swap(held, "dp", bits[0])
    if eight:
        a_came, e_came, _ = together(a_came, e_came, held)
        a_keep, a_send, e_keep, e_send = weight_step(
            kernel_v_one, 2, 0, 384, a_keep, a_came, e_keep, e_came
        )
        a_came = swap(a_send, "dp", 2)
        e_came = swap(e_send, "dp", 4)
        came, _ = together(came, a_send)
    for step, bit in enumerate(bits[1:], 1):
        slots = 1 << (step - 1)

        def kernel(*refs, slots=slots):
            kernel_gather(slots, *refs)

        (held,) = call(
            kernel, [], [held, came], [], [vmem((2 * slots + 2, 8, WIDTH), f32)], [], 4, 10**5, 10**5
        )
        came = swap(held, "dp", bit)
        if step == 1:
            h_far, _ = together(h_far, held)
            (grad_tokens,) = call(
                kernel_f, [], [tokens, h_own, h_far, grad_middle, mods_a, k_att], [],
                [plain((SHARE, WIDTH), f32)],
                [pltpu.VMEM((TILES, SHARE_GRID_ROWS, 128), f32), share_tiles, share_tiles, taps],
                6, 10**7, 6 * 10**6,
            )
            came, _ = together(came, grad_tokens)
    if eight:
        a_came, e_came, _ = together(a_came, e_came, held)
        a_keep, a_send, e_keep, e_send = weight_step(
            kernel_v_two, 1, 0, 384, a_keep, a_came, e_keep, e_came
        )
        a_came = swap(a_send, "dp", 4)
        e_came = swap(e_send, "dp", 1)
        came, _ = together(came, a_send)

    share = w_mod.shape[0] // items

    def kernel(*refs):
        kernel_g(items, share, *refs)

    grad_w_mod, grad_b_mod, grad_class, grad_k_att, grad_b_out = call(
        kernel, [ids], [held, came, w_mod_late], [],
        [
            plain((share, WIDTH), f32), plain(w_mod.shape[:1], f32), plain(class_table.shape, f32),
            plain((9, WIDTH), f32), plain((WIDTH,), f32),
        ],
        [
            pltpu.VMEM((items + 2, 8, WIDTH), f32), pltpu.VMEM((items, 6 * WIDTH), bf16),
            pltpu.VMEM((items, WIDTH), f32), pltpu.VMEM(((share + 254) // 128 * 128, WIDTH), f32),
        ],
        12, 10**8, 14 * 10**6,
    )

    if eight:
        rows = plain((BLOCK, WIDTH), f32)
        flat = plain((WIDTH,), f32)
        grad_down, grad_up, grad_k_ffn, grad_b_up, grad_b_down = call(
            kernel_w_end, [], [d_keep, d_came, u_keep, u_came], [],
            [rows, rows, plain((9, WIDTH), f32), flat, flat], [], 4, 10**6, 2 * 10**6,
        )
        a_came, e_came, _, _ = together(a_came, e_came, grad_b_mod, grad_b_up)
        grad_qkv, grad_out = call(
            kernel_v_end, [], [a_keep, a_came, e_keep, e_came], [],
            [plain((3, BLOCK, HEAD_WIDTH), f32), plain((BLOCK, HEAD_WIDTH), f32)], [], 4, 10**6, 10**6,
        )
        grad_qkv = jnp.transpose(grad_qkv, (1, 0, 2))
    else:
        grad_down, grad_up = ffn_grads[0], ffn_grads[1]
        grad_k_ffn, grad_b_up, grad_b_down = early[:9], early[9], early[10]
        grad_qkv = att_grads[:, : 3 * HEAD_WIDTH].reshape(-1, 3, HEAD_WIDTH)
        grad_out = att_grads[:, 3 * HEAD_WIDTH :]
    return (
        block_out,
        grad_tokens,
        grad_class,
        grad_w_mod,
        grad_b_mod,
        grad_k_att,
        grad_qkv,
        grad_out,
        grad_b_out,
        grad_up,
        grad_b_up,
        grad_k_ffn,
        grad_down,
        grad_b_down,
    )


def solution(mesh):
    placed = (
        P("dp", None),
        P("dp", None),
        P("dp"),
        P("dp"),
        P("dp"),
        P(),
        P(),
        P(),
        P(),
        P(None, None, "tensor"),
        P(None, "tensor"),
        P(),
        P(None, "tensor"),
        P("tensor"),
        P(None, "tensor"),
        P(None, "tensor"),
        P(),
    )
    return jax.shard_map(
        shards,
        mesh=mesh,
        in_specs=placed,
        out_specs=(
            P(("dp", "tensor"), None),
            P(("dp", "tensor"), None),
            P(),
            P("dp", None),
            P(),
            P(),
            P("dp", None, "tensor"),
            P("dp", "tensor"),
            P(),
            P("dp", "tensor"),
            P("tensor"),
            P(None, "tensor"),
            P("dp", "tensor"),
            P(),
        ),
        check_vma=False,
    )
```

```python
import math

import jax
import jax.numpy as jnp
from jax import lax
from jax.experimental import pallas as pl
from jax.experimental.pallas import tpu as pltpu
from jax.sharding import PartitionSpec as P

f32 = jnp.float32
bf16 = jnp.bfloat16

WIDTH = 768
TILES = WIDTH // 128
SIDE = 32
ITEM = SIDE * SIDE
HALF = ITEM // 2
SHARE = ITEM // 4
HALO = SHARE + 2 * SIDE
HEADS_HERE = 3
HEAD_WIDTH = 192
PITCH = 40
GRID_ROWS = 34 * PITCH + 8
SHARE_GRID_ROWS = 10 * PITCH + 16

norm_eps = 1e-06
score_scale = 0.125
gelu_slope = math.sqrt(2.0 / math.pi)
gelu_cubic = 0.044715
BLOCK = 96
TAIL = 16


def dot_nn(left, right):
    return lax.dot_general(left, right, (((1,), (0,)), ((), ())), preferred_element_type=f32)


def dot_nt(left, right):
    return lax.dot_general(left, right, (((1,), (1,)), ((), ())), preferred_element_type=f32)


def dot_tn(left, right):
    return lax.dot_general(left, right, (((0,), (0,)), ((), ())), preferred_element_type=f32)


def at(start, size):
    return pl.ds(pl.multiple_of(start, size), size)


def at16(start, size):
    return pl.ds(pl.multiple_of(start, 16), size)


def tile_cols(tile):
    return pl.ds(pl.multiple_of(tile * 128, 128), 128)


def spot(row, col):
    return (row + 1) * PITCH + 8 + col


def every_other(start):
    return pl.ds(start, 16, stride=2)


def window(grid, tile, i):
    return [
        [grid[tile, every_other(spot(2 * i + row, col)), :] for col in range(-1, 3)]
        for row in range(-1, 3)
    ]


def here_core():
    place = lax.axis_index("tensor")
    return lax.rem(place, 2), lax.div(place, 2), place


def normed_of(values):
    center = values - jnp.mean(values, axis=-1, keepdims=True)
    scale = lax.rsqrt(jnp.mean(center * center, axis=-1, keepdims=True) + norm_eps)
    return center * scale, scale


def norm_back(normed, scale, grad):
    spread = jnp.mean(grad * normed, axis=-1, keepdims=True)
    return scale * (grad - jnp.mean(grad, axis=-1, keepdims=True) - normed * spread)


def row_of(flat, start=0):
    return flat[pl.ds(start, WIDTH)].astype(f32).reshape(1, WIDTH)


def column_sum(values):
    return jnp.sum(values, axis=0, keepdims=True)


def head_masks():
    lane = lax.broadcasted_iota(jnp.int32, (SHARE, HEAD_WIDTH), 1)
    return [(lane >= 64 * h) & (lane < 64 * h + 64) for h in range(HEADS_HERE)]


def split_halves(values, core, group, keep, send):
    for x in range(2):
        rows = at(x * SHARE + group * 64, 64)
        keep[rows, :] = values[at((2 * x + core) * 64, 64), :].astype(bf16)
        send[rows, :] = values[at((2 * x + 1 - core) * 64, 64), :].astype(bf16)


def join_halves(own, other, core, full):
    for half, h in ((own, core), (other, 1 - core)):
        for x in range(2):
            for g in range(4):
                rows = at(g * SHARE + (8 * x + 4 * h) * 16, 64)
                full[rows, :] = half[x * SHARE + g * 64 : x * SHARE + g * 64 + 64, :]


def take_half(natural, core, tile, half, cols):
    for x in range(2):
        for g in range(4):
            for ii in range(4):
                i = 8 * x + 4 * core + ii
                row = x * SHARE + g * 64 + ii * 16
                seen = natural[tile, every_other((2 * i + g // 2) * SIDE + g % 2), :]
                half[row : row + 16, cols] = seen.astype(half.dtype)


def modulation(act, weights, bias, pieces, first):
    return [
        dot_nt(act, weights[(p - first) * WIDTH : (p - first + 1) * WIDTH, :])[:1]
        + row_of(bias, p * WIDTH)
        for p in pieces
    ]


def kernel_a(
    act, tokens_far, b_mod_far, k_att_far, w_qkv_far, w_out_far, w_mod,
    mods_out, source, keep, send, mixed_out, q_out, k_out, v_out, att_out, lse_out,
    grid, natural, temp, kernel, tokens, b_mod, k_att, w_qkv, w_out, weights,
    mixed, q_all, k_all, v_all, att_all, lse_all, sems, in_sems,
):
    core, _, _ = here_core()
    fetches = [
        pltpu.make_async_copy(far, near, in_sems.at[n])
        for n, (far, near) in enumerate(
            (
                (w_mod.at[pl.ds(0, 2 * WIDTH), :], weights),
                (b_mod_far, b_mod),
                (k_att_far, k_att),
                (tokens_far, tokens),
                (w_qkv_far, w_qkv),
                (w_out_far, w_out),
            )
        )
    ]
    for fetch in fetches:
        fetch.start()
    grid[...] = jnp.zeros_like(grid)
    for fetch in fetches[:4]:
        fetch.wait()
    kernel[0:9, :] = k_att[...].astype(f32)
    shift, scale = modulation(act[...], weights, b_mod, (0, 1), 0)
    mods_out[0:1, :] = shift
    mods_out[1:2, :] = scale
    scale = 1.0 + scale

    def norm(i, carry):
        values = tokens[at(i * 64, 64), :].astype(f32)
        shaped = normed_of(values)[0] * scale + shift
        for tile in range(TILES):
            cols = slice(tile * 128, tile * 128 + 128)
            natural[tile, at(i * 64, 64), :] = values[:, cols]
            for r in range(2):
                rows = pl.ds(pl.multiple_of((2 * i + r + 1) * PITCH + 8, 8), SIDE)
                grid[tile, rows, :] = shaped[SIDE * r : SIDE * r + SIDE, cols]
        return carry

    lax.fori_loop(0, 16, norm, 0)

    def conv(tile, carry):
        cols = tile_cols(tile)
        taps = [kernel[t : t + 1, cols] for t in range(9)]

        def row(i, inner):
            seen = window(grid, tile, i)
            for a in range(2):
                for b in range(2):
                    total = taps[0] * seen[a][b]
                    for t in range(1, 9):
                        total = total + taps[t] * seen[a + t // 3][b + t % 3]
                    mixed[at16((2 * a + b) * SHARE + i * 16, 16), cols] = total.astype(bf16)
            return inner

        lax.fori_loop(0, 16, row, 0)
        take_half(natural, core, tile, source, cols)
        return carry

    lax.fori_loop(0, TILES, conv, 0)
    for fetch in fetches[4:]:
        fetch.wait()
    masks = head_masks()
    lane = lax.broadcasted_iota(jnp.int32, (SHARE, 128), 1)
    pairs = (
        (mixed, mixed_out), (q_all, q_out), (k_all, k_out),
        (v_all, v_out), (att_all, att_out), (lse_all, lse_out),
    )

    def copies(g):
        rows = at(g * SHARE, SHARE)
        return [
            pltpu.make_async_copy(left.at[rows, :], right.at[rows, :], sems.at[n, g])
            for n, (left, right) in enumerate(pairs)
        ]

    def attend(g, carry):
        rows = at(g * SHARE, SHARE)
        values = mixed[rows, :]
        query, keys, vals = (dot_nt(values, w_qkv[kind]).astype(bf16) for kind in range(3))
        q_all[rows, :] = query
        k_all[rows, :] = keys
        v_all[rows, :] = vals
        attended = jnp.zeros((SHARE, HEAD_WIDTH), f32)
        lse = jnp.zeros((SHARE, 128), f32)
        for h in range(HEADS_HERE):
            scores = dot_nt(jnp.where(masks[h], query, jnp.zeros_like(query)), keys) * score_scale
            top = jnp.max(scores, axis=-1, keepdims=True)
            grown = jnp.exp(scores - top)
            total = jnp.sum(grown, axis=-1, keepdims=True)
            probs = (grown * (1.0 / total)).astype(bf16)
            attended = jnp.where(masks[h], dot_nn(probs, vals), attended)
            lse = jnp.where(lane == h, top + jnp.log(total), lse)
        lse_all[rows, :] = lse
        attended = attended.astype(bf16)
        att_all[rows, :] = attended
        for copy in copies(g):
            copy.start()
        temp[...] = dot_nn(attended, w_out[...])
        split_halves(temp, core, g, keep, send)
        return carry

    lax.fori_loop(0, 4, attend, 0)

    def finish(g, carry):
        for copy in copies(g):
            copy.wait()
        return carry

    lax.fori_loop(0, 4, finish, 0)


def kernel_p(
    count, cotangent, act, b_mod, w_mod,
    mods_out, grad_branch, half, other,
    natural, weights, sem,
):
    core, _, _ = here_core()
    fetch = pltpu.make_async_copy(w_mod.at[pl.ds(2 * WIDTH, 4 * WIDTH), :], weights, sem)
    fetch.start()
    live = jnp.where(count[0] > 0, 1.0, 0.0)

    def spread(i, carry):
        values = cotangent[at(i * 64, 64), :].astype(f32) * live
        for tile in range(TILES):
            natural[tile, at(i * 64, 64), :] = values[:, tile * 128 : tile * 128 + 128]
        return carry

    lax.fori_loop(0, 16, spread, 0)
    fetch.wait()
    for p, row in zip(range(2, 6), modulation(act[...], weights, b_mod, range(2, 6), 2)):
        mods_out[p : p + 1, :] = row

    def group(tile, carry):
        cols = tile_cols(tile)
        gate = mods_out[5:6, cols]

        def row(i, inner):
            for g in range(4):
                seen = natural[tile, every_other((2 * i + g // 2) * SIDE + g % 2), :]
                grad_branch[at16(g * SHARE + i * 16, 16), cols] = (seen * gate).astype(bf16)
            return inner

        lax.fori_loop(0, 16, row, 0)
        take_half(natural, core, tile, half, cols)
        take_half(natural, 1 - core, tile, other, cols)
        return carry

    lax.fori_loop(0, TILES, group, 0)


def kernel_ga(grad_branch, w_down, grad_act):
    def step(g, carry):
        rows = at(g * SHARE, SHARE)
        grad_act[rows, :] = dot_nn(grad_branch[rows, :], w_down[...])
        return carry

    lax.fori_loop(0, 4, step, 0)


def kernel_b(chip, far, source, mods, b_out, branch_out, middle_out, shaped_out):
    gate = mods[2:3, :]
    shift = mods[3:4, :]
    scale = 1.0 + mods[4:5, :]
    bias = row_of(b_out)

    def step(r, carry):
        rows = at(r * 64, 64)
        branch = chip[rows, :].astype(f32) + far[rows, :].astype(f32) + bias
        middle = source[rows, :] + gate * branch
        branch_out[rows, :] = branch
        middle_out[rows, :] = middle
        shaped_out[rows, :] = (normed_of(middle)[0] * scale + shift).astype(bf16)
        return carry

    lax.fori_loop(0, HALF // 64, step, 0)


def kernel_c(
    own, other, grad_branch, grad_act, w_up, w_down, b_up, k_ffn,
    shaped, activated, grad_hidden, sums, b_keep, b_send, g_keep, g_send,
    hidden, grad_conv, temp, kernel,
):
    core, _, _ = here_core()
    hidden[...] = jnp.zeros_like(hidden)
    grad_conv[...] = jnp.zeros_like(grad_conv)
    kernel[0:9, :] = k_ffn[...].astype(f32)
    bias = row_of(b_up)
    join_halves(own, other, core, shaped)

    def up(g, carry):
        rows = at(g * SHARE, SHARE)
        a = lax.div(g, 2)
        b = lax.rem(g, 2)
        temp[...] = dot_nn(shaped[rows, :], w_up[...]) + bias

        def place(i, inner):
            for tile in range(TILES):
                values = temp[at(i * 16, 16), tile * 128 : tile * 128 + 128]
                hidden[tile, every_other(spot(2 * i + a, b)), :] = values
            return inner

        lax.fori_loop(0, 16, place, 0)
        return carry

    lax.fori_loop(0, 4, up, 0)

    def conv(tile, carry):
        cols = tile_cols(tile)
        taps = [kernel[t : t + 1, cols] for t in range(9)]

        def row(i, inner):
            seen = window(hidden, tile, i)
            for a in range(2):
                for b in range(2):
                    rows = at16((2 * a + b) * SHARE + i * 16, 16)
                    u = taps[0] * seen[a][b]
                    for t in range(1, 9):
                        u = u + taps[t] * seen[a + t // 3][b + t % 3]
                    square = u * u
                    bent = jnp.tanh(gelu_slope * u * (1.0 + gelu_cubic * square))
                    part = 0.5 + 0.5 * bent
                    activated[rows, cols] = (u * part).astype(bf16)
                    bend = (1.0 - bent * bent) * (1.0 + (3.0 * gelu_cubic) * square)
                    slope = part + (0.5 * gelu_slope) * u * bend
                    back = grad_act[rows, cols] * slope
                    grad_conv[tile, every_other(spot(2 * i + a, b)), :] = back
            return inner

        lax.fori_loop(0, 16, row, 0)
        return carry

    lax.fori_loop(0, TILES, conv, 0)

    def back(tile, carry):
        cols = tile_cols(tile)
        taps = [kernel[t : t + 1, cols] for t in range(9)]

        def row(i, held):
            held = list(held)
            seen = window(grad_conv, tile, i)
            for a in range(2):
                for b in range(2):
                    here = hidden[tile, every_other(spot(2 * i + a, b)), :]
                    total = None
                    for t in range(9):
                        view = seen[a + 2 - t // 3][b + 2 - t % 3]
                        term = taps[t] * view
                        total = term if total is None else total + term
                        product = here * view
                        held[t] = held[t] + (product[:8] + product[8:])
                    low = total.astype(bf16)
                    grad_hidden[at16((2 * a + b) * SHARE + i * 16, 16), cols] = low
                    low = low.astype(f32)
                    held[9] = held[9] + (low[:8] + low[8:])
            return tuple(held)

        zeros = tuple(jnp.zeros((8, 128), f32) for _ in range(10))
        held = lax.fori_loop(0, 16, row, zeros)
        for t in range(10):
            sums[t : t + 1, cols] = column_sum(held[t])
        return carry

    lax.fori_loop(0, TILES, back, 0)

    def out(g, total):
        rows = at(g * SHARE, SHARE)
        temp[...] = dot_nt(grad_hidden[rows, :], w_up[...])
        split_halves(temp, core, g, g_keep, g_send)
        temp[...] = dot_nt(activated[rows, :], w_down[...])
        split_halves(temp, core, g, b_keep, b_send)
        return total + column_sum(grad_branch[rows, :].astype(f32))

    sums[10:11, :] = lax.fori_loop(0, 4, out, jnp.zeros((1, WIDTH), f32))
    sums[11:16, :] = jnp.zeros((5, WIDTH), f32)


def kernel_d(chip, far, branch, middle, half, mods, grad_middle, grad_attn, sums):
    gate = mods[2:3, :]
    scale = 1.0 + mods[4:5, :]

    def step(r, held):
        rows = at(r * 64, 64)
        grad = chip[rows, :].astype(f32) + far[rows, :].astype(f32)
        normed, size = normed_of(middle[rows, :])
        total = half[rows, :].astype(f32) + norm_back(normed, size, grad * scale)
        low = (total * gate).astype(bf16)
        grad_middle[rows, :] = total
        grad_attn[rows, :] = low
        terms = (total * branch[rows, :], grad, grad * normed, low.astype(f32))
        return tuple(h + column_sum(t) for h, t in zip(held, terms))

    zeros = tuple(jnp.zeros((1, WIDTH), f32) for _ in range(4))
    held = lax.fori_loop(0, HALF // 64, step, zeros)
    for t in range(4):
        sums[t : t + 1, :] = held[t]


def kernel_o(count, near, far, middle, mods, b_down, out, natural):
    _, side, _ = here_core()
    live = jnp.where(count[0] > 0, 1.0, 0.0)
    gate = mods[5:6, :]
    bias = row_of(b_down)
    for g in range(4):
        part = slice(g * 64, g * 64 + 64)
        rows = at(side * SHARE + g * 64, 64)
        branch = near[part, :].astype(f32) + far[part, :].astype(f32) + bias
        result = (middle[rows, :] + gate * branch) * live
        for ii in range(4):
            place = every_other((2 * ii + g // 2) * SIDE + g % 2)
            for tile in range(TILES):
                cols = slice(tile * 128, tile * 128 + 128)
                natural[tile, place, :] = result[ii * 16 : ii * 16 + 16, cols]
    for tile in range(TILES):
        out[:, tile * 128 : tile * 128 + 128] = natural[tile, :, :].astype(bf16)


def kernel_p_again(q_all, k_all, lse_all, probs_all):
    masks = head_masks()

    def step(g, carry):
        rows = at(g * SHARE, SHARE)
        query = q_all[rows, :]
        keys = k_all[rows, :]
        for h in range(HEADS_HERE):
            scores = dot_nt(jnp.where(masks[h], query, jnp.zeros_like(query)), keys) * score_scale
            probs_all[HEADS_HERE * g + h] = jnp.exp(scores - lse_all[rows, h : h + 1])
        return carry

    lax.fori_loop(0, 4, step, 0)


def kernel_e(
    own, other, q_all, k_all, v_all, att_all, probs_all, w_qkv, w_out, mixed_far,
    grad_branch, right, mixed, mixed_near, keep, send,
    padded, sem,
):
    core, _, _ = here_core()
    fetch = pltpu.make_async_copy(mixed_far, mixed_near, sem)
    fetch.start()
    join_halves(own, other, core, grad_branch)
    masks = head_masks()
    for g in range(4):
        padded[g, 0:16, :] = jnp.zeros((16, WIDTH), bf16)
        padded[g, 272:288, :] = jnp.zeros((16, WIDTH), bf16)

    def attend(g, carry):
        rows = at(g * SHARE, SHARE)
        grad = dot_nt(grad_branch[rows, :], w_out[...]).astype(bf16)
        query = q_all[rows, :]
        keys = k_all[rows, :]
        vals = v_all[rows, :]
        zero = jnp.zeros_like(query)
        g_query = jnp.zeros((SHARE, HEAD_WIDTH), f32)
        g_keys = g_query
        g_vals = g_query
        for h in range(HEADS_HERE):
            probs = probs_all[HEADS_HERE * g + h]
            g_probs = dot_nt(jnp.where(masks[h], grad, zero), vals)
            spread = jnp.sum(probs * g_probs, axis=-1, keepdims=True)
            g_scores = (probs * (g_probs - spread)).astype(bf16)
            g_query = jnp.where(masks[h], dot_nn(g_scores, keys), g_query)
            g_keys = jnp.where(masks[h], dot_tn(g_scores, query), g_keys)
            g_vals = jnp.where(masks[h], dot_tn(probs.astype(bf16), grad), g_vals)
        g_query = (g_query * score_scale).astype(bf16)
        g_keys = (g_keys * score_scale).astype(bf16)
        g_vals = g_vals.astype(bf16)
        right[rows, :] = jnp.concatenate([g_query, g_keys, g_vals, att_all[rows, :]], axis=1)
        total = dot_nn(g_query, w_qkv[0]) + dot_nn(g_keys, w_qkv[1]) + dot_nn(g_vals, w_qkv[2])
        low = total.astype(bf16)
        padded[g, 16:272, :] = low
        mixed[rows, :] = low
        return carry

    lax.fori_loop(0, 4, attend, 0)
    for out, h in ((keep, core), (send, 1 - core)):
        for x in range(2):
            share = 2 * x + h
            first = x * HALO
            for g in range(4):
                rows = at16((1 + 4 * share) * 16, 64)
                out[first + g * 64 : first + g * 64 + 64, :] = padded[g, rows, :]
            for b in range(2):
                row = first + SHARE + b * 16
                out[row : row + 16, :] = padded[2 + b, at16(4 * share * 16, 16), :]
                row = row + SIDE
                out[row : row + 16, :] = padded[b, at16((4 * share + 5) * 16, 16), :]
    fetch.wait()


def kernel_n(tokens, natural):
    def step(i, carry):
        normed = normed_of(tokens[at(i * 64, 64), :].astype(f32))[0]
        for tile in range(TILES):
            natural[tile, at(i * 64, 64), :] = normed[:, tile * 128 : tile * 128 + 128]
        return carry

    lax.fori_loop(0, 16, step, 0)


def kernel_q(keep, send, own, other, b_down, sums):
    _, _, place = here_core()
    once = jnp.where(place == 0, 1.0, 0.0)
    bias = row_of(b_down) * once

    def step(r, total):
        rows = at(r * 64, 64)
        near = own[rows, :].astype(f32) * (keep[rows, :].astype(f32) + bias)
        away = other[rows, :].astype(f32) * (send[rows, :].astype(f32) + bias)
        return total + column_sum(near + away)

    sums[0:1, :] = lax.fori_loop(0, HALF // 64, step, jnp.zeros((1, WIDTH), f32))


def kernel_s(natural, mixed, mods, k_att, sums_d, sums_q, low, out, grid, kernel):
    _, side, _ = here_core()
    grid[...] = jnp.zeros_like(grid)
    kernel[0:9, :] = k_att[...].astype(f32)

    def norm(i, carry):
        for g in range(4):
            values = mixed[at16(g * SHARE + i * 16, 16), :].astype(f32)
            place = every_other(spot(2 * i + g // 2, g % 2))
            for tile in range(TILES):
                grid[tile, place, :] = values[:, tile * 128 : tile * 128 + 128]
        return carry

    lax.fori_loop(0, 16, norm, 0)

    def gather(tile, carry):
        cols = tile_cols(tile)
        taps = [kernel[t : t + 1, cols] for t in range(9)]

        def row(i, held):
            held = list(held)
            seen = window(grid, tile, i)
            for a in range(2):
                for b in range(2):
                    here = natural[tile, every_other((2 * i + a) * SIDE + b), :]
                    for t in range(9):
                        product = here * seen[a + 2 - t // 3][b + 2 - t % 3]
                        held[t] = held[t] + (product[:8] + product[8:])
                    center = seen[a + 1][b + 1]
                    held[9] = held[9] + (center[:8] + center[8:])
            return tuple(held)

        zeros = tuple(jnp.zeros((8, 128), f32) for _ in range(10))
        held = [column_sum(h) for h in lax.fori_loop(0, 16, row, zeros)]
        edge_row = [
            column_sum(grid[tile, pl.ds(spot(r, 0), SIDE), :]) if r is not None else 0.0
            for r in (0, None, SIDE - 1)
        ]
        edge_col = [
            column_sum(grid[tile, pl.ds(spot(0, c), SIDE, stride=PITCH), :])
            if c is not None
            else 0.0
            for c in (0, None, SIDE - 1)
        ]
        shift = mods[0:1, cols]
        scale = 1.0 + mods[1:2, cols]
        shift_sum = jnp.zeros((1, 128), f32)
        scale_sum = jnp.zeros((1, 128), f32)
        for t in range(9):
            a, b = t // 3, t % 3
            plain = held[9] - edge_row[a] - edge_col[b]
            if a != 1 and b != 1:
                corner = spot((SIDE - 1) * (a // 2), (SIDE - 1) * (b // 2))
                plain = plain + grid[tile, pl.ds(corner, 1), :]
            out[6 + t : 7 + t, cols] = scale * held[t] + shift * plain
            shift_sum = shift_sum + taps[t] * plain
            scale_sum = scale_sum + taps[t] * held[t]
        out[0:1, cols] = shift_sum
        out[1:2, cols] = scale_sum
        return carry

    lax.fori_loop(0, TILES, gather, 0)
    once = jnp.where(side == 0, 1.0, 0.0)
    out[2:5, :] = sums_d[0:3, :] * once
    out[5:6, :] = sums_q[0:1, :]
    out[15:16, :] = sums_d[3:4, :] * once
    low[...] = out[...].astype(bf16)


def kernel_f(tokens, near, far, grad_middle, mods, k_att, out, grid, grad_shaped, middle, kernel):
    _, side, place = here_core()
    grid[...] = jnp.zeros_like(grid)
    kernel[0:9, :] = k_att[...].astype(f32)
    scale = 1.0 + mods[1:2, :]

    def fetch(start, rows):
        part = slice(start, start + rows)
        total = near[part, :].astype(f32) + far[part, :].astype(f32)
        return total.astype(bf16).astype(f32)

    for g in range(4):
        a, b = g // 2, g % 2
        values = fetch(g * 64, 64)
        grads = grad_middle[at(side * SHARE + g * 64, 64), :]
        for ii in range(4):
            rows = slice(ii * 16, ii * 16 + 16)
            for tile in range(TILES):
                cols = slice(tile * 128, tile * 128 + 128)
                grid[tile, every_other(spot(2 * ii + a, b)), :] = values[rows, cols]
                middle[tile, every_other((2 * ii + a) * SIDE + b), :] = grads[rows, cols]
    for b in range(2):
        above = fetch(SHARE + b * 16, 16)
        below = fetch(SHARE + SIDE + b * 16, 16)
        for tile in range(TILES):
            cols = slice(tile * 128, tile * 128 + 128)
            grid[tile, every_other(spot(-1, b)), :] = above[:, cols]
            grid[tile, every_other(spot(8, b)), :] = below[:, cols]

    def conv(tile, carry):
        cols = tile_cols(tile)
        taps = [kernel[t : t + 1, cols] for t in range(9)]

        def row(i, inner):
            seen = window(grid, tile, i)
            for a in range(2):
                for b in range(2):
                    total = taps[0] * seen[a + 2][b + 2]
                    for t in range(1, 9):
                        total = total + taps[t] * seen[a + 2 - t // 3][b + 2 - t % 3]
                    grad_shaped[tile, every_other((2 * i + a) * SIDE + b), :] = total
            return inner

        lax.fori_loop(0, 4, row, 0)
        return carry

    lax.fori_loop(0, TILES, conv, 0)

    def finish(r, carry):
        rows = at(r * SIDE, SIDE)
        values = tokens[at(place * SHARE + r * SIDE, SIDE), :].astype(f32)
        normed, size = normed_of(values)
        grad = jnp.concatenate([grad_shaped[tile, rows, :] for tile in range(TILES)], axis=1)
        base = jnp.concatenate([middle[tile, rows, :] for tile in range(TILES)], axis=1)
        out[rows, :] = base + norm_back(normed, size, grad * scale)
        return carry

    lax.fori_loop(0, SHARE // SIDE, finish, 0)


def bit_here(bit):
    return lax.rem(lax.div(lax.axis_index("dp"), bit), 2)


def split_blocks(blocks, stride, bit, values, keep, send):
    mine = bit_here(bit)
    for j in range(blocks // 2):
        base = (j // stride) * 2 * stride + j % stride
        rows = slice(j * BLOCK, (j + 1) * BLOCK)
        keep[rows, :] = values(at16((base + mine * stride) * BLOCK, BLOCK))
        send[rows, :] = values(at16((base + (1 - mine) * stride) * BLOCK, BLOCK)).astype(bf16)


def summed(held, came):
    return lambda rows: held[rows, :] + came[rows, :].astype(f32)


def product_tn(left, right, total):
    def step(i, carry):
        total[at(i * 256, 256), :] = dot_tn(left[:, at(i * 256, 256)], right[...])
        return carry

    lax.fori_loop(0, 3, step, 0)


def kernel_w_down(grad, activated, sums, keep, send, total):
    product_tn(grad, activated, total)
    split_blocks(8, 1, 1, lambda rows: total[rows, :], keep, send)
    keep[4 * BLOCK :, :] = sums[...].astype(bf16).astype(f32)
    send[4 * BLOCK :, :] = sums[...].astype(bf16)


def kernel_w_up(shaped, hidden, keep, send, total):
    product_tn(shaped, hidden, total)
    split_blocks(8, 2, 2, lambda rows: total[rows, :], keep, send)


def kernel_w_one(d_held, d_came, u_held, u_came, d_keep, d_send, u_keep, u_send):
    split_blocks(4, 1, 2, summed(d_held, d_came), d_keep, d_send)
    tail = summed(d_held, d_came)(slice(4 * BLOCK, 4 * BLOCK + TAIL)).astype(bf16)
    d_keep[2 * BLOCK :, :] = tail.astype(f32)
    d_send[2 * BLOCK :, :] = tail
    split_blocks(4, 1, 1, summed(u_held, u_came), u_keep, u_send)


def kernel_w_two(d_held, d_came, u_held, u_came, keep, send):
    mine = bit_here(4)
    for n, (held, came) in enumerate(((d_held, d_came), (u_held, u_came))):
        total = summed(held, came)
        rows = slice(n * BLOCK, (n + 1) * BLOCK)
        keep[rows, :] = total(at16(mine * BLOCK, BLOCK))
        send[rows, :] = total(at16((1 - mine) * BLOCK, BLOCK)).astype(bf16)
    tail = summed(d_held, d_came)(slice(2 * BLOCK, 2 * BLOCK + TAIL)).astype(bf16)
    keep[2 * BLOCK :, :] = tail.astype(f32)
    send[2 * BLOCK :, :] = tail


def kernel_w_end(held, came, down, up, k_out, b_up, b_down):
    total = summed(held, came)
    down[...] = total(slice(0, BLOCK))
    up[...] = total(slice(BLOCK, 2 * BLOCK))
    tail = total(slice(2 * BLOCK, 2 * BLOCK + TAIL))
    k_out[...] = tail[0:9, :]
    b_up[...] = tail[9:10, :].reshape(WIDTH)
    b_down[...] = tail[10:11, :].reshape(WIDTH)


def kernel_v(mixed, grad_branch, right, keep, send, total):
    lane = lax.broadcasted_iota(jnp.int32, (256, 256), 1)

    def step(i, carry):
        cols = at(i * 256, 256)
        total[cols, 0:512] = dot_tn(mixed[:, cols], right[:, 0:512])
        last = right[:, 512:768]
        total[cols, 512:768] = jnp.where(
            lane < 64, dot_tn(mixed[:, cols], last), dot_tn(grad_branch[:, cols], last)
        )
        return carry

    lax.fori_loop(0, 3, step, 0)
    split_blocks(8, 1, 1, lambda rows: total[rows, :], keep, send)


def kernel_v_one(held, came, keep, send):
    split_blocks(4, 1, 2, summed(held, came), keep, send)


def kernel_v_two(held, came, keep, send):
    split_blocks(2, 1, 4, summed(held, came), keep, send)


def kernel_v_end(held, came, qkv, out):
    total = summed(held, came)(slice(0, BLOCK))
    for kind in range(3):
        qkv[kind] = total[:, kind * HEAD_WIDTH : (kind + 1) * HEAD_WIDTH]
    out[...] = total[:, 3 * HEAD_WIDTH :]


def kernel_join(near, came, chip):
    chip[...] = (near[...].astype(f32) + came[...].astype(f32)).astype(bf16)


def kernel_join_split(near, came, own, send):
    _, side, _ = here_core()
    rows = own.shape[0]
    for out, x in ((own, side), (send, 1 - side)):
        where = at16(x * rows, rows)
        out[...] = (near[where, :].astype(f32) + came[where, :].astype(f32)).astype(bf16)


def kernel_slot(late, cond, out):
    parts = [late[n].astype(f32) for n in range(4)]
    total = (parts[0] + parts[1]) + (parts[2] + parts[3])
    high = cond[...].astype(bf16).astype(f32)
    out[0] = jnp.concatenate([total[0:6, :], high, cond[...] - high]).astype(bf16)
    out[1] = total[6:14, :].astype(bf16)
    out[2] = jnp.concatenate([total[14:16, :], jnp.zeros((6, WIDTH), f32)]).astype(bf16)


def kernel_gather(slots, held, came, out):
    out[0:slots] = held[0:slots].astype(out.dtype)
    out[slots : 2 * slots] = came[0:slots].astype(out.dtype)
    total = held[slots : slots + 2].astype(f32) + came[slots : slots + 2].astype(f32)
    out[2 * slots : 2 * slots + 2] = total.astype(out.dtype)


def kernel_g(
    size, share, ids, near, came, w_mod,
    w_out, b_out, class_out, k_out, bias_out,
    held, lanes, grads, outer,
):
    here = lax.axis_index("dp")
    kernel_gather(size // 2, near, came, held)
    class_out[...] = jnp.zeros_like(class_out)
    conds = held[0:size, 6, :] + held[0:size, 7, :]
    sig = 1.0 / (1.0 + jnp.exp(-conds))
    act = (conds * sig).astype(bf16)
    total = jnp.zeros((size, WIDTH), f32)
    for p in range(6):
        piece = held[0:size, p, :].astype(bf16)
        lanes[:, p * WIDTH : (p + 1) * WIDTH] = piece
        total = total + dot_nn(piece, w_mod[p * WIDTH : (p + 1) * WIDTH, :])
    grads[...] = total * (sig * (1.0 + conds * (1.0 - sig)))
    reach = outer.shape[0]
    first = jnp.minimum(lax.div(here * share, 128) * 128, 6 * WIDTH - reach)
    outer[...] = dot_tn(lanes[:, pl.ds(pl.multiple_of(first, 128), reach)], act)
    w_out[...] = outer[pl.ds(pl.multiple_of(here * share - first, 8), share), :]

    def item(i, bias):
        slot = lax.bitwise_xor(here, i)
        row = pl.ds(ids[slot], 1)
        class_out[row, :] = class_out[row, :] + grads[pl.ds(slot, 1), :]
        return bias + held[slot]

    bias = lax.fori_loop(0, size, item, jnp.zeros((8, WIDTH), f32))
    for p in range(6):
        b_out[pl.ds(p * WIDTH, WIDTH)] = bias[p : p + 1, :].reshape(WIDTH)
    k_out[0:8, :] = held[size]
    k_out[8:9, :] = held[size + 1, 0:1, :]
    bias_out[...] = held[size + 1, 1:2, :].reshape(WIDTH)


def vmem(shape, dtype):
    return pltpu.VMEM(shape, dtype)


def hbm(shape, dtype):
    return pltpu.HBM(shape, dtype)


def plain(shape, dtype):
    return jax.ShapeDtypeStruct(shape, dtype)


def call(kernel, scalars, arrays, far_arrays, outs, scratch, mebibytes, flops, moved, cost=0):
    spots = (
        [pl.BlockSpec(memory_space=pltpu.SMEM)] * len(scalars)
        + [pl.BlockSpec(memory_space=pltpu.VMEM)] * len(arrays)
        + [pl.BlockSpec(memory_space=pltpu.HBM)] * len(far_arrays)
    )
    spaces = [pltpu.VMEM if getattr(o, "memory_space", None) != pltpu.HBM else pltpu.HBM for o in outs]
    return pl.pallas_call(
        kernel,
        out_shape=tuple(outs),
        in_specs=spots,
        out_specs=tuple(pl.BlockSpec(memory_space=m) for m in spaces),
        scratch_shapes=scratch,
        compiler_params=pltpu.CompilerParams(vmem_limit_bytes=mebibytes << 20),
        cost_estimate=pl.CostEstimate(flops=0, bytes_accessed=cost, transcendentals=0),
    )(
        *scalars,
        *(pltpu.with_memory_space_constraint(a, pltpu.VMEM) for a in arrays),
        *(pltpu.with_memory_space_constraint(a, pltpu.HBM) for a in far_arrays),
    )


def swap(values, axis, bit):
    size = lax.axis_size(axis)
    return lax.ppermute(values, axis, [(i, i ^ bit) for i in range(size)])


def bits_of(axis):
    return [1 << b for b in range(lax.axis_size(axis).bit_length() - 1)]


def butterfly(values, axis):
    for bit in bits_of(axis):
        values = values + swap(values, axis, bit)
    return values


def gather_xor(values):
    for bit in bits_of("dp"):
        values = jnp.concatenate([values, swap(values, "dp", bit)], axis=0)
    return values


def scatter_plain(total):
    size = lax.axis_size("dp")
    here = lax.axis_index("dp")
    held = total.reshape(total.shape[0], size, -1, total.shape[-1])
    for bit in bits_of("dp"):
        mine = (here // bit) % 2
        parts, blocks, rows, width = held.shape
        halves = held.reshape(parts, blocks // 2, 2, rows, width)
        keep = lax.dynamic_index_in_dim(halves, mine, 2, keepdims=False)
        send = lax.dynamic_index_in_dim(halves, 1 - mine, 2, keepdims=False).astype(bf16)
        held = keep + swap(send, "dp", bit).astype(f32)
    return held[:, 0]


def join(near, came):
    (chip,) = call(kernel_join, [], [near, came], [], [vmem(near.shape, bf16)], [], 4, 10**6, 3 * 10**6)
    return chip


def join_split(near, came):
    part = vmem((near.shape[0] // 2, WIDTH), bf16)
    return call(kernel_join_split, [], [near, came], [], [part, part], [], 4, 10**6, 3 * 10**6)


def weight_step(kernel, shapes, *arrays):
    outs = [vmem(shape, kind) for shape in shapes for kind in (f32, bf16)]
    return call(kernel, [], list(arrays), [], outs, [], 4, 10**6, 4 * 10**6)


def time_features(timestep):
    half_width = WIDTH // 2
    freqs = jnp.exp(-math.log(10000.0) * jnp.arange(half_width, dtype=f32) / half_width)
    angles = timestep.astype(f32)[:, None] * freqs[None, :]
    return jnp.concatenate([jnp.cos(angles), jnp.sin(angles)], axis=1)


def together(*values):
    return lax.optimization_barrier(values)


def shards(
    tokens,
    cotangent,
    item_count,
    timestep,
    class_id,
    class_table,
    w_mod,
    b_mod,
    k_att,
    w_qkv,
    w_out,
    b_out,
    w_up,
    b_up,
    k_ffn,
    w_down,
    b_down,
):
    items = lax.axis_size("dp")
    bits = bits_of("dp")
    eight = items * BLOCK == WIDTH
    full = (ITEM, WIDTH)
    half = (HALF, WIDTH)
    head = (ITEM, HEAD_WIDTH)
    grid = pltpu.VMEM((TILES, GRID_ROWS, 128), f32)
    natural = pltpu.VMEM((TILES, ITEM, 128), f32)
    share_tiles = pltpu.VMEM((TILES, SHARE, 128), f32)
    temp = pltpu.VMEM((SHARE, WIDTH), f32)
    taps = pltpu.VMEM((16, WIDTH), f32)
    sem = pltpu.SemaphoreType.DMA

    row = lax.dynamic_slice(class_table, (class_id[0], 0), (1, WIDTH), allow_negative_indices=False)
    cond = time_features(timestep) + row.astype(f32)
    act = jnp.broadcast_to(jax.nn.silu(cond).astype(bf16), (16, WIDTH))
    w_three = jnp.transpose(w_qkv, (1, 2, 0))
    w_back = w_out.T

    mods_a, source, keep, send, mixed, query, keys, vals, attended, lse = call(
        kernel_a, [], [act], [tokens, b_mod, k_att, w_three, w_back, w_mod],
        [
            vmem((8, WIDTH), f32), vmem(half, f32), vmem(half, bf16), vmem(half, bf16),
            hbm(full, bf16), hbm(head, bf16), hbm(head, bf16), hbm(head, bf16), hbm(head, bf16),
            hbm((ITEM, 128), f32),
        ],
        [
            grid, natural, temp, taps, pltpu.VMEM(full, bf16), pltpu.VMEM(b_mod.shape, bf16),
            pltpu.VMEM(k_att.shape, bf16), pltpu.VMEM(w_three.shape, bf16),
            pltpu.VMEM(w_back.shape, bf16), pltpu.VMEM((2 * WIDTH, WIDTH), bf16), pltpu.VMEM(full, bf16),
            pltpu.VMEM(head, bf16), pltpu.VMEM(head, bf16), pltpu.VMEM(head, bf16),
            pltpu.VMEM(head, bf16), pltpu.VMEM((ITEM, 128), f32), sem((6, 4)), sem((6,)),
        ],
        24, 3 * 10**9, 10**7,
    )
    chip = join(keep, swap(send, "tensor", 1))
    far = swap(chip, "tensor", 2)
    _, cotangent, class_id = together(chip, cotangent, class_id)
    mods_p, grad_ffn, cot_half, cot_other = call(
        kernel_p, [item_count], [cotangent, act, b_mod], [w_mod],
        [vmem((8, WIDTH), f32), vmem(full, bf16), vmem(half, bf16), vmem(half, bf16)],
        [natural, pltpu.VMEM((4 * WIDTH, WIDTH), bf16), sem], 12, 10**8, 8 * 10**6,
    )
    (grad_act,) = call(
        kernel_ga, [], [grad_ffn, w_down], [], [vmem(full, f32)], [], 6, 12 * 10**8, 6 * 10**6
    )
    ids = gather_xor(class_id)
    far, mods_p, ids, _ = together(far, mods_p, ids, grad_act)
    branch, middle, shaped_own = call(
        kernel_b, [], [chip, far, source, mods_p, b_out], [],
        [vmem(half, f32), vmem(half, f32), vmem(half, bf16)], [], 6, 10**7, 7 * 10**6,
    )
    shaped_other = swap(shaped_own, "tensor", 1)

    shaped, activated, grad_hidden, sums_c, b_keep, b_send, g_keep, g_send = call(
        kernel_c, [], [shaped_own, shaped_other, grad_ffn, grad_act, w_up, w_down, b_up, k_ffn], [],
        [vmem(full, bf16)] * 3 + [vmem((16, WIDTH), f32)] + [vmem(half, bf16)] * 4,
        [grid, grid, temp, taps], 13, 5 * 10**9, 12 * 10**6,
    )
    g_came = swap(g_send, "tensor", 1)
    total_scratch = [pltpu.VMEM((WIDTH, WIDTH), f32)]
    if eight:
        d_keep, d_send = call(
            kernel_w_down, [], [grad_ffn, activated, sums_c], [],
            [vmem((4 * BLOCK + TAIL, WIDTH), f32), vmem((4 * BLOCK + TAIL, WIDTH), bf16)],
            total_scratch, 6, 12 * 10**8, 5 * 10**6,
        )
        g_came, _ = together(g_came, d_send)
    chip = join(g_keep, g_came)
    far = swap(chip, "tensor", 2)
    _, shaped, b_send = together(chip, shaped, b_send)
    b_came = swap(b_send, "tensor", 1)
    if eight:
        u_keep, u_send = call(
            kernel_w_up, [], [shaped, grad_hidden], [],
            [vmem((4 * BLOCK, WIDTH), f32), vmem((4 * BLOCK, WIDTH), bf16)],
            total_scratch, 6, 12 * 10**8, 5 * 10**6,
        )
        d_came = swap(d_send, "dp", 1)
        u_came = swap(u_send, "dp", 2)
        tokens_n, b_keep, _, _ = together(tokens, b_keep, d_send, u_send)
    else:
        ffn_grads = scatter_plain(
            jnp.stack([dot_tn(grad_ffn, activated), dot_tn(shaped, grad_hidden)])
        )
        early = butterfly(sums_c, "dp")
        tokens_n = tokens
    (normed,) = call(
        kernel_n, [], [tokens_n], [], [vmem((TILES, ITEM, 128), f32)], [], 4, 10**7, 5 * 10**6
    )
    (sums_q,) = call(
        kernel_q, [], [b_keep, b_send, cot_half, cot_other, b_down], [], [vmem((8, WIDTH), f32)], [],
        4, 10**7, 4 * 10**6,
    )
    query, _ = together(query, sums_q)
    (probs,) = call(
        kernel_p_again, [], [query, keys, lse], [], [vmem((12, SHARE, SHARE), f32)], [],
        6, 10**8, 4 * 10**6,
    )
    b_own, b_part = join_split(b_keep, b_came)
    far, b_part, _, _ = together(far, b_part, normed, probs)
    b_far = swap(b_part, "tensor", 2)
    if eight:
        far, d_came, u_came = together(far, d_came, u_came)
    grad_middle, attn_own, sums_d = call(
        kernel_d, [], [chip, far, branch, middle, cot_half, mods_p], [],
        [vmem(half, f32), vmem(half, bf16), vmem((8, WIDTH), f32)], [], 6, 10**7, 8 * 10**6,
    )
    attn_other = swap(attn_own, "tensor", 1)
    if eight:
        d_came, u_came, _ = together(d_came, u_came, attn_own)
        d_keep, d_send, u_keep, u_send = weight_step(
            kernel_w_one, [(2 * BLOCK + TAIL, WIDTH), (2 * BLOCK, WIDTH)], d_keep, d_came, u_keep, u_came
        )
        attn_other, _, _ = together(attn_other, d_send, u_send)
        d_came = swap(d_send, "dp", 2)
        u_came = swap(u_send, "dp", 1)

    grad_attn, right, mixed_grad, mixed, h_keep, h_send = call(
        kernel_e, [],
        [attn_own, attn_other, query, keys, vals, attended, probs, w_three, w_back], [mixed],
        [vmem(full, bf16)] * 4 + [vmem((2 * HALO, WIDTH), bf16)] * 2,
        [pltpu.VMEM((4, 288, WIDTH), bf16), sem], 8, 3 * 10**9, 10**7,
    )
    if eight:
        d_came, u_came, b_far, right, h_send = together(d_came, u_came, b_far, right, h_send)
    h_came = swap(h_send, "tensor", 1)
    w_mod_late, _ = together(w_mod, mixed_grad)
    if eight:
        ffn_keep, ffn_send = weight_step(
            kernel_w_two, [(2 * BLOCK + TAIL, WIDTH)], d_keep, d_came, u_keep, u_came
        )
        a_keep, a_send = call(
            kernel_v, [], [mixed, grad_attn, right], [],
            [vmem((4 * BLOCK, WIDTH), f32), vmem((4 * BLOCK, WIDTH), bf16)],
            [pltpu.VMEM((WIDTH, WIDTH), f32)], 6, 16 * 10**8, 7 * 10**6,
        )
        h_came, _, _ = together(h_came, a_send, ffn_send)
        a_came = swap(a_send, "dp", 1)
        ffn_came = swap(ffn_send, "dp", 4)
    else:
        last = dot_tn(grad_attn, right[:, 3 * HEAD_WIDTH :])
        total = jnp.concatenate([dot_tn(mixed, right[:, : 3 * HEAD_WIDTH]), last], axis=1)
        att_grads = scatter_plain(total[None])[0]
    h_own, part = join_split(h_keep, h_came)
    mixed_grad, _ = together(mixed_grad, part)
    (late,) = call(
        kernel_s, [], [normed, mixed_grad, mods_a, k_att, sums_d, sums_q], [],
        [vmem((16, WIDTH), bf16)], [taps, grid, taps], 8, 10**8, 4 * 10**6,
    )
    late = lax.all_gather(late, "tensor")
    (held,) = call(
        kernel_slot, [], [late, cond], [], [vmem((3, 8, WIDTH), bf16)], [], 2, 10**5, 10**5
    )
    part, _ = together(part, held)
    part_far = swap(part, "tensor", 2)
    for step, bit in enumerate(bits):
        came = swap(held, "dp", bit)
        if step == len(bits) - 1:
            part_far, _ = together(part_far, held)
            (grad_tokens,) = call(
                kernel_f, [], [tokens, h_own, part_far, grad_middle, mods_a, k_att], [],
                [plain((SHARE, WIDTH), f32)],
                [pltpu.VMEM((TILES, SHARE_GRID_ROWS, 128), f32), share_tiles, share_tiles, taps],
                6, 10**7, 6 * 10**6, 0,
            )
            (block_out,) = call(
                kernel_o, [item_count], [b_own, b_far, middle, mods_p, b_down], [],
                [plain((SHARE, WIDTH), bf16)], [share_tiles], 4, 10**7, 4 * 10**6,
            )
            came, _, _ = together(came, grad_tokens, block_out)
            break
        slots = 1 << step

        def kernel(*refs, slots=slots):
            kernel_gather(slots, *refs)

        (held,) = call(
            kernel, [], [held, came], [], [vmem((2 * slots + 2, 8, WIDTH), bf16)], [], 4, 10**5, 10**5
        )
        if eight and step == 0:
            a_came, ffn_came, _ = together(a_came, ffn_came, held)
            a_keep, a_send = weight_step(kernel_v_one, [(2 * BLOCK, WIDTH)], a_keep, a_came)
            a_came = swap(a_send, "dp", 2)
    if eight:
        a_came, _ = together(a_came, held)
        a_keep, a_send = weight_step(kernel_v_two, [(BLOCK, WIDTH)], a_keep, a_came)
        a_came = swap(a_send, "dp", 4)
        came, _ = together(came, a_send)

    share = w_mod.shape[0] // items

    def kernel(*refs):
        kernel_g(items, share, *refs)

    grad_w_mod, grad_b_mod, grad_class, grad_k_att, grad_b_out = call(
        kernel, [ids], [held, came, w_mod_late], [],
        [
            plain((share, WIDTH), f32), plain(w_mod.shape[:1], f32), plain(class_table.shape, f32),
            plain((9, WIDTH), f32), plain((WIDTH,), f32),
        ],
        [
            pltpu.VMEM((items + 2, 8, WIDTH), f32), pltpu.VMEM((items, 6 * WIDTH), bf16),
            pltpu.VMEM((items, WIDTH), f32), pltpu.VMEM(((share + 254) // 128 * 128, WIDTH), f32),
        ],
        12, 10**8, 14 * 10**6,
    )

    if eight:
        rows = plain((BLOCK, WIDTH), f32)
        flat = plain((WIDTH,), f32)
        grad_down, grad_up, grad_k_ffn, grad_b_up, grad_b_down = call(
            kernel_w_end, [], [ffn_keep, ffn_came], [],
            [rows, rows, plain((9, WIDTH), f32), flat, flat], [], 4, 10**6, 2 * 10**6,
        )
        a_came, _, _ = together(a_came, grad_b_mod, grad_b_up)
        grad_qkv, grad_out = call(
            kernel_v_end, [], [a_keep, a_came], [],
            [plain((3, BLOCK, HEAD_WIDTH), f32), plain((BLOCK, HEAD_WIDTH), f32)], [], 4, 10**6, 10**6,
        )
        grad_qkv = jnp.transpose(grad_qkv, (1, 0, 2))
    else:
        grad_down, grad_up = ffn_grads[0], ffn_grads[1]
        grad_k_ffn, grad_b_up, grad_b_down = early[:9], early[9], early[10]
        grad_qkv = att_grads[:, : 3 * HEAD_WIDTH].reshape(-1, 3, HEAD_WIDTH)
        grad_out = att_grads[:, 3 * HEAD_WIDTH :]
    return (
        block_out,
        grad_tokens,
        grad_class,
        grad_w_mod,
        grad_b_mod,
        grad_k_att,
        grad_qkv,
        grad_out,
        grad_b_out,
        grad_up,
        grad_b_up,
        grad_k_ffn,
        grad_down,
        grad_b_down,
    )


def solution(mesh):
    placed = (
        P("dp", None),
        P("dp", None),
        P("dp"),
        P("dp"),
        P("dp"),
        P(),
        P(),
        P(),
        P(),
        P(None, None, "tensor"),
        P(None, "tensor"),
        P(),
        P(None, "tensor"),
        P("tensor"),
        P(None, "tensor"),
        P(None, "tensor"),
        P(),
    )
    return jax.shard_map(
        shards,
        mesh=mesh,
        in_specs=placed,
        out_specs=(
            P(("dp", "tensor"), None),
            P(("dp", "tensor"), None),
            P(),
            P("dp", None),
            P(),
            P(),
            P("dp", None, "tensor"),
            P("dp", "tensor"),
            P(),
            P("dp", "tensor"),
            P("tensor"),
            P(None, "tensor"),
            P("dp", "tensor"),
            P(),
        ),
        check_vma=False,
    )
```

```python
import math

import jax
import jax.numpy as jnp
from jax import lax
from jax.experimental import pallas as pl
from jax.experimental.pallas import tpu as pltpu
from jax.sharding import PartitionSpec as P

f32 = jnp.float32
bf16 = jnp.bfloat16

WIDTH = 768
TILES = WIDTH // 128
SIDE = 32
ITEM = SIDE * SIDE
HALF = ITEM // 2
SHARE = ITEM // 4
HALO = SHARE + 2 * SIDE
HEADS_HERE = 3
HEAD_WIDTH = 192
PITCH = 40
GRID_ROWS = 34 * PITCH + 8
SHARE_GRID_ROWS = 10 * PITCH + 16

norm_eps = 1e-06
score_scale = 0.125
gelu_slope = math.sqrt(2.0 / math.pi)
gelu_cubic = 0.044715
BLOCK = 96
TAIL = 16


def dot_nn(left, right):
    return lax.dot_general(left, right, (((1,), (0,)), ((), ())), preferred_element_type=f32)


def dot_nt(left, right):
    return lax.dot_general(left, right, (((1,), (1,)), ((), ())), preferred_element_type=f32)


def dot_tn(left, right):
    return lax.dot_general(left, right, (((0,), (0,)), ((), ())), preferred_element_type=f32)


def at(start, size):
    return pl.ds(start if isinstance(start, int) else pl.multiple_of(start, size), size)


def at16(start, size):
    return pl.ds(pl.multiple_of(start, 16), size)


def tile_cols(tile):
    return pl.ds(pl.multiple_of(tile * 128, 128), 128)


def spot(row, col):
    return (row + 1) * PITCH + 8 + col


def every_other(start):
    return pl.ds(start, 16, stride=2)


def window(grid, tile, i):
    return [
        [grid[tile, every_other(spot(2 * i + row, col)), :] for col in range(-1, 3)]
        for row in range(-1, 3)
    ]


def here_core():
    place = lax.axis_index("tensor")
    return lax.rem(place, 2), lax.div(place, 2), place


def normed_of(values):
    center = values - jnp.mean(values, axis=-1, keepdims=True)
    scale = lax.rsqrt(jnp.mean(center * center, axis=-1, keepdims=True) + norm_eps)
    return center * scale, scale


def norm_back(normed, scale, grad):
    spread = jnp.mean(grad * normed, axis=-1, keepdims=True)
    return scale * (grad - jnp.mean(grad, axis=-1, keepdims=True) - normed * spread)


def row_of(flat, start=0):
    return flat[pl.ds(start, WIDTH)].astype(f32).reshape(1, WIDTH)


def column_sum(values):
    return jnp.sum(values, axis=0, keepdims=True)


def head_masks():
    lane = lax.broadcasted_iota(jnp.int32, (SHARE, HEAD_WIDTH), 1)
    return [(lane >= 64 * h) & (lane < 64 * h + 64) for h in range(HEADS_HERE)]


def split_halves(values, core, group, keep, send):
    for x in range(2):
        rows = at(x * SHARE + group * 64, 64)
        keep[rows, :] = values[at((2 * x + core) * 64, 64), :].astype(bf16)
        send[rows, :] = values[at((2 * x + 1 - core) * 64, 64), :].astype(bf16)


def join_halves(own, other, core, full):
    for half, h in ((own, core), (other, 1 - core)):
        for x in range(2):
            for g in range(4):
                rows = at(g * SHARE + (8 * x + 4 * h) * 16, 64)
                full[rows, :] = half[x * SHARE + g * 64 : x * SHARE + g * 64 + 64, :]


def take_half(natural, core, tile, half, cols):
    for x in range(2):
        for g in range(4):
            for ii in range(4):
                i = 8 * x + 4 * core + ii
                row = x * SHARE + g * 64 + ii * 16
                seen = natural[tile, every_other((2 * i + g // 2) * SIDE + g % 2), :]
                half[row : row + 16, cols] = seen.astype(half.dtype)


def modulation(act, weights, bias, pieces, first):
    return [
        dot_nt(act, weights[(p - first) * WIDTH : (p - first + 1) * WIDTH, :])[:1]
        + row_of(bias, p * WIDTH)
        for p in pieces
    ]


def kernel_a(
    act, tokens_far, b_mod_far, k_att_far, w_qkv_far, w_out_far, w_mod,
    mods_out, keep, send, lse_all, mixed_out, q_out, k_out, v_out, att_out,
    grid, temp, kernel, tokens, b_mod, k_att, w_qkv, w_out, weights,
    mixed, q_all, k_all, v_all, att_all, sems, in_sems,
):
    core, _, _ = here_core()
    fetches = [
        pltpu.make_async_copy(far, near, in_sems.at[n])
        for n, (far, near) in enumerate(
            (
                (w_mod.at[pl.ds(0, 2 * WIDTH), :], weights),
                (b_mod_far, b_mod),
                (k_att_far, k_att),
                (tokens_far, tokens),
                (w_qkv_far, w_qkv),
                (w_out_far, w_out),
            )
        )
    ]
    for fetch in fetches:
        fetch.start()
    grid[...] = jnp.zeros_like(grid)
    for fetch in fetches[:4]:
        fetch.wait()
    kernel[0:9, :] = k_att[...].astype(f32)
    shift, scale = modulation(act[...], weights, b_mod, (0, 1), 0)
    mods_out[0:1, :] = shift
    mods_out[1:2, :] = scale
    scale = 1.0 + scale

    def norm(i, carry):
        values = tokens[at(i * 64, 64), :].astype(f32)
        shaped = normed_of(values)[0] * scale + shift
        for tile in range(TILES):
            cols = slice(tile * 128, tile * 128 + 128)
            for r in range(2):
                rows = pl.ds(pl.multiple_of((2 * i + r + 1) * PITCH + 8, 8), SIDE)
                grid[tile, rows, :] = shaped[SIDE * r : SIDE * r + SIDE, cols]
        return carry

    lax.fori_loop(0, 16, norm, 0, unroll=4)

    def conv(tile, carry):
        cols = tile_cols(tile)
        taps = [kernel[t : t + 1, cols] for t in range(9)]

        def row(i, inner):
            seen = window(grid, tile, i)
            for a in range(2):
                for b in range(2):
                    total = taps[0] * seen[a][b]
                    for t in range(1, 9):
                        total = total + taps[t] * seen[a + t // 3][b + t % 3]
                    mixed[at16((2 * a + b) * SHARE + i * 16, 16), cols] = total.astype(bf16)
            return inner

        lax.fori_loop(0, 16, row, 0, unroll=2)
        return carry

    lax.fori_loop(0, TILES, conv, 0)
    for fetch in fetches[4:]:
        fetch.wait()
    masks = head_masks()
    pairs = (
        (mixed, mixed_out), (q_all, q_out), (k_all, k_out), (v_all, v_out), (att_all, att_out),
    )

    def copies(g):
        rows = at(g * SHARE, SHARE)
        return [
            pltpu.make_async_copy(left.at[rows, :], right.at[rows, :], sems.at[n, g])
            for n, (left, right) in enumerate(pairs)
        ]

    def attend(g, carry):
        rows = at(g * SHARE, SHARE)
        values = mixed[rows, :]
        query, keys, vals = (dot_nt(values, w_qkv[kind]).astype(bf16) for kind in range(3))
        q_all[rows, :] = query
        k_all[rows, :] = keys
        v_all[rows, :] = vals
        attended = jnp.zeros((SHARE, HEAD_WIDTH), f32)
        for h in range(HEADS_HERE):
            scores = dot_nt(jnp.where(masks[h], keys, jnp.zeros_like(keys)), query) * score_scale
            top = jnp.max(scores, axis=0, keepdims=True)
            grown = jnp.exp(scores - top)
            total = jnp.sum(grown, axis=0, keepdims=True)
            probs = (grown * (1.0 / total)).astype(bf16)
            attended = jnp.where(masks[h], dot_tn(probs, vals), attended)
            lse_all[pl.ds(g, 1), h * SHARE : (h + 1) * SHARE] = top + jnp.log(total)
        attended = attended.astype(bf16)
        att_all[rows, :] = attended
        for copy in copies(g):
            copy.start()
        temp[g % 2] = dot_nn(attended, w_out[...])
        split_halves(temp.at[g % 2], core, g, keep, send)
        return carry

    for g in range(4):
        attend(g, 0)

    def finish(g, carry):
        for copy in copies(g):
            copy.wait()
        return carry

    lax.fori_loop(0, 4, finish, 0)


def kernel_p(
    count, cotangent, act, b_mod, w_mod,
    mods_out, grad_branch, half, other,
    natural, weights, sem,
):
    core, _, _ = here_core()
    fetch = pltpu.make_async_copy(w_mod.at[pl.ds(2 * WIDTH, 4 * WIDTH), :], weights, sem)
    fetch.start()
    live = jnp.where(count[0] > 0, 1.0, 0.0)

    def spread(i, carry):
        values = cotangent[at(i * 64, 64), :].astype(f32) * live
        for tile in range(TILES):
            natural[tile, at(i * 64, 64), :] = values[:, tile * 128 : tile * 128 + 128]
        return carry

    lax.fori_loop(0, 16, spread, 0, unroll=2)
    fetch.wait()
    for p, row in zip(range(2, 6), modulation(act[...], weights, b_mod, range(2, 6), 2)):
        mods_out[p : p + 1, :] = row

    def group(tile, carry):
        cols = tile_cols(tile)
        gate = mods_out[5:6, cols]

        def row(i, inner):
            for g in range(4):
                seen = natural[tile, every_other((2 * i + g // 2) * SIDE + g % 2), :]
                grad_branch[at16(g * SHARE + i * 16, 16), cols] = (seen * gate).astype(bf16)
            return inner

        lax.fori_loop(0, 16, row, 0, unroll=2)
        take_half(natural, core, tile, half, cols)
        take_half(natural, 1 - core, tile, other, cols)
        return carry

    lax.fori_loop(0, TILES, group, 0)


def kernel_source(tokens, source, natural):
    core, _, _ = here_core()

    def spread(i, carry):
        values = tokens[at(i * 64, 64), :].astype(f32)
        for tile in range(TILES):
            natural[tile, at(i * 64, 64), :] = values[:, tile * 128 : tile * 128 + 128]
        return carry

    lax.fori_loop(0, 16, spread, 0, unroll=2)

    def group(tile, carry):
        take_half(natural, core, tile, source, tile_cols(tile))
        return carry

    lax.fori_loop(0, TILES, group, 0)


def kernel_ga(grad_branch, w_down, grad_act):
    def step(g, carry):
        rows = at(g * SHARE, SHARE)
        grad_act[rows, :] = dot_nn(grad_branch[rows, :], w_down[...])
        return carry

    lax.fori_loop(0, 4, step, 0)


def kernel_b(chip, far, source, mods, b_out, branch_out, middle_out, shaped_out):
    gate = mods[2:3, :]
    shift = mods[3:4, :]
    scale = 1.0 + mods[4:5, :]
    bias = row_of(b_out)

    def step(r, carry):
        rows = at(r * 64, 64)
        branch = chip[rows, :].astype(f32) + far[rows, :].astype(f32) + bias
        middle = source[rows, :] + gate * branch
        branch_out[rows, :] = branch
        middle_out[rows, :] = middle
        shaped_out[rows, :] = (normed_of(middle)[0] * scale + shift).astype(bf16)
        return carry

    lax.fori_loop(0, HALF // 64, step, 0, unroll=2)


def kernel_c(
    class_id, own, other, grad_branch, grad_act, w_up, b_up, k_ffn,
    shaped, activated, grad_hidden, sums, g_keep, g_send,
    hidden, grad_conv, temp, kernel,
):
    core, _, _ = here_core()
    hidden[...] = jnp.zeros_like(hidden)
    grad_conv[...] = jnp.zeros_like(grad_conv)
    kernel[0:9, :] = k_ffn[...].astype(f32)
    bias = row_of(b_up)
    join_halves(own, other, core, shaped)

    def up(g, carry):
        rows = at(g * SHARE, SHARE)
        a = lax.div(g, 2)
        b = lax.rem(g, 2)
        temp[...] = dot_nn(shaped[rows, :], w_up[...]) + bias

        def place(i, inner):
            for tile in range(TILES):
                values = temp[at(i * 16, 16), tile * 128 : tile * 128 + 128]
                hidden[tile, every_other(spot(2 * i + a, b)), :] = values
            return inner

        lax.fori_loop(0, 16, place, 0, unroll=4)
        return carry

    lax.fori_loop(0, 4, up, 0)

    def conv(tile, carry):
        cols = tile_cols(tile)
        taps = [kernel[t : t + 1, cols] for t in range(9)]

        def row(i, inner):
            seen = window(hidden, tile, i)
            for a in range(2):
                for b in range(2):
                    rows = at16((2 * a + b) * SHARE + i * 16, 16)
                    u = taps[0] * seen[a][b]
                    for t in range(1, 9):
                        u = u + taps[t] * seen[a + t // 3][b + t % 3]
                    square = u * u
                    bent = jnp.tanh(u * (gelu_slope + (gelu_slope * gelu_cubic) * square))
                    part = 0.5 + 0.5 * bent
                    value = u * part
                    activated[rows, cols] = value.astype(bf16)
                    bend = 2.0 * gelu_slope + (6.0 * gelu_slope * gelu_cubic) * square
                    slope = part + value * ((1.0 - part) * bend)
                    back = grad_act[rows, cols] * slope
                    grad_conv[tile, every_other(spot(2 * i + a, b)), :] = back
            return inner

        lax.fori_loop(0, 16, row, 0, unroll=2)
        return carry

    lax.fori_loop(0, TILES, conv, 0)

    def back(tile, carry):
        cols = tile_cols(tile)
        taps = [kernel[t : t + 1, cols] for t in range(9)]

        def row(i, held):
            held = list(held)
            seen = window(grad_conv, tile, i)
            for a in range(2):
                for b in range(2):
                    here = hidden[tile, every_other(spot(2 * i + a, b)), :]
                    total = None
                    for t in range(9):
                        view = seen[a + 2 - t // 3][b + 2 - t % 3]
                        term = taps[t] * view
                        total = term if total is None else total + term
                        product = here * view
                        held[t] = held[t] + (product[:8] + product[8:])
                    low = total.astype(bf16)
                    grad_hidden[at16((2 * a + b) * SHARE + i * 16, 16), cols] = low
                    low = low.astype(f32)
                    held[9] = held[9] + (low[:8] + low[8:])
            return tuple(held)

        zeros = tuple(jnp.zeros((8, 128), f32) for _ in range(10))
        held = lax.fori_loop(0, 16, row, zeros, unroll=2)
        for t in range(10):
            sums[t : t + 1, cols] = column_sum(held[t])
        return carry

    lax.fori_loop(0, TILES, back, 0)

    def out(g, total):
        rows = at(g * SHARE, SHARE)
        temp[...] = dot_nt(grad_hidden[rows, :], w_up[...])
        split_halves(temp, core, g, g_keep, g_send)
        return total + column_sum(grad_branch[rows, :].astype(f32))

    sums[10:11, :] = lax.fori_loop(0, 4, out, jnp.zeros((1, WIDTH), f32), unroll=True)
    lane = lax.broadcasted_iota(jnp.int32, (1, WIDTH), 1)
    mine = lane == lax.axis_index("dp")
    high = lax.div(class_id[0], 32)
    for row, digit in ((11, high), (12, class_id[0] - 32 * high)):
        sums[row : row + 1, :] = jnp.where(mine, digit.astype(f32), 0.0)
    sums[13:16, :] = jnp.zeros((3, WIDTH), f32)


def kernel_branch(activated, w_down, b_keep, b_send, temp):
    core, _, _ = here_core()

    def out(g, carry):
        temp[...] = dot_nt(activated[at(g * SHARE, SHARE), :], w_down[...])
        split_halves(temp, core, g, b_keep, b_send)
        return carry

    lax.fori_loop(0, 4, out, 0, unroll=True)


def kernel_d(chip, far, branch, middle, half, mods, grad_middle, grad_attn, sums):
    gate = mods[2:3, :]
    scale = 1.0 + mods[4:5, :]

    def step(r, held):
        rows = at(r * 64, 64)
        grad = chip[rows, :].astype(f32) + far[rows, :].astype(f32)
        normed, size = normed_of(middle[rows, :])
        total = half[rows, :].astype(f32) + norm_back(normed, size, grad * scale)
        low = (total * gate).astype(bf16)
        grad_middle[rows, :] = total
        grad_attn[rows, :] = low
        terms = (total * branch[rows, :], grad, grad * normed, low.astype(f32))
        return tuple(h + column_sum(t) for h, t in zip(held, terms))

    zeros = tuple(jnp.zeros((1, WIDTH), f32) for _ in range(4))
    held = lax.fori_loop(0, HALF // 64, step, zeros, unroll=2)
    for t in range(4):
        sums[t : t + 1, :] = held[t]


def kernel_o(count, near, far, middle, mods, b_down, out, natural):
    _, side, _ = here_core()
    live = jnp.where(count[0] > 0, 1.0, 0.0)
    gate = mods[5:6, :]
    bias = row_of(b_down)
    for g in range(4):
        part = slice(g * 64, g * 64 + 64)
        rows = at(side * SHARE + g * 64, 64)
        branch = near[part, :].astype(f32) + far[part, :].astype(f32) + bias
        result = (middle[rows, :] + gate * branch) * live
        for ii in range(4):
            place = every_other((2 * ii + g // 2) * SIDE + g % 2)
            for tile in range(TILES):
                cols = slice(tile * 128, tile * 128 + 128)
                natural[tile, place, :] = result[ii * 16 : ii * 16 + 16, cols]
    for tile in range(TILES):
        out[:, tile * 128 : tile * 128 + 128] = natural[tile, :, :].astype(bf16)


def kernel_p_again(q_all, k_all, lse_all, probs_all):
    masks = head_masks()

    def step(g, carry):
        rows = at(g * SHARE, SHARE)
        query = q_all[rows, :]
        keys = k_all[rows, :]
        for h in range(HEADS_HERE):
            scores = dot_nt(jnp.where(masks[h], keys, jnp.zeros_like(keys)), query) * score_scale
            lse = lse_all[pl.ds(g, 1), h * SHARE : (h + 1) * SHARE]
            probs_all[HEADS_HERE * g + h] = jnp.exp(scores - lse)
        return carry

    lax.fori_loop(0, 4, step, 0)


def kernel_e(
    own, other, q_all, k_all, v_all, att_all, probs_all, w_qkv, w_out, mixed_far,
    grad_branch, right, mixed, mixed_near, keep, send,
    padded, sem,
):
    core, _, _ = here_core()
    fetch = pltpu.make_async_copy(mixed_far, mixed_near, sem)
    fetch.start()
    join_halves(own, other, core, grad_branch)
    masks = head_masks()
    for g in range(4):
        padded[g, 0:16, :] = jnp.zeros((16, WIDTH), bf16)
        padded[g, 272:288, :] = jnp.zeros((16, WIDTH), bf16)

    def attend(g, carry):
        rows = at(g * SHARE, SHARE)
        grad = dot_nt(grad_branch[rows, :], w_out[...]).astype(bf16)
        query = q_all[rows, :]
        keys = k_all[rows, :]
        vals = v_all[rows, :]
        zero = jnp.zeros_like(query)
        g_query = jnp.zeros((SHARE, HEAD_WIDTH), f32)
        g_keys = g_query
        g_vals = g_query
        for h in range(HEADS_HERE):
            probs = probs_all[HEADS_HERE * g + h]
            g_probs = dot_nt(jnp.where(masks[h], vals, zero), grad)
            spread = jnp.sum(probs * g_probs, axis=0, keepdims=True)
            g_scores = (probs * (g_probs - spread)).astype(bf16)
            g_query = jnp.where(masks[h], dot_tn(g_scores, keys), g_query)
            g_keys = jnp.where(masks[h], dot_nn(g_scores, query), g_keys)
            g_vals = jnp.where(masks[h], dot_nn(probs.astype(bf16), grad), g_vals)
        g_query = (g_query * score_scale).astype(bf16)
        g_keys = (g_keys * score_scale).astype(bf16)
        g_vals = g_vals.astype(bf16)
        right[rows, :] = jnp.concatenate([g_query, g_keys, g_vals, att_all[rows, :]], axis=1)
        total = dot_nn(g_query, w_qkv[0]) + dot_nn(g_keys, w_qkv[1]) + dot_nn(g_vals, w_qkv[2])
        low = total.astype(bf16)
        padded[g, 16:272, :] = low
        mixed[rows, :] = low
        return carry

    for g in range(4):
        attend(g, 0)
    for out, h in ((keep, core), (send, 1 - core)):
        for x in range(2):
            share = 2 * x + h
            first = x * HALO
            for g in range(4):
                rows = at16((1 + 4 * share) * 16, 64)
                out[first + g * 64 : first + g * 64 + 64, :] = padded[g, rows, :]
            for b in range(2):
                row = first + SHARE + b * 16
                out[row : row + 16, :] = padded[2 + b, at16(4 * share * 16, 16), :]
                row = row + SIDE
                out[row : row + 16, :] = padded[b, at16((4 * share + 5) * 16, 16), :]
    fetch.wait()


def kernel_n(tokens, natural):
    def step(i, carry):
        normed = normed_of(tokens[at(i * 64, 64), :].astype(f32))[0]
        for tile in range(TILES):
            natural[tile, at(i * 64, 64), :] = normed[:, tile * 128 : tile * 128 + 128]
        return carry

    lax.fori_loop(0, 16, step, 0, unroll=2)


def kernel_q(keep, send, own, other, b_down, sums):
    _, _, place = here_core()
    once = jnp.where(place == 0, 1.0, 0.0)
    bias = row_of(b_down) * once

    def step(r, total):
        rows = at(r * 64, 64)
        near = own[rows, :].astype(f32) * (keep[rows, :].astype(f32) + bias)
        away = other[rows, :].astype(f32) * (send[rows, :].astype(f32) + bias)
        return total + column_sum(near + away)

    sums[0:1, :] = lax.fori_loop(0, HALF // 64, step, jnp.zeros((1, WIDTH), f32))


def kernel_s(natural, mixed, mods, k_att, sums_d, sums_q, low, out, grid, kernel):
    _, side, _ = here_core()
    grid[...] = jnp.zeros_like(grid)
    kernel[0:9, :] = k_att[...].astype(f32)

    def norm(i, carry):
        for g in range(4):
            values = mixed[at16(g * SHARE + i * 16, 16), :].astype(f32)
            place = every_other(spot(2 * i + g // 2, g % 2))
            for tile in range(TILES):
                grid[tile, place, :] = values[:, tile * 128 : tile * 128 + 128]
        return carry

    lax.fori_loop(0, 16, norm, 0, unroll=4)

    def gather(tile, carry):
        cols = tile_cols(tile)
        taps = [kernel[t : t + 1, cols] for t in range(9)]

        def row(i, held):
            held = list(held)
            seen = window(grid, tile, i)
            for a in range(2):
                for b in range(2):
                    here = natural[tile, every_other((2 * i + a) * SIDE + b), :]
                    for t in range(9):
                        product = here * seen[a + 2 - t // 3][b + 2 - t % 3]
                        held[t] = held[t] + (product[:8] + product[8:])
                    center = seen[a + 1][b + 1]
                    held[9] = held[9] + (center[:8] + center[8:])
            return tuple(held)

        zeros = tuple(jnp.zeros((8, 128), f32) for _ in range(10))
        held = [column_sum(h) for h in lax.fori_loop(0, 16, row, zeros, unroll=2)]
        edge_row = [
            column_sum(grid[tile, pl.ds(spot(r, 0), SIDE), :]) if r is not None else 0.0
            for r in (0, None, SIDE - 1)
        ]
        edge_col = [
            column_sum(grid[tile, pl.ds(spot(0, c), SIDE, stride=PITCH), :])
            if c is not None
            else 0.0
            for c in (0, None, SIDE - 1)
        ]
        shift = mods[0:1, cols]
        scale = 1.0 + mods[1:2, cols]
        shift_sum = jnp.zeros((1, 128), f32)
        scale_sum = jnp.zeros((1, 128), f32)
        for t in range(9):
            a, b = t // 3, t % 3
            plain = held[9] - edge_row[a] - edge_col[b]
            if a != 1 and b != 1:
                corner = spot((SIDE - 1) * (a // 2), (SIDE - 1) * (b // 2))
                plain = plain + grid[tile, pl.ds(corner, 1), :]
            out[6 + t : 7 + t, cols] = scale * held[t] + shift * plain
            shift_sum = shift_sum + taps[t] * plain
            scale_sum = scale_sum + taps[t] * held[t]
        out[0:1, cols] = shift_sum
        out[1:2, cols] = scale_sum
        return carry

    lax.fori_loop(0, TILES, gather, 0)
    once = jnp.where(side == 0, 1.0, 0.0)
    out[2:5, :] = sums_d[0:3, :] * once
    out[5:6, :] = sums_q[0:1, :]
    out[15:16, :] = sums_d[3:4, :] * once
    low[...] = out[...].astype(bf16)


def kernel_f(tokens, near, far, grad_middle, mods, k_att, out, grid, grad_shaped, middle, kernel):
    _, side, place = here_core()
    grid[...] = jnp.zeros_like(grid)
    kernel[0:9, :] = k_att[...].astype(f32)
    scale = 1.0 + mods[1:2, :]

    def fetch(start, rows):
        part = slice(start, start + rows)
        total = near[part, :].astype(f32) + far[part, :].astype(f32)
        return total.astype(bf16).astype(f32)

    for g in range(4):
        a, b = g // 2, g % 2
        values = fetch(g * 64, 64)
        grads = grad_middle[at(side * SHARE + g * 64, 64), :]
        for ii in range(4):
            rows = slice(ii * 16, ii * 16 + 16)
            for tile in range(TILES):
                cols = slice(tile * 128, tile * 128 + 128)
                grid[tile, every_other(spot(2 * ii + a, b)), :] = values[rows, cols]
                middle[tile, every_other((2 * ii + a) * SIDE + b), :] = grads[rows, cols]
    for b in range(2):
        above = fetch(SHARE + b * 16, 16)
        below = fetch(SHARE + SIDE + b * 16, 16)
        for tile in range(TILES):
            cols = slice(tile * 128, tile * 128 + 128)
            grid[tile, every_other(spot(-1, b)), :] = above[:, cols]
            grid[tile, every_other(spot(8, b)), :] = below[:, cols]

    def conv(tile, carry):
        cols = tile_cols(tile)
        taps = [kernel[t : t + 1, cols] for t in range(9)]

        def row(i, inner):
            seen = window(grid, tile, i)
            for a in range(2):
                for b in range(2):
                    total = taps[0] * seen[a + 2][b + 2]
                    for t in range(1, 9):
                        total = total + taps[t] * seen[a + 2 - t // 3][b + 2 - t % 3]
                    grad_shaped[tile, every_other((2 * i + a) * SIDE + b), :] = total
            return inner

        lax.fori_loop(0, 4, row, 0, unroll=2)
        return carry

    lax.fori_loop(0, TILES, conv, 0)

    def finish(r, carry):
        rows = at(r * SIDE, SIDE)
        values = tokens[at(place * SHARE + r * SIDE, SIDE), :].astype(f32)
        normed, size = normed_of(values)
        grad = jnp.concatenate([grad_shaped[tile, rows, :] for tile in range(TILES)], axis=1)
        base = jnp.concatenate([middle[tile, rows, :] for tile in range(TILES)], axis=1)
        out[rows, :] = base + norm_back(normed, size, grad * scale)
        return carry

    lax.fori_loop(0, SHARE // SIDE, finish, 0, unroll=2)


def bit_here(bit):
    return lax.rem(lax.div(lax.axis_index("dp"), bit), 2)


def split_blocks(blocks, stride, bit, values, keep, send):
    mine = bit_here(bit)
    for j in range(blocks // 2):
        base = (j // stride) * 2 * stride + j % stride
        rows = slice(j * BLOCK, (j + 1) * BLOCK)
        keep[rows, :] = values(at16((base + mine * stride) * BLOCK, BLOCK))
        send[rows, :] = values(at16((base + (1 - mine) * stride) * BLOCK, BLOCK)).astype(bf16)


def summed(held, came):
    return lambda rows: held[rows, :] + came[rows, :].astype(f32)


def product_tn(left, right, total):
    def step(i, carry):
        total[at(i * 256, 256), :] = dot_tn(left[:, at(i * 256, 256)], right[...])
        return carry

    lax.fori_loop(0, 3, step, 0)


def kernel_w_down(grad, activated, sums, keep, send, total):
    product_tn(grad, activated, total)
    split_blocks(8, 1, 1, lambda rows: total[rows, :], keep, send)
    keep[4 * BLOCK :, :] = sums[...].astype(bf16).astype(f32)
    send[4 * BLOCK :, :] = sums[...].astype(bf16)


def kernel_w_up(shaped, hidden, keep, send, total):
    product_tn(shaped, hidden, total)
    split_blocks(8, 2, 2, lambda rows: total[rows, :], keep, send)


def kernel_w_one(d_held, d_came, u_held, u_came, d_keep, d_send, u_keep, u_send):
    split_blocks(4, 1, 2, summed(d_held, d_came), d_keep, d_send)
    tail = summed(d_held, d_came)(slice(4 * BLOCK, 4 * BLOCK + TAIL)).astype(bf16)
    d_keep[2 * BLOCK :, :] = tail.astype(f32)
    d_send[2 * BLOCK :, :] = tail
    split_blocks(4, 1, 1, summed(u_held, u_came), u_keep, u_send)


def kernel_w_two(d_held, d_came, u_held, u_came, keep, send):
    mine = bit_here(4)
    for n, (held, came) in enumerate(((d_held, d_came), (u_held, u_came))):
        total = summed(held, came)
        rows = slice(n * BLOCK, (n + 1) * BLOCK)
        keep[rows, :] = total(at16(mine * BLOCK, BLOCK))
        send[rows, :] = total(at16((1 - mine) * BLOCK, BLOCK)).astype(bf16)
    tail = summed(d_held, d_came)(slice(2 * BLOCK, 2 * BLOCK + TAIL)).astype(bf16)
    keep[2 * BLOCK :, :] = tail.astype(f32)
    send[2 * BLOCK :, :] = tail


def kernel_w_end(held, came, down, up, k_out, b_up, b_down, ids):
    total = summed(held, came)
    down[...] = total(slice(0, BLOCK))
    up[...] = total(slice(BLOCK, 2 * BLOCK))
    tail = total(slice(2 * BLOCK, 2 * BLOCK + TAIL))
    k_out[...] = tail[0:9, :]
    b_up[...] = tail[9:10, :].reshape(WIDTH)
    b_down[...] = tail[10:11, :].reshape(WIDTH)
    ids[...] = (32.0 * tail[11:12, 0:128] + tail[12:13, 0:128]).astype(jnp.int32)


def kernel_v(mixed, grad_branch, right, keep, send, total):
    lane = lax.broadcasted_iota(jnp.int32, (256, 256), 1)

    def step(i, carry):
        cols = at(i * 256, 256)
        total[cols, 0:512] = dot_tn(mixed[:, cols], right[:, 0:512])
        last = right[:, 512:768]
        total[cols, 512:768] = jnp.where(
            lane < 64, dot_tn(mixed[:, cols], last), dot_tn(grad_branch[:, cols], last)
        )
        return carry

    lax.fori_loop(0, 3, step, 0)
    split_blocks(8, 1, 1, lambda rows: total[rows, :], keep, send)


def kernel_v_one(held, came, keep, send):
    split_blocks(4, 1, 2, summed(held, came), keep, send)


def kernel_v_two(held, came, keep, send):
    split_blocks(2, 1, 4, summed(held, came), keep, send)


def kernel_v_end(held, came, qkv, out):
    total = summed(held, came)(slice(0, BLOCK))
    for kind in range(3):
        qkv[kind] = total[:, kind * HEAD_WIDTH : (kind + 1) * HEAD_WIDTH]
    out[...] = total[:, 3 * HEAD_WIDTH :]


def kernel_join(near, came, chip):
    chip[...] = (near[...].astype(f32) + came[...].astype(f32)).astype(bf16)


def kernel_join_split(near, came, own, send):
    _, side, _ = here_core()
    rows = own.shape[0]
    for out, x in ((own, side), (send, 1 - side)):
        where = at16(x * rows, rows)
        out[...] = (near[where, :].astype(f32) + came[where, :].astype(f32)).astype(bf16)


def kernel_slot(late, cond, out):
    parts = [late[n].astype(f32) for n in range(4)]
    total = (parts[0] + parts[1]) + (parts[2] + parts[3])
    high = cond[...].astype(bf16).astype(f32)
    out[0] = jnp.concatenate([total[0:6, :], high, cond[...] - high]).astype(bf16)
    out[1] = total[6:14, :].astype(bf16)
    out[2] = jnp.concatenate([total[14:16, :], jnp.zeros((6, WIDTH), f32)]).astype(bf16)


def kernel_gather(slots, held, came, out):
    out[0:slots] = held[0:slots].astype(out.dtype)
    out[slots : 2 * slots] = came[0:slots].astype(out.dtype)
    total = held[slots : slots + 2].astype(f32) + came[slots : slots + 2].astype(f32)
    out[2 * slots : 2 * slots + 2] = total.astype(out.dtype)


def kernel_g(
    size, share, ids, near, came, w_mod,
    w_out, b_out, class_out, k_out, bias_out,
    held, lanes, grads, outer,
):
    here = lax.axis_index("dp")
    kernel_gather(size // 2, near, came, held)
    class_out[...] = jnp.zeros_like(class_out)
    conds = held[0:size, 6, :] + held[0:size, 7, :]
    sig = 1.0 / (1.0 + jnp.exp(-conds))
    act = (conds * sig).astype(bf16)
    total = jnp.zeros((size, WIDTH), f32)
    for p in range(6):
        piece = held[0:size, p, :].astype(bf16)
        lanes[:, p * WIDTH : (p + 1) * WIDTH] = piece
        total = total + dot_nn(piece, w_mod[p * WIDTH : (p + 1) * WIDTH, :])
    grads[...] = total * (sig * (1.0 + conds * (1.0 - sig)))
    reach = outer.shape[0]
    first = jnp.minimum(lax.div(here * share, 128) * 128, 6 * WIDTH - reach)
    outer[...] = dot_tn(lanes[:, pl.ds(pl.multiple_of(first, 128), reach)], act)
    w_out[...] = outer[pl.ds(pl.multiple_of(here * share - first, 8), share), :]

    def item(i, bias):
        slot = lax.bitwise_xor(here, i)
        row = pl.ds(ids[i], 1)
        class_out[row, :] = class_out[row, :] + grads[pl.ds(slot, 1), :]
        return bias + held[slot]

    bias = lax.fori_loop(0, size, item, jnp.zeros((8, WIDTH), f32))
    for p in range(6):
        b_out[pl.ds(p * WIDTH, WIDTH)] = bias[p : p + 1, :].reshape(WIDTH)
    k_out[0:8, :] = held[size]
    k_out[8:9, :] = held[size + 1, 0:1, :]
    bias_out[...] = held[size + 1, 1:2, :].reshape(WIDTH)


def vmem(shape, dtype):
    return pltpu.VMEM(shape, dtype)


def hbm(shape, dtype):
    return pltpu.HBM(shape, dtype)


def plain(shape, dtype):
    return jax.ShapeDtypeStruct(shape, dtype)


def call(kernel, scalars, arrays, far_arrays, outs, scratch, mebibytes, flops, moved, cost=0):
    spots = (
        [pl.BlockSpec(memory_space=pltpu.SMEM)] * len(scalars)
        + [pl.BlockSpec(memory_space=pltpu.VMEM)] * len(arrays)
        + [pl.BlockSpec(memory_space=pltpu.HBM)] * len(far_arrays)
    )
    spaces = [pltpu.VMEM if getattr(o, "memory_space", None) != pltpu.HBM else pltpu.HBM for o in outs]
    return pl.pallas_call(
        kernel,
        out_shape=tuple(outs),
        in_specs=spots,
        out_specs=tuple(pl.BlockSpec(memory_space=m) for m in spaces),
        scratch_shapes=scratch,
        compiler_params=pltpu.CompilerParams(vmem_limit_bytes=mebibytes << 20),
        cost_estimate=pl.CostEstimate(flops=0, bytes_accessed=cost, transcendentals=0),
    )(
        *scalars,
        *(pltpu.with_memory_space_constraint(a, pltpu.VMEM) for a in arrays),
        *(pltpu.with_memory_space_constraint(a, pltpu.HBM) for a in far_arrays),
    )


def swap(values, axis, bit):
    size = lax.axis_size(axis)
    return lax.ppermute(values, axis, [(i, i ^ bit) for i in range(size)])


def bits_of(axis):
    return [1 << b for b in range(lax.axis_size(axis).bit_length() - 1)]


def butterfly(values, axis):
    for bit in bits_of(axis):
        values = values + swap(values, axis, bit)
    return values


def scatter_plain(total):
    size = lax.axis_size("dp")
    here = lax.axis_index("dp")
    held = total.reshape(total.shape[0], size, -1, total.shape[-1])
    for bit in bits_of("dp"):
        mine = (here // bit) % 2
        parts, blocks, rows, width = held.shape
        halves = held.reshape(parts, blocks // 2, 2, rows, width)
        keep = lax.dynamic_index_in_dim(halves, mine, 2, keepdims=False)
        send = lax.dynamic_index_in_dim(halves, 1 - mine, 2, keepdims=False).astype(bf16)
        held = keep + swap(send, "dp", bit).astype(f32)
    return held[:, 0]


def join(near, came):
    (chip,) = call(kernel_join, [], [near, came], [], [vmem(near.shape, bf16)], [], 4, 10**6, 3 * 10**6)
    return chip


def join_split(near, came):
    part = vmem((near.shape[0] // 2, WIDTH), bf16)
    return call(kernel_join_split, [], [near, came], [], [part, part], [], 4, 10**6, 3 * 10**6)


def weight_step(kernel, shapes, *arrays):
    outs = [vmem(shape, kind) for shape in shapes for kind in (f32, bf16)]
    return call(kernel, [], list(arrays), [], outs, [], 4, 10**6, 4 * 10**6)


def time_features(timestep):
    half_width = WIDTH // 2
    freqs = jnp.exp(-math.log(10000.0) * jnp.arange(half_width, dtype=f32) / half_width)
    angles = timestep.astype(f32)[:, None] * freqs[None, :]
    return jnp.concatenate([jnp.cos(angles), jnp.sin(angles)], axis=1)


def together(*values):
    return lax.optimization_barrier(values)


def shards(
    tokens,
    cotangent,
    item_count,
    timestep,
    class_id,
    class_table,
    w_mod,
    b_mod,
    k_att,
    w_qkv,
    w_out,
    b_out,
    w_up,
    b_up,
    k_ffn,
    w_down,
    b_down,
):
    items = lax.axis_size("dp")
    bits = bits_of("dp")
    eight = items * BLOCK == WIDTH
    full = (ITEM, WIDTH)
    half = (HALF, WIDTH)
    head = (ITEM, HEAD_WIDTH)
    grid = pltpu.VMEM((TILES, GRID_ROWS, 128), f32)
    natural = pltpu.VMEM((TILES, ITEM, 128), f32)
    share_tiles = pltpu.VMEM((TILES, SHARE, 128), f32)
    temp = pltpu.VMEM((SHARE, WIDTH), f32)
    taps = pltpu.VMEM((16, WIDTH), f32)
    sem = pltpu.SemaphoreType.DMA

    row = lax.dynamic_slice(class_table, (class_id[0], 0), (1, WIDTH), allow_negative_indices=False)
    cond = time_features(timestep) + row.astype(f32)
    act = jnp.broadcast_to(jax.nn.silu(cond).astype(bf16), (16, WIDTH))
    w_three = jnp.transpose(w_qkv, (1, 2, 0))
    w_back = w_out.T

    mods_a, keep, send, lse, mixed, query, keys, vals, attended = call(
        kernel_a, [], [act], [tokens, b_mod, k_att, w_three, w_back, w_mod],
        [
            vmem((8, WIDTH), f32), vmem(half, bf16), vmem(half, bf16),
            vmem((8, HEADS_HERE * SHARE), f32),
            hbm(full, bf16), hbm(head, bf16), hbm(head, bf16), hbm(head, bf16), hbm(head, bf16),
        ],
        [
            grid, pltpu.VMEM((2, SHARE, WIDTH), f32), taps, pltpu.VMEM(full, bf16),
            pltpu.VMEM(b_mod.shape, bf16),
            pltpu.VMEM(k_att.shape, bf16), pltpu.VMEM(w_three.shape, bf16),
            pltpu.VMEM(w_back.shape, bf16), pltpu.VMEM((2 * WIDTH, WIDTH), bf16), pltpu.VMEM(full, bf16),
            pltpu.VMEM(head, bf16), pltpu.VMEM(head, bf16), pltpu.VMEM(head, bf16),
            pltpu.VMEM(head, bf16), sem((5, 4)), sem((6,)),
        ],
        21, 3 * 10**9, 10**7,
    )
    chip = join(keep, swap(send, "tensor", 1))
    far = swap(chip, "tensor", 2)
    _, cotangent, tokens_b = together(chip, cotangent, tokens)
    (source,) = call(kernel_source, [], [tokens_b], [], [vmem(half, f32)], [natural], 6, 0, 0)
    mods_p, grad_ffn, cot_half, cot_other = call(
        kernel_p, [item_count], [cotangent, act, b_mod], [w_mod],
        [vmem((8, WIDTH), f32), vmem(full, bf16), vmem(half, bf16), vmem(half, bf16)],
        [natural, pltpu.VMEM((4 * WIDTH, WIDTH), bf16), sem], 12, 10**8, 8 * 10**6,
    )
    (grad_act,) = call(
        kernel_ga, [], [grad_ffn, w_down], [], [vmem(full, f32)], [], 6, 12 * 10**8, 6 * 10**6
    )
    far, mods_p, source, _ = together(far, mods_p, source, grad_act)
    branch, middle, shaped_own = call(
        kernel_b, [], [chip, far, source, mods_p, b_out], [],
        [vmem(half, f32), vmem(half, f32), vmem(half, bf16)], [], 6, 10**7, 7 * 10**6,
    )
    shaped_other = swap(shaped_own, "tensor", 1)

    shaped, activated, grad_hidden, sums_c, g_keep, g_send = call(
        kernel_c, [class_id], [shaped_own, shaped_other, grad_ffn, grad_act, w_up, b_up, k_ffn], [],
        [vmem(full, bf16)] * 3 + [vmem((16, WIDTH), f32)] + [vmem(half, bf16)] * 2,
        [grid, grid, temp, taps], 13, 5 * 10**9, 12 * 10**6,
    )
    g_came = swap(g_send, "tensor", 1)
    total_scratch = [pltpu.VMEM((WIDTH, WIDTH), f32)]
    if eight:
        d_keep, d_send = call(
            kernel_w_down, [], [grad_ffn, activated, sums_c], [],
            [vmem((4 * BLOCK + TAIL, WIDTH), f32), vmem((4 * BLOCK + TAIL, WIDTH), bf16)],
            total_scratch, 6, 12 * 10**8, 5 * 10**6,
        )
        g_came, _ = together(g_came, d_send)
    chip = join(g_keep, g_came)
    far = swap(chip, "tensor", 2)
    _, shaped = together(chip, shaped)
    if eight:
        u_keep, u_send = call(
            kernel_w_up, [], [shaped, grad_hidden], [],
            [vmem((4 * BLOCK, WIDTH), f32), vmem((4 * BLOCK, WIDTH), bf16)],
            total_scratch, 6, 12 * 10**8, 5 * 10**6,
        )
        d_came = swap(d_send, "dp", 1)
        u_came = swap(u_send, "dp", 2)
        tokens_n, activated, _, _ = together(tokens, activated, d_send, u_send)
    else:
        ffn_grads = scatter_plain(
            jnp.stack([dot_tn(grad_ffn, activated), dot_tn(shaped, grad_hidden)])
        )
        early = butterfly(sums_c, "dp")
        tokens_n = tokens
    b_keep, b_send = call(
        kernel_branch, [], [activated, w_down], [], [vmem(half, bf16)] * 2, [temp], 6, 0, 0
    )
    (normed,) = call(
        kernel_n, [], [tokens_n], [], [vmem((TILES, ITEM, 128), f32)], [], 4, 10**7, 5 * 10**6
    )
    (sums_q,) = call(
        kernel_q, [], [b_keep, b_send, cot_half, cot_other, b_down], [], [vmem((8, WIDTH), f32)], [],
        4, 10**7, 4 * 10**6,
    )
    query, _ = together(query, sums_q)
    (probs,) = call(
        kernel_p_again, [], [query, keys, lse], [], [vmem((12, SHARE, SHARE), f32)], [],
        6, 10**8, 4 * 10**6,
    )
    far, b_send, _, _ = together(far, b_send, normed, probs)
    if eight:
        far, d_came, u_came = together(far, d_came, u_came)
    grad_middle, attn_own, sums_d = call(
        kernel_d, [], [chip, far, branch, middle, cot_half, mods_p], [],
        [vmem(half, f32), vmem(half, bf16), vmem((8, WIDTH), f32)], [], 6, 10**7, 8 * 10**6,
    )
    attn_other = swap(attn_own, "tensor", 1)
    if eight:
        d_came, u_came, _ = together(d_came, u_came, attn_own)
        d_keep, d_send, u_keep, u_send = weight_step(
            kernel_w_one, [(2 * BLOCK + TAIL, WIDTH), (2 * BLOCK, WIDTH)], d_keep, d_came, u_keep, u_came
        )
        attn_other, _, _ = together(attn_other, d_send, u_send)
        d_came = swap(d_send, "dp", 2)
        u_came = swap(u_send, "dp", 1)

    grad_attn, right, mixed_grad, mixed, h_keep, h_send = call(
        kernel_e, [],
        [attn_own, attn_other, query, keys, vals, attended, probs, w_three, w_back], [mixed],
        [vmem(full, bf16)] * 4 + [vmem((2 * HALO, WIDTH), bf16)] * 2,
        [pltpu.VMEM((4, 288, WIDTH), bf16), sem], 8, 3 * 10**9, 10**7,
    )
    if eight:
        d_came, u_came, b_send, right, h_send = together(d_came, u_came, b_send, right, h_send)
    h_came = swap(h_send, "tensor", 1)
    b_came = swap(b_send, "tensor", 1)
    h_came, b_came = together(h_came, b_came)
    w_mod_late, _ = together(w_mod, mixed_grad)
    if eight:
        ffn_keep, ffn_send = weight_step(
            kernel_w_two, [(2 * BLOCK + TAIL, WIDTH)], d_keep, d_came, u_keep, u_came
        )
        a_keep, a_send = call(
            kernel_v, [], [mixed, grad_attn, right], [],
            [vmem((4 * BLOCK, WIDTH), f32), vmem((4 * BLOCK, WIDTH), bf16)],
            [pltpu.VMEM((WIDTH, WIDTH), f32)], 6, 16 * 10**8, 7 * 10**6,
        )
        h_came, _, _ = together(h_came, a_send, ffn_send)
        a_came = swap(a_send, "dp", 1)
        ffn_came = swap(ffn_send, "dp", 4)
    else:
        last = dot_tn(grad_attn, right[:, 3 * HEAD_WIDTH :])
        total = jnp.concatenate([dot_tn(mixed, right[:, : 3 * HEAD_WIDTH]), last], axis=1)
        att_grads = scatter_plain(total[None])[0]
    h_own, part = join_split(h_keep, h_came)
    mixed_grad, _ = together(mixed_grad, part)
    (late,) = call(
        kernel_s, [], [normed, mixed_grad, mods_a, k_att, sums_d, sums_q], [],
        [vmem((16, WIDTH), bf16)], [taps, grid, taps], 8, 10**8, 4 * 10**6,
    )
    late = lax.all_gather(late, "tensor")
    (held,) = call(
        kernel_slot, [], [late, cond], [], [vmem((3, 8, WIDTH), bf16)], [], 2, 10**5, 10**5
    )
    part, _ = together(part, held)
    part_far = swap(part, "tensor", 2)
    b_own, b_part = join_split(b_keep, b_came)
    if not eight:
        b_far = swap(b_part, "tensor", 2)
    for step, bit in enumerate(bits):
        came = swap(held, "dp", bit)
        if step == len(bits) - 1:
            part_far, _ = together(part_far, held)
            (grad_tokens,) = call(
                kernel_f, [], [tokens, h_own, part_far, grad_middle, mods_a, k_att], [],
                [plain((SHARE, WIDTH), f32)],
                [pltpu.VMEM((TILES, SHARE_GRID_ROWS, 128), f32), share_tiles, share_tiles, taps],
                6, 10**7, 6 * 10**6, 0,
            )
            (block_out,) = call(
                kernel_o, [item_count], [b_own, b_far, middle, mods_p, b_down], [],
                [plain((SHARE, WIDTH), bf16)], [share_tiles], 4, 10**7, 4 * 10**6,
            )
            came, _, _ = together(came, grad_tokens, block_out)
            break
        slots = 1 << step
        if eight and step == 1:
            came, part_far = together(came, part_far)

        def kernel(*refs, slots=slots):
            kernel_gather(slots, *refs)

        (held,) = call(
            kernel, [], [held, came], [], [vmem((2 * slots + 2, 8, WIDTH), bf16)], [], 4, 10**5, 10**5
        )
        if eight and step == 0:
            a_came, ffn_came, b_part, _ = together(a_came, ffn_came, b_part, held)
            b_far = swap(b_part, "tensor", 2)
            a_keep, a_send = weight_step(kernel_v_one, [(2 * BLOCK, WIDTH)], a_keep, a_came)
            a_came = swap(a_send, "dp", 2)
    if eight:
        a_came, _ = together(a_came, held)
        a_keep, a_send = weight_step(kernel_v_two, [(BLOCK, WIDTH)], a_keep, a_came)
        a_came = swap(a_send, "dp", 4)
        came, _ = together(came, a_send)

    if eight:
        rows = plain((BLOCK, WIDTH), f32)
        flat = plain((WIDTH,), f32)
        grad_down, grad_up, grad_k_ffn, grad_b_up, grad_b_down, ids = call(
            kernel_w_end, [], [ffn_keep, ffn_came], [],
            [rows, rows, plain((9, WIDTH), f32), flat, flat, plain((1, 128), jnp.int32)],
            [], 4, 10**6, 2 * 10**6,
        )
        ids = ids[0, :items]
    else:
        ids = (32.0 * early[11, :items] + early[12, :items]).astype(jnp.int32)
    share = w_mod.shape[0] // items

    def kernel(*refs):
        kernel_g(items, share, *refs)

    grad_w_mod, grad_b_mod, grad_class, grad_k_att, grad_b_out = call(
        kernel, [ids], [held, came, w_mod_late], [],
        [
            plain((share, WIDTH), f32), plain(w_mod.shape[:1], f32), plain(class_table.shape, f32),
            plain((9, WIDTH), f32), plain((WIDTH,), f32),
        ],
        [
            pltpu.VMEM((items + 2, 8, WIDTH), f32), pltpu.VMEM((items, 6 * WIDTH), bf16),
            pltpu.VMEM((items, WIDTH), f32), pltpu.VMEM(((share + 254) // 128 * 128, WIDTH), f32),
        ],
        12, 10**8, 14 * 10**6,
    )

    if eight:
        a_came, _, _ = together(a_came, grad_b_mod, grad_b_up)
        grad_qkv, grad_out = call(
            kernel_v_end, [], [a_keep, a_came], [],
            [plain((3, BLOCK, HEAD_WIDTH), f32), plain((BLOCK, HEAD_WIDTH), f32)], [], 4, 10**6, 10**6,
        )
        grad_qkv = jnp.transpose(grad_qkv, (1, 0, 2))
    else:
        grad_down, grad_up = ffn_grads[0], ffn_grads[1]
        grad_k_ffn, grad_b_up, grad_b_down = early[:9], early[9], early[10]
        grad_qkv = att_grads[:, : 3 * HEAD_WIDTH].reshape(-1, 3, HEAD_WIDTH)
        grad_out = att_grads[:, 3 * HEAD_WIDTH :]
    return (
        block_out,
        grad_tokens,
        grad_class,
        grad_w_mod,
        grad_b_mod,
        grad_k_att,
        grad_qkv,
        grad_out,
        grad_b_out,
        grad_up,
        grad_b_up,
        grad_k_ffn,
        grad_down,
        grad_b_down,
    )


def solution(mesh):
    placed = (
        P("dp", None),
        P("dp", None),
        P("dp"),
        P("dp"),
        P("dp"),
        P(),
        P(),
        P(),
        P(),
        P(None, None, "tensor"),
        P(None, "tensor"),
        P(),
        P(None, "tensor"),
        P("tensor"),
        P(None, "tensor"),
        P(None, "tensor"),
        P(),
    )
    return jax.shard_map(
        shards,
        mesh=mesh,
        in_specs=placed,
        out_specs=(
            P(("dp", "tensor"), None),
            P(("dp", "tensor"), None),
            P(),
            P("dp", None),
            P(),
            P(),
            P("dp", None, "tensor"),
            P("dp", "tensor"),
            P(),
            P("dp", "tensor"),
            P("tensor"),
            P(None, "tensor"),
            P("dp", "tensor"),
            P(),
        ),
        check_vma=False,
    )
```
